32 devices in a mesh: ctx: 8 (over z, y), head: 4 (over x, core).
Axes of the slice: x: 2, y: 2, z: 4, core: 2. Of those that a mesh axis runs over, the one named last changes fastest.
Arguments:
- queries: bfloat16 [8192, 2048], P('ctx', 'head'), may hold values from -6 to 6
- keys: bfloat16 [8192, 2048], P('ctx', 'head'), may hold values from -6 to 6
- values: bfloat16 [8192, 2048], P('ctx', 'head'), may hold values from -36 to 36
- mem_route: int32 [8192], P('ctx'), may hold values from 0 to 3
- head_gain: float32 [2048], P('head'), may hold values from 0.25 to 1.75
- residual_in: bfloat16 [8192, 2048], P(('ctx', 'head')), may hold values from -24 to 24
- ffn_gain: float32 [2048], replicated, may hold values from 0.25 to 1.75
- expert_ids: int32 [8192, 2], P(('ctx', 'head')), may hold values from 0 to 255, all different within a row; in each aligned block of 256 rows (0 to 255, 256 to 511, ...) at most 4 rows name the same one
- expert_gates: float32 [8192, 2], P(('ctx', 'head')), may hold values from 0.2 to 1
- w_gate: bfloat16 [256, 2048, 512], P(('ctx', 'head')), may hold values from -0.125 to 0.125
- w_up: bfloat16 [256, 2048, 512], P(('ctx', 'head')), may hold values from -0.125 to 0.125
- w_down: bfloat16 [256, 512, 2048], P(('ctx', 'head')), may hold values from -0.25 to 0.25
Outputs:
- layer_out: bfloat16 [8192, 2048], P(('ctx', 'head'))
The draws below stay inside these ranges and needn't reach their ends.
Inputs may be any that keep to these rules, and one draw needn't show every extreme that they name: `expert_ids`: the two experts of a token differ. Among the 512 choices of the tokens of one device, no expert is named more than 4 times, a bound that some block reaches.
All inputs are finite; a program needn't handle non-finite values.
Results may differ from the reference program's by a relative error of at most 0.0095.
Values may be sent and summed in bfloat16 or wider, within the bound.
No kernel may reach another device: no remote copies, remote signals or barrier semaphores. Data moves between devices by JAX's collectives and lax.ppermute only.
A program may use at most 128 MiB of HBM per device.

```python
import math
import jax
import jax.numpy as jnp
import numpy as np
from jax import lax

H = 16
HD = 128
D = 2048
M = 4
E = 256
FF = 512
CAP = 4
TOK_DEV = 256
TOKENS = 8192


def scaled_field(key, rows, cols, low, high):
    base_key, row_key, col_key = jax.random.split(key, 3)
    base = jnp.clip(jax.random.normal(base_key, (rows, cols), jnp.float32), -6.0, 6.0)
    row_scale = jnp.exp(jax.random.uniform(row_key, (rows, 1), jnp.float32, math.log(0.5), math.log(2.0)))
    col_scale = jnp.exp(jax.random.uniform(col_key, (1, cols), jnp.float32, math.log(low), math.log(high)))
    return (base * row_scale * col_scale).astype(jnp.bfloat16)


def draw_values(key, part):
    return scaled_field(jax.random.fold_in(key, 11), TOKENS, D, 0.3, 3.0)


def draw_residual_in(key, part):
    return scaled_field(jax.random.fold_in(key, 23), TOKENS, D, 0.5, 2.0)


def with_ends(values, own_key, low, largest):
    longest = values.shape.index(max(values.shape))
    spots = []
    for shift in (0, 1):
        where = [jax.random.randint(jax.random.fold_in(own_key, axis), (), 0, length) for axis, length in enumerate(values.shape)]
        where[longest] = (where[longest] + shift) % values.shape[longest]
        spots.append(tuple(where))
    return values.at[spots[0]].set(low).at[spots[1]].set(largest)


def steps_of(key, dims, shards, least, high):
    gain = 1.0
    for position, parts in shards:
        steps = jax.random.uniform(jax.random.fold_in(jax.random.fold_in(key, 6), position), (parts,), jnp.float32, least / len(shards), high / len(shards))
        gain = gain * jnp.repeat(jnp.exp(steps), dims[position] // parts).reshape((-1,) + (1,) * (len(dims) - 1 - position))
    return gain


def assign_block(stream_key, own, number, rows, number_of, top, limit, slope):
    ranking = jax.random.permutation(stream_key, number_of)
    heavy_load, common = load_shares(number_of, rows * top, limit, slope, True), load_shares(number_of, rows * top, limit, slope, False)
    places = jnp.arange(number_of)

    def named(tallies, rotation):
        used = int((tallies > 0).sum())
        fixed = max(1, used // 4)
        passed = fixed + (places - fixed + rotation * (used - fixed)) % max(1, number_of - fixed)
        return jnp.zeros((number_of,), jnp.int32).at[ranking[jnp.where(places < fixed, places, passed)]].set(jnp.asarray(tallies, jnp.int32))

    tallies = jnp.where(number % 4 == 0, named(heavy_load, number // 4), named(common, number - number // 4 - 1))
    mixed = jax.random.permutation(jax.random.fold_in(own, 3), number_of)
    giver, taker = mixed[0:number_of // 2 * 2:2], mixed[1:number_of // 2 * 2:2]
    slack = jnp.minimum(tallies[giver] - 1, limit - tallies[taker]) // 2
    slack = jnp.where((giver == ranking[0]) | (taker == ranking[0]) | (tallies[taker] == 0), 0, jnp.maximum(slack, 0))
    passed = jax.random.randint(jax.random.fold_in(own, 4), (number_of // 2,), 0, 1 << 20) % (slack + 1)
    tallies = tallies.at[giver].add(-passed).at[taker].add(passed)
    members = jnp.searchsorted(jnp.cumsum(tallies), jnp.arange(rows * top), side="right").astype(jnp.int32)
    listing = members.reshape(top, rows).T
    listing = listing[jax.random.permutation(jax.random.fold_in(own, 1), rows)]
    rotation = jax.random.randint(jax.random.fold_in(own, 2), (rows, 1), 0, top)
    return jnp.take_along_axis(listing, (jnp.arange(top)[None, :] + rotation) % top, axis=1)


def load_shares(amount, total, bound, lean, full):
    loads = [(1 << 20) // math.isqrt(rank ** lean) + 1 for rank in range(1, amount + 1)]
    largest = bound if full else min(bound, max(-(-total // amount), total * loads[0] // sum(loads)))
    least = 1 if total - largest >= amount - 1 else 0
    given, spare = [largest] + [least] * (amount - 1), total - largest - least * (amount - 1)
    while spare > 0:
        candidates = [i for i in range(1, amount) if given[i] < largest] or [i for i in range(1, amount) if given[i] < bound]
        mass, budget = sum([loads[i] for i in candidates]), spare
        for i in candidates:
            extra = min(bound - given[i], max(1, budget * loads[i] // mass), spare)
            given[i] = given[i] + extra
            spare = spare - extra
    return np.array(given)


def normal_values(rng, shape, spread, reach, cuts=(), held_as=jnp.bfloat16):
    values = spread * jax.random.normal(rng, shape, jnp.float32)
    if cuts:
        values = values * steps_of(rng, shape, cuts, -0.22, 0.18)
    return jnp.clip(values, -reach, reach).astype(held_as)


def setup_inputs(seed: int = 0) -> dict:
    arg_keys = jax.random.split(jax.random.key(seed), 13)
    queries = normal_values(arg_keys[0], (TOKENS, D), 1.0, 6.0, ((0, 8), (1, 4)))
    keys = normal_values(arg_keys[1], (TOKENS, D), 1.0, 6.0, ((0, 8), (1, 4)))
    values = draw_values(jax.random.fold_in(arg_keys[12], 71), 0)
    mem_route = with_ends(jax.random.randint(arg_keys[3], (TOKENS,), 0, M), jax.random.fold_in(arg_keys[3], 1), 0, M - 1).astype(jnp.int32)
    head_gain = jnp.clip(1.0 + 0.15 * jax.random.normal(arg_keys[4], (D,), jnp.float32), 0.25, 1.75)
    residual_in = draw_residual_in(jax.random.fold_in(arg_keys[12], 71), 0)
    ffn_gain = jnp.clip(1.0 + 0.15 * jax.random.normal(arg_keys[6], (D,), jnp.float32), 0.25, 1.75)
    expert_ids_keys = jax.random.split(jax.random.fold_in(arg_keys[7], 1), TOKENS // TOK_DEV)
    expert_ids_turns = jax.random.permutation(jax.random.fold_in(arg_keys[7], 3), TOKENS // TOK_DEV)
    expert_ids = jax.vmap(lambda own, number: assign_block(jax.random.fold_in(arg_keys[7], 2), own, number, TOK_DEV, E, 2, CAP, 2))(expert_ids_keys, expert_ids_turns).reshape((TOKENS, 2))
    expert_gates = jnp.clip(0.2 + 0.8 * jax.random.uniform(arg_keys[8], (TOKENS, 2), jnp.float32) ** steps_of(arg_keys[8], (TOKENS, 2), ((0, 32),), -0.2, 0.2), 0.2, 1.0)
    w_gate = normal_values(arg_keys[9], (E, D, FF), D ** -0.5, 0.125, ((0, 32),))
    w_up = normal_values(arg_keys[10], (E, D, FF), D ** -0.5, 0.125, ((0, 32),))
    w_down = normal_values(arg_keys[11], (E, FF, D), FF ** -0.5, 0.25, ((0, 32),))
    return {"queries": queries, "keys": keys, "values": values, "mem_route": mem_route, "head_gain": head_gain, "residual_in": residual_in, "ffn_gain": ffn_gain, "expert_ids": expert_ids, "expert_gates": expert_gates, "w_gate": w_gate, "w_up": w_up, "w_down": w_down}


def reference(queries, keys, values, mem_route, head_gain, residual_in, ffn_gain, expert_ids, expert_gates, w_gate, w_up, w_down):
    highest = lax.Precision.HIGHEST
    block_rows = min(512, TOKENS)
    block_count = TOKENS // block_rows
    shaped = (block_count, block_rows, H, HD)
    query_blocks = queries.reshape(shaped)
    key_blocks = keys.reshape(shaped)
    value_blocks = values.reshape(shaped)
    route_blocks = mem_route.reshape(block_count, block_rows)
    memory_ids = jnp.arange(M, dtype=jnp.int32)
    positions = jnp.arange(block_rows, dtype=jnp.int32)
    causal = positions[:, None] >= positions[None, :]

    def advance(state, inputs):
        query_part, key_part, value_part, route_part = inputs
        query_wide = query_part.astype(jnp.float32)
        key_wide = key_part.astype(jnp.float32)
        value_wide = value_part.astype(jnp.float32)
        member = (route_part[:, None] == memory_ids[None, :]).astype(jnp.float32)
        scores = jnp.einsum('thd,shd->hts', query_wide, key_wide, precision=highest)
        same = (route_part[:, None] == route_part[None, :]).astype(jnp.float32)
        weights = jnp.where(causal, 1.0 + same, 0.0)
        local_part = jnp.einsum('hts,shd->thd', scores * weights[None], value_wide, precision=highest)
        projected = jnp.einsum('thd,hmde->thme', query_wide, state, precision=highest)
        prior = jnp.einsum('thme,tm->the', projected, 1.0 + member, precision=highest)
        masked_keys = key_wide[:, :, None, :] * member[:, None, :, None]
        state = state + jnp.einsum('thmd,the->hmde', masked_keys, value_wide, precision=highest)
        return (state, local_part + prior)
    start_state = jnp.zeros((H, M, HD, HD), jnp.float32)
    final_state, mixed = lax.scan(advance, start_state, (query_blocks, key_blocks, value_blocks, route_blocks))
    mixed = mixed.reshape(TOKENS, H, HD)
    scale = lax.rsqrt(lax.optimization_barrier(jnp.mean(mixed * mixed, axis=-1, keepdims=True)) + 1e-06)
    normed = (mixed * scale * head_gain.reshape(H, HD)).astype(jnp.bfloat16).reshape(TOKENS, D)
    stream = (residual_in.astype(jnp.float32) + normed.astype(jnp.float32)).astype(jnp.bfloat16)
    widened = stream.astype(jnp.float32)
    ffn_in = (widened * lax.rsqrt(lax.optimization_barrier(jnp.mean(widened * widened, axis=-1, keepdims=True)) + 1e-06) * ffn_gain).astype(jnp.bfloat16)
    flat_ids = expert_ids.reshape(-1)
    most_rows = TOKENS // TOK_DEV * CAP
    filler = 2 * TOKENS

    def one_expert(expert, gathered):
        picked = jnp.nonzero(flat_ids == expert, size=most_rows, fill_value=filler)[0].astype(jnp.int32)
        rows = ffn_in[jnp.minimum(picked // 2, TOKENS - 1)]
        gate = jnp.dot(rows, w_gate[expert], preferred_element_type=jnp.float32)
        upward = jnp.dot(rows, w_up[expert], preferred_element_type=jnp.float32)
        hidden = (jax.nn.silu(gate) * upward).astype(jnp.bfloat16)
        result = jnp.dot(hidden, w_down[expert], preferred_element_type=jnp.float32).astype(jnp.bfloat16)
        return gathered.at[picked].set(result, mode='drop')
    gathered = lax.fori_loop(0, E, one_expert, jnp.zeros((2 * TOKENS, D), jnp.bfloat16))
    pair = gathered.astype(jnp.float32).reshape(TOKENS, 2, D)
    total = widened + expert_gates[:, 0:1] * pair[:, 0] + expert_gates[:, 1:2] * pair[:, 1]
    return total.astype(jnp.bfloat16)
```

```python
import functools

import jax
import jax.numpy as jnp
from jax import lax
from jax.experimental import pallas as pl
from jax.experimental.pallas import tpu as pltpu
from jax.sharding import PartitionSpec as P

HD = 128
M = 4
CAP = 4
PAIR = 2
GROUP_ROWS = PAIR * CAP
EPS = 1e-06
F32 = jnp.float32
BF16 = jnp.bfloat16


def params(**more):
    return pltpu.CompilerParams(vmem_limit_bytes=60 * 1024 * 1024, **more)


def contract(a, b, dims):
    return lax.dot_general(a, b, (dims, ((), ())), preferred_element_type=F32)


def state_kernel(key_ref, value_ref, route_ref, out_ref):
    keys_t = key_ref[...].T
    values = value_ref[...]
    route = route_ref[...]
    for m in range(M):
        mask = (route == m).astype(F32).astype(BF16)
        out_ref[pl.ds(m * HD, HD), :] = contract(keys_t * mask, values, ((1,), (0,))).astype(BF16)


def block_states(keys, values, route_row):
    length, width = keys.shape
    heads = width // HD
    return pl.pallas_call(
        state_kernel,
        name="block_states",
        grid=(heads,),
        in_specs=[
            pl.BlockSpec((length, HD), lambda h: (0, h)),
            pl.BlockSpec((length, HD), lambda h: (0, h)),
            pl.BlockSpec((1, length), lambda h: (0, 0)),
        ],
        out_specs=pl.BlockSpec((M * HD, HD), lambda h: (h, 0)),
        out_shape=jax.ShapeDtypeStruct((heads * M * HD, HD), BF16),
        compiler_params=params(),
    )(keys, values, route_row)


def prefix_kernel(ranks, piece_ref, out_ref):
    total = jnp.zeros(piece_ref.shape[1:], F32)
    for r in range(ranks):
        out_ref[r] = total.astype(BF16)
        if r + 1 < ranks:
            total = total + piece_ref[r].astype(F32)


def exclusive_prefix(pieces):
    return pl.pallas_call(
        functools.partial(prefix_kernel, pieces.shape[0]),
        name="exclusive_prefix",
        out_shape=jax.ShapeDtypeStruct(pieces.shape, BF16),
        compiler_params=params(),
    )(pieces)


def local_kernel(rows, query_ref, key_ref, value_ref, route_row_ref, route_col_ref, out_ref, weight_ref):
    length = query_ref.shape[0]

    @pl.when(pl.program_id(0) == 0)
    def _():
        route_row = route_row_ref[...]
        for i in range(length // rows):
            span = (i + 1) * rows
            column = route_col_ref[pl.ds(i * rows, rows), :]
            same = jnp.where(column == route_row[:, :span], 2.0, 1.0)
            t = lax.broadcasted_iota(jnp.int32, (rows, span), 0) + i * rows
            s = lax.broadcasted_iota(jnp.int32, (rows, span), 1)
            weight_ref[pl.ds(i * rows, rows), :span] = jnp.where(t >= s, same, 0.0)

    for i in range(length // rows):
        span = (i + 1) * rows
        query = query_ref[pl.ds(i * rows, rows), :]
        scores = contract(query, key_ref[:span, :], ((1,), (1,)))
        weighted = (scores * weight_ref[pl.ds(i * rows, rows), :span]).astype(BF16)
        out_ref[pl.ds(i * rows, rows), :] = contract(weighted, value_ref[:span, :], ((1,), (0,)))


def local_attention(queries, keys, values, route_row, route_col):
    length, width = queries.shape
    heads = width // HD
    rows = min(256, length)
    wide = pl.BlockSpec((length, HD), lambda h: (0, h))
    return pl.pallas_call(
        functools.partial(local_kernel, rows),
        name="local_attention",
        grid=(heads,),
        in_specs=[
            wide,
            wide,
            wide,
            pl.BlockSpec((1, length), lambda h: (0, 0)),
            pl.BlockSpec((length, 1), lambda h: (0, 0)),
        ],
        out_specs=wide,
        out_shape=jax.ShapeDtypeStruct((length, width), F32),
        scratch_shapes=[pltpu.VMEM((length, length), F32)],
        compiler_params=params(),
    )(queries, keys, values, route_row, route_col)


def mix_kernel(query_ref, state_ref, local_ref, route_col_ref, gain_ref, out_ref):
    parts, rows, _ = out_ref.shape
    query = query_ref[...]
    column = route_col_ref[...]
    wide = jnp.concatenate(
        [query * jnp.where(column == m, 2.0, 1.0).astype(BF16) for m in range(M)], axis=1
    )
    mixed = contract(wide, state_ref[...], ((1,), (0,))) + local_ref[...]
    scale = lax.rsqrt(jnp.mean(mixed * mixed, axis=-1, keepdims=True) + EPS)
    normed = (mixed * scale * gain_ref[...]).astype(BF16)
    for p in range(parts):
        out_ref[p] = normed[p * rows:(p + 1) * rows]


def mix_and_norm(queries, state, local, route_col, head_gain, parts):
    length, width = queries.shape
    heads = width // HD
    wide = pl.BlockSpec((length, HD), lambda h: (0, h))
    return pl.pallas_call(
        mix_kernel,
        name="mix_and_norm",
        grid=(heads,),
        in_specs=[
            wide,
            pl.BlockSpec((M * HD, HD), lambda h: (h, 0)),
            wide,
            pl.BlockSpec((length, 1), lambda h: (0, 0)),
            pl.BlockSpec((1, HD), lambda h: (0, h)),
        ],
        out_specs=pl.BlockSpec((parts, length // parts, HD), lambda h: (0, 0, h)),
        out_shape=jax.ShapeDtypeStruct((parts, length // parts, width), BF16),
        compiler_params=params(),
    )(queries, state, local, route_col, head_gain)


def slot_columns(ids, experts, local_experts):
    tokens = ids.shape[0]
    owners = experts // local_experts
    lanes = lax.broadcasted_iota(jnp.int32, (tokens, experts), 1)
    chosen = [(ids[:, j:j + 1] == lanes).astype(F32) for j in range(2)]
    t = lax.broadcasted_iota(jnp.int32, (tokens, tokens), 0)
    s = lax.broadcasted_iota(jnp.int32, (tokens, tokens), 1)
    earlier = contract(
        (t > s).astype(F32).astype(BF16), (chosen[0] + chosen[1]).astype(BF16), ((1,), (0,))
    )
    slots = []
    for j in range(2):
        rank = jnp.sum(earlier * chosen[j], axis=1, keepdims=True).astype(jnp.int32)
        expert = ids[:, j:j + 1]
        owner = expert // local_experts
        local = expert % local_experts
        slots.append(
            ((local // PAIR) * owners + owner) * GROUP_ROWS + (local % PAIR) * CAP + rank
        )
    return slots


def pack_kernel(chunks, local_experts, residual_ref, piece_ref, gain_ref, ids_ref, *refs):
    stream_ref, out_refs = refs[0], refs[1:1 + chunks]
    parts, rows, _ = piece_ref.shape
    owners, groups, _, width = out_refs[0].shape
    normed = jnp.concatenate([piece_ref[p] for p in range(parts)], axis=1)
    stream = (residual_ref[...].astype(F32) + normed.astype(F32)).astype(BF16)
    stream_ref[...] = stream
    wide = stream.astype(F32)
    scale = lax.rsqrt(jnp.mean(wide * wide, axis=-1, keepdims=True) + EPS)
    ffn_in = (wide * scale * gain_ref[...]).astype(BF16)
    experts = owners * local_experts
    slot0, slot1 = slot_columns(ids_ref[...], experts, local_experts)
    span = owners * GROUP_ROWS
    for c in range(chunks):
        for g in range(groups):
            base = (c * groups + g) * span
            lanes = lax.broadcasted_iota(jnp.int32, (rows, span), 1) + base
            spread = jnp.where((slot0 == lanes) | (slot1 == lanes), 1.0, 0.0).astype(BF16)
            packed = contract(spread, ffn_in, ((0,), (0,))).astype(BF16)
            out_refs[c][:, g] = packed.reshape(owners, GROUP_ROWS, width)


def pack(residual, pieces, gain, ids, chunks, owners, local_experts):
    tokens, width = residual.shape
    groups = local_experts // PAIR // chunks
    parcel = jax.ShapeDtypeStruct((owners, groups, GROUP_ROWS, width), BF16)
    out = pl.pallas_call(
        functools.partial(pack_kernel, chunks, local_experts),
        name="pack",
        out_shape=[jax.ShapeDtypeStruct((tokens, width), BF16)] + [parcel] * chunks,
        compiler_params=params(),
    )(residual, pieces, gain, ids)
    return out[0], out[1:]


def expert_kernel(x_ref, gate_ref, up_ref, down_ref, out_ref, acc_ref):
    e = pl.program_id(1)
    f = pl.program_id(2)
    owners, rows, width = x_ref.shape
    x = x_ref[...].reshape(owners * rows, width)
    gate = contract(x, gate_ref[...], ((1,), (0,)))
    upward = contract(x, up_ref[...], ((1,), (0,)))
    row = lax.broadcasted_iota(jnp.int32, gate.shape, 0)
    mine = (row // CAP) % PAIR == e
    hidden = gate / (1.0 + jnp.exp(-gate)) * upward
    hidden = jnp.where(mine, hidden, 0.0).astype(BF16)
    part = contract(hidden, down_ref[...], ((1,), (0,)))
    first = (e == 0) & (f == 0)

    @pl.when(first)
    def _():
        acc_ref[...] = part

    @pl.when(jnp.logical_not(first))
    def _():
        acc_ref[...] = acc_ref[...] + part

    @pl.when((e == pl.num_programs(1) - 1) & (f == pl.num_programs(2) - 1))
    def _():
        out_ref[...] = acc_ref[...].astype(BF16).reshape(owners, rows, width)


def serve_experts(received, w_gate, w_up, w_down, chunk):
    owners, groups, rows, width = received.shape
    hidden = w_gate.shape[2]
    split = 2
    step = hidden // split
    first = chunk * groups * PAIR
    token_spec = pl.BlockSpec((owners, None, rows, width), lambda g, e, f: (0, g, 0, 0))
    in_spec = pl.BlockSpec((None, width, step), lambda g, e, f: (first + g * PAIR + e, 0, f))
    return pl.pallas_call(
        expert_kernel,
        name=f"experts_{chunk}",
        grid=(groups, PAIR, split),
        in_specs=[
            token_spec,
            in_spec,
            in_spec,
            pl.BlockSpec((None, step, width), lambda g, e, f: (first + g * PAIR + e, f, 0)),
        ],
        out_specs=token_spec,
        out_shape=jax.ShapeDtypeStruct(received.shape, BF16),
        scratch_shapes=[pltpu.VMEM((owners * rows, width), F32)],
        compiler_params=params(),
    )(received, w_gate, w_up, w_down)


def combine_kernel(chunks, local_experts, stream_ref, ids_ref, gates_ref, *refs):
    back_refs, out_ref, first_ref, second_ref = refs[:chunks], refs[chunks], refs[-2], refs[-1]
    tokens = stream_ref.shape[0]
    owners, groups, rows, _ = back_refs[0].shape
    span = owners * rows

    @pl.when(pl.program_id(0) == 0)
    def _():
        slot0, slot1 = slot_columns(ids_ref[...], owners * local_experts, local_experts)
        lanes = lax.broadcasted_iota(jnp.int32, first_ref.shape, 1)
        first_ref[...] = jnp.where(slot0 == lanes, 1.0, 0.0).astype(BF16)
        second_ref[...] = jnp.where(slot1 == lanes, 1.0, 0.0).astype(BF16)

    back = jnp.concatenate(
        [
            back_refs[c][:, g].reshape(span, back_refs[c].shape[3])
            for c in range(chunks)
            for g in range(groups)
        ],
        axis=0,
    )
    gates = gates_ref[...]
    total = stream_ref[...].astype(F32)
    total = total + gates[:, 0:1] * contract(first_ref[...], back, ((1,), (0,)))
    total = total + gates[:, 1:2] * contract(second_ref[...], back, ((1,), (0,)))
    out_ref[...] = total.astype(BF16)


def combine(stream, ids, gates, backs, local_experts):
    tokens, width = stream.shape
    owners, groups, rows, _ = backs[0].shape
    chunks = len(backs)
    slots = owners * groups * rows * chunks
    step = min(512, width)
    back_spec = pl.BlockSpec((owners, groups, rows, step), lambda d: (0, 0, 0, d))
    return pl.pallas_call(
        functools.partial(combine_kernel, chunks, local_experts),
        name="combine",
        grid=(width // step,),
        in_specs=[
            pl.BlockSpec((tokens, step), lambda d: (0, d)),
            pl.BlockSpec(ids.shape, lambda d: (0, 0)),
            pl.BlockSpec(gates.shape, lambda d: (0, 0)),
        ]
        + [back_spec] * chunks,
        out_specs=pl.BlockSpec((tokens, step), lambda d: (0, d)),
        out_shape=jax.ShapeDtypeStruct((tokens, width), BF16),
        scratch_shapes=[pltpu.VMEM((tokens, slots), BF16)] * 2,
        compiler_params=params(),
    )(stream, ids, gates, *backs)


def body(
    queries,
    keys,
    values,
    mem_route,
    head_gain,
    residual_in,
    ffn_gain,
    expert_ids,
    expert_gates,
    w_gate,
    w_up,
    w_down,
):
    length = queries.shape[0]
    ctx_count = lax.axis_size("ctx")
    head_count = lax.axis_size("head")
    owners = ctx_count * head_count
    local_experts = w_gate.shape[0]
    pairs = local_experts // PAIR
    chunks = 2 if pairs % 2 == 0 else 1
    route_row = mem_route.reshape(1, length)
    route_col = mem_route.reshape(length, 1)

    states = block_states(keys, values, route_row)
    pieces = lax.all_to_all(states, "ctx", split_axis=0, concat_axis=0, tiled=True)
    before = exclusive_prefix(pieces.reshape(ctx_count, -1, HD))
    carried = lax.all_to_all(
        before.reshape(states.shape), "ctx", split_axis=0, concat_axis=0, tiled=True
    )
    local = local_attention(queries, keys, values, route_row, route_col)
    normed = mix_and_norm(queries, carried, local, route_col, head_gain[None], head_count)
    by_token = lax.all_to_all(normed, "head", split_axis=0, concat_axis=0, tiled=True)

    stream, parcels = pack(
        residual_in, by_token, ffn_gain[None], expert_ids, chunks, owners, local_experts
    )
    backs = []
    for c in range(chunks):
        received = lax.all_to_all(
            parcels[c], ("ctx", "head"), split_axis=0, concat_axis=0, tiled=True
        )
        served = serve_experts(received, w_gate, w_up, w_down, c)
        backs.append(
            lax.all_to_all(served, ("ctx", "head"), split_axis=0, concat_axis=0, tiled=True)
        )
    return combine(stream, expert_ids, expert_gates, backs, local_experts)


def solution(mesh):
    placed = (
        P("ctx", "head"),
        P("ctx", "head"),
        P("ctx", "head"),
        P("ctx"),
        P("head"),
        P(("ctx", "head"), None),
        P(),
        P(("ctx", "head"), None),
        P(("ctx", "head"), None),
        P(("ctx", "head"), None, None),
        P(("ctx", "head"), None, None),
        P(("ctx", "head"), None, None),
    )
    return jax.shard_map(
        body, mesh=mesh, in_specs=placed, out_specs=P(("ctx", "head"), None), check_vma=False
    )
```

```python
import functools

import jax
import jax.numpy as jnp
from jax import lax
from jax.experimental import pallas as pl
from jax.experimental.pallas import tpu as pltpu
from jax.sharding import PartitionSpec as P


HD = 128
M = 4
CAP = 4
PAIR = 2
GROUP_ROWS = PAIR * CAP
EPS = 1e-06
F32 = jnp.float32
BF16 = jnp.bfloat16


def params(**more):
    return pltpu.CompilerParams(vmem_limit_bytes=60 * 1024 * 1024, **more)


def contract(a, b, dims):
    return lax.dot_general(a, b, (dims, ((), ())), preferred_element_type=F32)


def state_kernel(tail, key_ref, value_ref, route_ref, meta_ref, out_ref):
    parts, rows, _ = out_ref.shape
    rows -= tail
    head = pl.program_id(0)
    keys_t = key_ref[...].T
    values = value_ref[...]
    route = route_ref[...]
    states = []
    for m in range(M):
        mask = (route == m).astype(F32).astype(BF16)
        states.append(contract(keys_t * mask, values, ((1,), (0,))).astype(BF16))
    flat = jnp.concatenate(states, axis=0)
    share = M * HD // rows
    for i in range(share):
        out_ref[head * share + i, :rows, :] = flat[i * rows:(i + 1) * rows]

    @pl.when(head == 0)
    def _():
        for p in range(parts):
            out_ref[p, rows:, :] = meta_ref[p].astype(BF16)


def block_states(keys, values, route_row, meta, parts):
    length, width = keys.shape
    heads = width // HD
    rows = heads * M * HD // parts
    tail = meta.shape[1]
    return pl.pallas_call(
        functools.partial(state_kernel, tail),
        name="block_states",
        grid=(heads,),
        in_specs=[
            pl.BlockSpec((length, HD), lambda h: (0, h)),
            pl.BlockSpec((length, HD), lambda h: (0, h)),
            pl.BlockSpec((1, length), lambda h: (0, 0)),
            pl.BlockSpec(meta.shape, lambda h: (0, 0, 0)),
        ],
        out_specs=pl.BlockSpec((parts, rows + tail, HD), lambda h: (0, 0, 0)),
        out_shape=jax.ShapeDtypeStruct((parts, rows + tail, HD), BF16),
        compiler_params=params(),
    )(keys, values, route_row, meta)


def prefix_kernel(ranks, piece_ref, out_ref):
    rows = out_ref.shape[1]
    total = jnp.zeros(out_ref.shape[1:], F32)
    for r in range(ranks):
        out_ref[r] = total.astype(BF16)
        if r + 1 < ranks:
            total = total + piece_ref[r, :rows, :].astype(F32)


def exclusive_prefix(pieces, tail):
    ranks, rows, width = pieces.shape
    return pl.pallas_call(
        functools.partial(prefix_kernel, ranks),
        name="exclusive_prefix",
        out_shape=jax.ShapeDtypeStruct((ranks, rows - tail, width), BF16),
        compiler_params=params(),
    )(pieces)


def local_kernel(rows, query_ref, key_ref, value_ref, route_row_ref, route_col_ref, out_ref, weight_ref):
    length = query_ref.shape[0]

    @pl.when(pl.program_id(0) == 0)
    def _():
        route_row = route_row_ref[...]
        for i in range(length // rows):
            span = (i + 1) * rows
            column = route_col_ref[pl.ds(i * rows, rows), :]
            same = jnp.where(column == route_row[:, :span], 2.0, 1.0)
            t = lax.broadcasted_iota(jnp.int32, (rows, span), 0) + i * rows
            s = lax.broadcasted_iota(jnp.int32, (rows, span), 1)
            weight_ref[pl.ds(i * rows, rows), :span] = jnp.where(t >= s, same, 0.0)

    for i in range(length // rows):
        span = (i + 1) * rows
        query = query_ref[pl.ds(i * rows, rows), :]
        scores = contract(query, key_ref[:span, :], ((1,), (1,)))
        weighted = (scores * weight_ref[pl.ds(i * rows, rows), :span]).astype(BF16)
        out_ref[pl.ds(i * rows, rows), :] = contract(weighted, value_ref[:span, :], ((1,), (0,)))


def local_attention(queries, keys, values, route_row, route_col):
    length, width = queries.shape
    heads = width // HD
    rows = min(256, length)
    wide = pl.BlockSpec((length, HD), lambda h: (0, h))
    return pl.pallas_call(
        functools.partial(local_kernel, rows),
        name="local_attention",
        grid=(heads,),
        in_specs=[
            wide,
            wide,
            wide,
            pl.BlockSpec((1, length), lambda h: (0, 0)),
            pl.BlockSpec((length, 1), lambda h: (0, 0)),
        ],
        out_specs=wide,
        out_shape=jax.ShapeDtypeStruct((length, width), F32),
        scratch_shapes=[pltpu.VMEM((length, length), F32)],
        compiler_params=params(),
    )(queries, keys, values, route_row, route_col)


def mix_kernel(query_ref, state_ref, local_ref, route_col_ref, gain_ref, meta_ref, out_ref):
    parts, rows, _ = out_ref.shape
    blocks = meta_ref.shape[0]
    rows -= blocks
    query = query_ref[...]
    column = route_col_ref[...]
    wide = jnp.concatenate(
        [query * jnp.where(column == m, 2.0, 1.0).astype(BF16) for m in range(M)], axis=1
    )
    mixed = contract(wide, state_ref[...], ((1,), (0,))) + local_ref[...]
    scale = lax.rsqrt(jnp.mean(mixed * mixed, axis=-1, keepdims=True) + EPS)
    normed = (mixed * scale * gain_ref[...]).astype(BF16)
    for p in range(parts):
        out_ref[p, :rows, :] = normed[p * rows:(p + 1) * rows]
        tail = [meta_ref[c, p:p + 1, :].astype(F32) for c in range(blocks)]
        out_ref[p, rows:, :] = jnp.concatenate(tail, axis=0).astype(BF16)


def mix_and_norm(queries, state, local, route_col, head_gain, meta, parts):
    length, width = queries.shape
    rows = length // parts + meta.shape[0]
    heads = width // HD
    wide = pl.BlockSpec((length, HD), lambda h: (0, h))
    return pl.pallas_call(
        mix_kernel,
        name="mix_and_norm",
        grid=(heads,),
        in_specs=[
            wide,
            pl.BlockSpec((M * HD, HD), lambda h: (h, 0)),
            wide,
            pl.BlockSpec((length, 1), lambda h: (0, 0)),
            pl.BlockSpec((1, HD), lambda h: (0, h)),
            pl.BlockSpec(meta.shape, lambda h: (0, 0, 0)),
        ],
        out_specs=pl.BlockSpec((parts, rows, HD), lambda h: (0, 0, h)),
        out_shape=jax.ShapeDtypeStruct((parts, rows, width), BF16),
        compiler_params=params(),
    )(queries, state, local, route_col, head_gain, meta)


def slot_columns(ids, experts, local_experts):
    tokens = ids.shape[0]
    owners = experts // local_experts
    lanes = lax.broadcasted_iota(jnp.int32, (tokens, experts), 1)
    chosen = [(ids[:, j:j + 1] == lanes).astype(F32) for j in range(2)]
    t = lax.broadcasted_iota(jnp.int32, (tokens, tokens), 0)
    s = lax.broadcasted_iota(jnp.int32, (tokens, tokens), 1)
    earlier = contract(
        (t > s).astype(F32).astype(BF16), (chosen[0] + chosen[1]).astype(BF16), ((1,), (0,))
    )
    slots = []
    for j in range(2):
        rank = jnp.sum(earlier * chosen[j], axis=1, keepdims=True).astype(jnp.int32)
        expert = ids[:, j:j + 1]
        owner = expert // local_experts
        local = expert % local_experts
        slots.append(
            ((local // PAIR) * owners + owner) * GROUP_ROWS + (local % PAIR) * CAP + rank
        )
    return slots


def pack_dense_kernel(chunks, local_experts, residual_ref, piece_ref, gain_ref, ids_ref, *refs):
    stream_ref, out_refs = refs[0], refs[1:1 + chunks]
    parts, rows = piece_ref.shape[0], residual_ref.shape[0]
    owners, groups, _, width = out_refs[0].shape
    normed = jnp.concatenate([piece_ref[p, :rows, :] for p in range(parts)], axis=1)
    stream = (residual_ref[...].astype(F32) + normed.astype(F32)).astype(BF16)
    stream_ref[...] = stream
    wide = stream.astype(F32)
    scale = lax.rsqrt(jnp.mean(wide * wide, axis=-1, keepdims=True) + EPS)
    ffn_in = (wide * scale * gain_ref[...]).astype(BF16)
    experts = owners * local_experts
    slot0, slot1 = slot_columns(ids_ref[...], experts, local_experts)
    span = owners * GROUP_ROWS
    for c in range(chunks):
        for g in range(groups):
            base = (c * groups + g) * span
            lanes = lax.broadcasted_iota(jnp.int32, (rows, span), 1) + base
            spread = jnp.where((slot0 == lanes) | (slot1 == lanes), 1.0, 0.0).astype(BF16)
            packed = contract(spread, ffn_in, ((0,), (0,))).astype(BF16)
            out_refs[c][:, g] = packed.reshape(owners, GROUP_ROWS, width)


def pack_dense(residual, pieces, gain, ids, chunks, owners, local_experts):
    tokens, width = residual.shape
    groups = local_experts // PAIR // chunks
    parcel = jax.ShapeDtypeStruct((owners, groups, GROUP_ROWS, width), BF16)
    out = pl.pallas_call(
        functools.partial(pack_dense_kernel, chunks, local_experts),
        name="pack_dense",
        out_shape=[jax.ShapeDtypeStruct((tokens, width), BF16)] + [parcel] * chunks,
        compiler_params=params(),
    )(residual, pieces, gain, ids)
    return out[0], out[1:]


def expert_dense_kernel(x_ref, gate_ref, up_ref, down_ref, out_ref, acc_ref):
    e = pl.program_id(1)
    f = pl.program_id(2)
    owners, rows, width = x_ref.shape
    x = x_ref[...].reshape(owners * rows, width)
    gate = contract(x, gate_ref[...], ((1,), (0,)))
    upward = contract(x, up_ref[...], ((1,), (0,)))
    row = lax.broadcasted_iota(jnp.int32, gate.shape, 0)
    mine = (row // CAP) % PAIR == e
    hidden = gate / (1.0 + jnp.exp(-gate)) * upward
    hidden = jnp.where(mine, hidden, 0.0).astype(BF16)
    part = contract(hidden, down_ref[...], ((1,), (0,)))
    first = (e == 0) & (f == 0)

    @pl.when(first)
    def _():
        acc_ref[...] = part

    @pl.when(jnp.logical_not(first))
    def _():
        acc_ref[...] = acc_ref[...] + part

    @pl.when((e == pl.num_programs(1) - 1) & (f == pl.num_programs(2) - 1))
    def _():
        out_ref[...] = acc_ref[...].astype(BF16).reshape(owners, rows, width)


def serve_dense(received, w_gate, w_up, w_down, chunk):
    owners, groups, rows, width = received.shape
    hidden = w_gate.shape[2]
    split = 2
    step = hidden // split
    first = chunk * groups * PAIR
    token_spec = pl.BlockSpec((owners, None, rows, width), lambda g, e, f: (0, g, 0, 0))
    in_spec = pl.BlockSpec((None, width, step), lambda g, e, f: (first + g * PAIR + e, 0, f))
    return pl.pallas_call(
        expert_dense_kernel,
        grid=(groups, PAIR, split),
        in_specs=[
            token_spec,
            in_spec,
            in_spec,
            pl.BlockSpec((None, step, width), lambda g, e, f: (first + g * PAIR + e, f, 0)),
        ],
        out_specs=token_spec,
        out_shape=jax.ShapeDtypeStruct(received.shape, BF16),
        scratch_shapes=[pltpu.VMEM((owners * rows, width), F32)],
        compiler_params=params(),
    )(received, w_gate, w_up, w_down)


def combine_dense_kernel(chunks, local_experts, stream_ref, ids_ref, gates_ref, *refs):
    back_refs, out_ref, first_ref, second_ref = refs[:chunks], refs[chunks], refs[-2], refs[-1]
    owners, groups, rows, _ = back_refs[0].shape
    span = owners * rows

    @pl.when(pl.program_id(0) == 0)
    def _():
        slot0, slot1 = slot_columns(ids_ref[...], owners * local_experts, local_experts)
        lanes = lax.broadcasted_iota(jnp.int32, first_ref.shape, 1)
        first_ref[...] = jnp.where(slot0 == lanes, 1.0, 0.0).astype(BF16)
        second_ref[...] = jnp.where(slot1 == lanes, 1.0, 0.0).astype(BF16)

    back = jnp.concatenate(
        [
            back_refs[c][:, g].reshape(span, back_refs[c].shape[3])
            for c in range(chunks)
            for g in range(groups)
        ],
        axis=0,
    )
    gates = gates_ref[...]
    total = stream_ref[...].astype(F32)
    total = total + gates[:, 0:1] * contract(first_ref[...], back, ((1,), (0,)))
    total = total + gates[:, 1:2] * contract(second_ref[...], back, ((1,), (0,)))
    out_ref[...] = total.astype(BF16)


def combine_dense(stream, ids, gates, backs, local_experts):
    tokens, width = stream.shape
    owners, groups, rows, _ = backs[0].shape
    chunks = len(backs)
    slots = owners * groups * rows * chunks
    step = min(512, width)
    back_spec = pl.BlockSpec((owners, groups, rows, step), lambda d: (0, 0, 0, d))
    return pl.pallas_call(
        functools.partial(combine_dense_kernel, chunks, local_experts),
        name="combine_dense",
        grid=(width // step,),
        in_specs=[
            pl.BlockSpec((tokens, step), lambda d: (0, d)),
            pl.BlockSpec(ids.shape, lambda d: (0, 0)),
            pl.BlockSpec(gates.shape, lambda d: (0, 0)),
        ]
        + [back_spec] * chunks,
        out_specs=pl.BlockSpec((tokens, step), lambda d: (0, d)),
        out_shape=jax.ShapeDtypeStruct((tokens, width), BF16),
        scratch_shapes=[pltpu.VMEM((tokens, slots), BF16)] * 2,
        compiler_params=params(),
    )(stream, ids, gates, *backs)


def route_kernel(local_experts, plan, ids_ref, code_ref, meta_ref):
    tokens = ids_ref.shape[0]
    owners = meta_ref.shape[0]
    experts = owners * local_experts
    ids = ids_ref[...]
    lanes = lax.broadcasted_iota(jnp.int32, (tokens, experts), 1)
    chosen = [(ids[:, j:j + 1] == lanes).astype(F32) for j in range(2)]
    both = (chosen[0] + chosen[1]).astype(BF16)
    t = lax.broadcasted_iota(jnp.int32, (tokens, tokens), 0)
    s = lax.broadcasted_iota(jnp.int32, (tokens, tokens), 1)
    earlier = contract((t > s).astype(F32).astype(BF16), both, ((1,), (0,)))
    counts = contract(jnp.ones((8, tokens), BF16), both, ((1,), (0,)))
    row = lax.broadcasted_iota(jnp.int32, (experts, experts), 0)
    col = lax.broadcasted_iota(jnp.int32, (experts, experts), 1)
    mates = row // local_experts == col // local_experts
    below = jnp.where(mates & (row < col), 1.0, 0.0).astype(BF16)
    ahead = jnp.where(mates & (row % local_experts < plan.ahead), 1.0, 0.0).astype(BF16)
    offsets = contract(counts.astype(BF16), below, ((1,), (0,)))[0:1]
    aheads = contract(counts.astype(BF16), ahead, ((1,), (0,)))[0:1]
    slot_lane = lax.broadcasted_iota(jnp.int32, code_ref.shape, 1)
    code = jnp.zeros(code_ref.shape, jnp.int32)
    owner_lane = lax.broadcasted_iota(jnp.int32, (tokens, owners), 1)
    local_lane = lax.broadcasted_iota(jnp.int32, (tokens, meta_ref.shape[1]), 1)
    parcel_counts = 0.0
    for j in range(2):
        expert = ids[:, j:j + 1]
        owner = expert // local_experts
        local = expert % local_experts
        place = jnp.sum((earlier + offsets) * chosen[j], axis=1, keepdims=True).astype(jnp.int32)
        front = jnp.sum(aheads * chosen[j], axis=1, keepdims=True).astype(jnp.int32)
        back = jnp.where(
            (local < plan.ahead) & (place < plan.back[0]),
            place,
            plan.back[0] + place - jnp.minimum(front, plan.back[0]),
        )
        for lane, value in ((j, owner), (2 + j, place), (4 + j, back)):
            code = jnp.where(slot_lane == lane, value, code)
        parcel_counts = parcel_counts + contract(
            (owner == owner_lane).astype(F32).astype(BF16),
            (local == local_lane).astype(F32).astype(BF16),
            ((0,), (0,)),
        )
    code_ref[...] = code
    total = jnp.sum(parcel_counts, axis=1, keepdims=True)
    lane = lax.broadcasted_iota(jnp.int32, meta_ref.shape, 1)
    front = jnp.sum(jnp.where(lane < plan.ahead, parcel_counts, 0.0), axis=1, keepdims=True)
    over = (total > sum(plan.out[:2])) | (
        total - jnp.minimum(front, plan.back[0]) > plan.back[1]
    )
    flag = jnp.max(jnp.where(over, 1.0, 0.0), axis=0, keepdims=True)
    meta_ref[...] = jnp.where(lane == local_experts, flag, parcel_counts)


def route(ids, owners, local_experts, plan):
    return pl.pallas_call(
        functools.partial(route_kernel, local_experts, plan),
        name="route",
        out_shape=[
            jax.ShapeDtypeStruct((ids.shape[0], 128), jnp.int32),
            jax.ShapeDtypeStruct((owners, 128), F32),
        ],
        compiler_params=params(),
    )(ids)


class Plan:
    def __init__(self, local_experts):
        dense = local_experts * CAP
        self.ahead = local_experts // 2
        first = self.ahead * CAP
        self.out = (first, first // 2, dense - first - first // 2)
        self.back = (first // 2, first, dense - first - first // 2)


def in_round(place, bounds, k, owner):
    low = sum(bounds[:k])
    inside = (place >= low) & (place < low + bounds[k])
    return jnp.where(inside, owner * bounds[k] + place - low, -1)


def one_hot(column, width):
    lanes = lax.broadcasted_iota(jnp.int32, (column.shape[0], width), 1)
    return jnp.where(column == lanes, 1.0, 0.0).astype(BF16)


def pack_kernel(
    plan, local_experts, residual_ref, piece_ref, gain_ref, code_ref, stream_ref, meta_ref, flag_ref, *out_refs
):
    parts, rows = piece_ref.shape[0], residual_ref.shape[0]
    normed = jnp.concatenate([piece_ref[p, :rows, :] for p in range(parts)], axis=1)
    tails = [piece_ref[p, rows:, :meta_ref.shape[2]].astype(F32) for p in range(parts)]
    over = 0.0
    for p, tail in enumerate(tails):
        meta_ref[p] = tail.astype(jnp.int32)
        lane = lax.broadcasted_iota(jnp.int32, tail.shape, 1)
        over = jnp.maximum(over, jnp.max(jnp.where(lane == local_experts, tail, 0.0)))
    flag = (over > 0.5).astype(jnp.int32)
    flag_ref[0] = flag
    stream = (residual_ref[...].astype(F32) + normed.astype(F32)).astype(BF16)
    stream_ref[...] = stream
    wide = stream.astype(F32)
    scale = lax.rsqrt(jnp.mean(wide * wide, axis=-1, keepdims=True) + EPS)
    ffn_in = (wide * scale * gain_ref[...]).astype(BF16)
    code = code_ref[...]

    def fill(k):
        owners, rows, width = out_refs[k].shape
        spread = sum(
            one_hot(
                in_round(code[:, 2 + j:3 + j], plan.out, k, code[:, j:j + 1]), owners * rows
            )
            for j in range(2)
        )
        packed = contract(spread, ffn_in, ((0,), (0,))).astype(BF16)
        out_refs[k][...] = packed.reshape(owners, rows, width)

    fill(0)
    fill(1)

    @pl.when(flag > 0)
    def _():
        fill(2)


VMEM = pl.BlockSpec(memory_space=pltpu.VMEM)
SMEM = pl.BlockSpec(memory_space=pltpu.SMEM)


def pack(residual, pieces, gain, code, local_experts, plan):
    tokens, width = residual.shape
    parts, rows, _ = pieces.shape
    blocks = rows - tokens
    owners = parts * blocks
    out = pl.pallas_call(
        functools.partial(pack_kernel, plan, local_experts),
        name="pack",
        in_specs=[VMEM] * 4,
        out_specs=[VMEM, VMEM, SMEM] + [VMEM] * 3,
        out_shape=[
            jax.ShapeDtypeStruct((tokens, width), BF16),
            jax.ShapeDtypeStruct((parts, blocks, 128), jnp.int32),
            jax.ShapeDtypeStruct((1,), jnp.int32),
        ]
        + [jax.ShapeDtypeStruct((owners, rows, width), BF16) for rows in plan.out],
        compiler_params=params(),
    )(residual, pieces, gain, code)
    meta = jnp.swapaxes(out[1], 0, 1).reshape(owners, 128)
    return out[0], meta, out[2], out[3:]


def batch_columns(meta, expert, local_experts, plan):
    owners = meta.shape[0]
    counts = jnp.where(
        lax.broadcasted_iota(jnp.int32, meta.shape, 1) < local_experts, meta, 0
    ).astype(F32)
    lanes = counts.shape[1]
    row = lax.broadcasted_iota(jnp.int32, (lanes, lanes), 0)
    col = lax.broadcasted_iota(jnp.int32, (lanes, lanes), 1)
    below = jnp.where(row < col, 1.0, 0.0).astype(BF16)
    offsets = contract(counts.astype(BF16), below, ((1,), (0,)))
    batch = owners * CAP
    source_row = lax.broadcasted_iota(jnp.int32, (batch, owners), 0) // CAP
    source_col = lax.broadcasted_iota(jnp.int32, (batch, owners), 1)
    expand = jnp.where(source_row == source_col, 1.0, 0.0).astype(BF16)
    lane = lax.broadcasted_iota(jnp.int32, (batch, lanes), 1)

    def column(values, picked):
        wide = contract(expand, values.astype(BF16), ((1,), (0,)))
        return jnp.sum(jnp.where(picked, wide, 0.0), axis=1, keepdims=True).astype(jnp.int32)

    count = column(counts, lane == expert)
    offset = column(offsets, lane == expert)
    front = column(counts, lane < plan.ahead)
    index = lax.broadcasted_iota(jnp.int32, (batch, 1), 0)
    rank = index % CAP
    valid = rank < count
    place = offset + rank
    back = jnp.where(
        (expert < plan.ahead) & (place < plan.back[0]),
        place,
        plan.back[0] + place - jnp.minimum(front, plan.back[0]),
    )
    return index // CAP, jnp.where(valid, place, -1), jnp.where(valid, back, -1)


def expert_kernel(
    first, taken, given, has_base, local_experts, plan, flag_ref, meta_ref, *refs
):
    x_refs, refs = refs[:len(taken)], refs[len(taken):]
    gate_ref, up_ref, down_ref = refs[:3]
    base_ref = refs[3] if has_base else None
    refs = refs[3 + has_base:]
    out_refs, (batch_ref, acc_ref, done_ref) = refs[:len(given)], refs[len(given):]
    e = pl.program_id(0)
    f = pl.program_id(1)
    last_f = pl.num_programs(1) - 1
    batch = batch_ref.shape[0]
    meta = meta_ref[...]

    @pl.when(f == 0)
    def _():
        source, place, _ = batch_columns(meta, first + e, local_experts, plan)

        def rows_of(i, k):
            owners, rows, width = x_refs[i].shape
            spread = one_hot(in_round(place, plan.out, k, source), owners * rows)
            return contract(spread, x_refs[i][...].reshape(owners * rows, width), ((1,), (0,)))

        total = 0.0
        for i, k in enumerate(taken):
            if k < 2:
                total = total + rows_of(i, k)
        batch_ref[...] = total.astype(BF16)
        for i, k in enumerate(taken):
            if k == 2:

                @pl.when(flag_ref[0] > 0)
                def _():
                    batch_ref[...] = batch_ref[...] + rows_of(i, k).astype(BF16)

    x = batch_ref[...]
    gate = contract(x, gate_ref[...], ((1,), (0,)))
    upward = contract(x, up_ref[...], ((1,), (0,)))
    hidden = (gate / (1.0 + jnp.exp(-gate)) * upward).astype(BF16)
    part = contract(hidden, down_ref[...], ((1,), (0,)))

    @pl.when(f == 0)
    def _():
        acc_ref[...] = part

    @pl.when((f > 0) & (f < last_f))
    def _():
        acc_ref[...] = acc_ref[...] + part

    @pl.when(f == last_f)
    def _():
        done_ref[e] = (acc_ref[...] + part).astype(BF16)

    @pl.when((e == pl.num_programs(0) - 1) & (f == last_f))
    def _():
        count = done_ref.shape[0]
        columns = [batch_columns(meta, first + i, local_experts, plan) for i in range(count)]
        source = jnp.concatenate([c[0] for c in columns], axis=0)
        back = jnp.concatenate([c[2] for c in columns], axis=0)
        done = done_ref[...].reshape(count * batch, done_ref.shape[2])

        def put(i, k):
            owners, rows, width = out_refs[i].shape
            spread = one_hot(in_round(back, plan.back, k, source), owners * rows)
            rows_out = contract(spread, done, ((0,), (0,)))
            if has_base and k == 1:
                rows_out = rows_out + base_ref[...].reshape(owners * rows, width).astype(F32)
            out_refs[i][...] = rows_out.astype(BF16).reshape(owners, rows, width)

        for i, k in enumerate(given):
            if k < 2:
                put(i, k)
            else:

                @pl.when(flag_ref[0] > 0)
                def _():
                    put(i, k)


def serve_experts(flag, meta, received, weights, base, first, taken, given, plan):
    w_gate, w_up, w_down = weights
    local_experts, width, hidden = w_gate.shape
    owners = meta.shape[0]
    count = plan.ahead
    split = 2
    step = hidden // split

    def whole(x):
        return pl.BlockSpec(x.shape, lambda e, f: (0,) * len(x.shape))

    in_spec = pl.BlockSpec((None, width, step), lambda e, f: (first + e, 0, f))
    extra = [] if base is None else [base]
    outs = [jax.ShapeDtypeStruct((owners, plan.back[k], width), BF16) for k in given]
    batch = owners * CAP
    return pl.pallas_call(
        functools.partial(
            expert_kernel, first, taken, given, base is not None, local_experts, plan
        ),
        grid=(count, split),
        in_specs=[SMEM, whole(meta)]
        + [whole(x) for x in received]
        + [
            in_spec,
            in_spec,
            pl.BlockSpec((None, step, width), lambda e, f: (first + e, f, 0)),
        ]
        + [whole(x) for x in extra],
        out_specs=[whole(x) for x in outs],
        out_shape=outs,
        scratch_shapes=[
            pltpu.VMEM((batch, width), BF16),
            pltpu.VMEM((batch, width), F32),
            pltpu.VMEM((count, batch, width), BF16),
        ],
        compiler_params=params(),
    )(flag, meta, *received, w_gate, w_up, w_down, *extra)


def combine_kernel(plan, flag_ref, stream_ref, code_ref, gates_ref, *refs):
    back_refs, out_ref, acc_ref = refs[:3], refs[3], refs[4]
    code = code_ref[...]
    gates = gates_ref[...]

    def part(k):
        owners, rows, width = back_refs[k].shape
        flat = back_refs[k][...].reshape(owners * rows, width)
        total = 0.0
        for j in range(2):
            spread = one_hot(
                in_round(code[:, 4 + j:5 + j], plan.back, k, code[:, j:j + 1]), owners * rows
            )
            total = total + gates[:, j:j + 1] * contract(spread, flat, ((1,), (0,)))
        return total

    acc_ref[...] = stream_ref[...].astype(F32) + part(0) + part(1)

    @pl.when(flag_ref[0] > 0)
    def _():
        acc_ref[...] = acc_ref[...] + part(2)

    out_ref[...] = acc_ref[...].astype(BF16)


def combine(flag, stream, code, gates, backs, plan):
    return pl.pallas_call(
        functools.partial(combine_kernel, plan),
        name="combine",
        in_specs=[SMEM] + [VMEM] * (3 + len(backs)),
        out_specs=VMEM,
        out_shape=jax.ShapeDtypeStruct(stream.shape, BF16),
        scratch_shapes=[pltpu.VMEM(stream.shape, F32)],
        compiler_params=params(),
    )(flag, stream, code, gates, *backs)


def everywhere(x):
    return lax.all_to_all(x, ("ctx", "head"), split_axis=0, concat_axis=0, tiled=True)


def everywhere_if(flag, x):
    return lax.cond(flag[0] > 0, everywhere, lambda y: y, x)


def body(
    queries,
    keys,
    values,
    mem_route,
    head_gain,
    residual_in,
    ffn_gain,
    expert_ids,
    expert_gates,
    w_gate,
    w_up,
    w_down,
):
    length = queries.shape[0]
    ctx_count = lax.axis_size("ctx")
    head_count = lax.axis_size("head")
    owners = ctx_count * head_count
    local_experts = w_gate.shape[0]
    compact = local_experts * CAP % (4 * GROUP_ROWS) == 0
    if compact:
        plan = Plan(local_experts)
        code, meta_out = route(expert_ids, owners, local_experts, plan)
        meta = everywhere(meta_out.reshape(owners, 1, -1)).reshape(owners, -1)
        flag = jnp.max(meta[:, local_experts])[None]
    route_row = mem_route.reshape(1, length)
    route_col = mem_route.reshape(length, 1)

    compact = local_experts * CAP % (4 * GROUP_ROWS) == 0
    if compact:
        plan = Plan(local_experts)
        code, counts = route(expert_ids, owners, local_experts, plan)
        tail = jnp.pad(counts.reshape(ctx_count, head_count, HD), ((0, 0), (0, -head_count % 8), (0, 0)))
    else:
        tail = jnp.zeros((ctx_count, head_count, HD), F32)
    tail_rows = tail.shape[1]
    states = block_states(keys, values, route_row, tail, ctx_count)
    pieces = lax.all_to_all(states, "ctx", split_axis=0, concat_axis=0, tiled=True)
    before = exclusive_prefix(pieces, tail_rows)
    carried = lax.all_to_all(before, "ctx", split_axis=0, concat_axis=0, tiled=True).reshape(-1, HD)
    local = local_attention(queries, keys, values, route_row, route_col)
    normed = mix_and_norm(
        queries, carried, local, route_col, head_gain[None], pieces[:, -tail_rows:], head_count
    )
    by_token = lax.all_to_all(normed, "head", split_axis=0, concat_axis=0, tiled=True)

    if compact:
        weights = (w_gate, w_up, w_down)
        stream, meta, flag, parcels = pack(
            residual_in, by_token, ffn_gain[None], code, local_experts, plan
        )
        received = [everywhere(parcels[0]), everywhere(parcels[1])]
        back_0, base = serve_experts(flag, meta, received[:1], weights, None, 0, (0,), (0, 1), plan)
        received.append(everywhere_if(flag, parcels[2]))
        back_0 = everywhere(back_0)
        back_1, back_2 = serve_experts(
            flag, meta, received, weights, base, plan.ahead, (0, 1, 2), (1, 2), plan
        )
        back_2 = everywhere_if(flag, back_2)
        back_1 = everywhere(back_1)
        backs = [back_0, back_1, back_2]
        return combine(flag, stream, code, expert_gates, backs, plan)

    pairs = local_experts // PAIR
    chunks = 2 if pairs % 2 == 0 else 1
    stream, parcels = pack_dense(
        residual_in, by_token, ffn_gain[None], expert_ids, chunks, owners, local_experts
    )
    backs = []
    for c in range(chunks):
        received = lax.all_to_all(
            parcels[c], ("ctx", "head"), split_axis=0, concat_axis=0, tiled=True
        )
        served = serve_dense(received, w_gate, w_up, w_down, c)
        backs.append(
            lax.all_to_all(served, ("ctx", "head"), split_axis=0, concat_axis=0, tiled=True)
        )
    return combine_dense(stream, expert_ids, expert_gates, backs, local_experts)


def solution(mesh):
    placed = (
        P("ctx", "head"),
        P("ctx", "head"),
        P("ctx", "head"),
        P("ctx"),
        P("head"),
        P(("ctx", "head"), None),
        P(),
        P(("ctx", "head"), None),
        P(("ctx", "head"), None),
        P(("ctx", "head"), None, None),
        P(("ctx", "head"), None, None),
        P(("ctx", "head"), None, None),
    )
    return jax.shard_map(
        body, mesh=mesh, in_specs=placed, out_specs=P(("ctx", "head"), None), check_vma=False
    )
```

```python
import functools

import jax
import jax.numpy as jnp
from jax import lax
from jax.experimental import pallas as pl
from jax.experimental.pallas import tpu as pltpu
from jax.sharding import PartitionSpec as P


HD = 128
M = 4
CAP = 4
PAIR = 2
GROUP_ROWS = PAIR * CAP
EPS = 1e-06
F32 = jnp.float32
BF16 = jnp.bfloat16


def params(**more):
    return pltpu.CompilerParams(vmem_limit_bytes=60 * 1024 * 1024, **more)


def contract(a, b, dims):
    return lax.dot_general(a, b, (dims, ((), ())), preferred_element_type=F32)


def state_kernel(key_ref, value_ref, route_ref, out_ref):
    keys_t = key_ref[...].T
    values = value_ref[...]
    route = route_ref[...]
    for m in range(M):
        mask = (route == m).astype(F32).astype(BF16)
        out_ref[pl.ds(m * HD, HD), :] = contract(keys_t * mask, values, ((1,), (0,))).astype(BF16)


def block_states(keys, values, route_row):
    length, width = keys.shape
    heads = width // HD
    return pl.pallas_call(
        state_kernel,
        name="block_states",
        grid=(heads,),
        in_specs=[
            pl.BlockSpec((length, HD), lambda h: (0, h)),
            pl.BlockSpec((length, HD), lambda h: (0, h)),
            pl.BlockSpec((1, length), lambda h: (0, 0)),
        ],
        out_specs=pl.BlockSpec((M * HD, HD), lambda h: (h, 0)),
        out_shape=jax.ShapeDtypeStruct((heads * M * HD, HD), BF16),
        compiler_params=params(),
    )(keys, values, route_row)


def prefix_kernel(ranks, piece_ref, out_ref):
    total = jnp.zeros(piece_ref.shape[1:], F32)
    for r in range(ranks):
        out_ref[r] = total.astype(BF16)
        if r + 1 < ranks:
            total = total + piece_ref[r].astype(F32)


def exclusive_prefix(pieces):
    return pl.pallas_call(
        functools.partial(prefix_kernel, pieces.shape[0]),
        name="exclusive_prefix",
        out_shape=jax.ShapeDtypeStruct(pieces.shape, BF16),
        compiler_params=params(),
    )(pieces)


def local_kernel(rows, query_ref, key_ref, value_ref, route_row_ref, route_col_ref, out_ref, weight_ref):
    length = query_ref.shape[0]

    @pl.when(pl.program_id(0) == 0)
    def _():
        route_row = route_row_ref[...]
        for i in range(length // rows):
            span = (i + 1) * rows
            column = route_col_ref[pl.ds(i * rows, rows), :]
            same = jnp.where(column == route_row[:, :span], 2.0, 1.0)
            t = lax.broadcasted_iota(jnp.int32, (rows, span), 0) + i * rows
            s = lax.broadcasted_iota(jnp.int32, (rows, span), 1)
            weight_ref[pl.ds(i * rows, rows), :span] = jnp.where(t >= s, same, 0.0)

    for i in range(length // rows):
        span = (i + 1) * rows
        query = query_ref[pl.ds(i * rows, rows), :]
        scores = contract(query, key_ref[:span, :], ((1,), (1,)))
        weighted = (scores * weight_ref[pl.ds(i * rows, rows), :span]).astype(BF16)
        out_ref[pl.ds(i * rows, rows), :] = contract(weighted, value_ref[:span, :], ((1,), (0,)))


def local_attention(queries, keys, values, route_row, route_col):
    length, width = queries.shape
    heads = width // HD
    rows = min(256, length)
    wide = pl.BlockSpec((length, HD), lambda h: (0, h))
    return pl.pallas_call(
        functools.partial(local_kernel, rows),
        name="local_attention",
        grid=(heads,),
        in_specs=[
            wide,
            wide,
            wide,
            pl.BlockSpec((1, length), lambda h: (0, 0)),
            pl.BlockSpec((length, 1), lambda h: (0, 0)),
        ],
        out_specs=wide,
        out_shape=jax.ShapeDtypeStruct((length, width), F32),
        scratch_shapes=[pltpu.VMEM((length, length), F32)],
        compiler_params=params(),
    )(queries, keys, values, route_row, route_col)


def mix_kernel(query_ref, state_ref, local_ref, route_col_ref, gain_ref, out_ref):
    parts, rows, _ = out_ref.shape
    query = query_ref[...]
    column = route_col_ref[...]
    wide = jnp.concatenate(
        [query * jnp.where(column == m, 2.0, 1.0).astype(BF16) for m in range(M)], axis=1
    )
    mixed = contract(wide, state_ref[...], ((1,), (0,))) + local_ref[...]
    scale = lax.rsqrt(jnp.mean(mixed * mixed, axis=-1, keepdims=True) + EPS)
    normed = (mixed * scale * gain_ref[...]).astype(BF16)
    for p in range(parts):
        out_ref[p] = normed[p * rows:(p + 1) * rows]


def mix_and_norm(queries, state, local, route_col, head_gain, parts):
    length, width = queries.shape
    heads = width // HD
    wide = pl.BlockSpec((length, HD), lambda h: (0, h))
    return pl.pallas_call(
        mix_kernel,
        name="mix_and_norm",
        grid=(heads,),
        in_specs=[
            wide,
            pl.BlockSpec((M * HD, HD), lambda h: (h, 0)),
            wide,
            pl.BlockSpec((length, 1), lambda h: (0, 0)),
            pl.BlockSpec((1, HD), lambda h: (0, h)),
        ],
        out_specs=pl.BlockSpec((parts, length // parts, HD), lambda h: (0, 0, h)),
        out_shape=jax.ShapeDtypeStruct((parts, length // parts, width), BF16),
        compiler_params=params(),
    )(queries, state, local, route_col, head_gain)


def slot_columns(ids, experts, local_experts):
    tokens = ids.shape[0]
    owners = experts // local_experts
    lanes = lax.broadcasted_iota(jnp.int32, (tokens, experts), 1)
    chosen = [(ids[:, j:j + 1] == lanes).astype(F32) for j in range(2)]
    t = lax.broadcasted_iota(jnp.int32, (tokens, tokens), 0)
    s = lax.broadcasted_iota(jnp.int32, (tokens, tokens), 1)
    earlier = contract(
        (t > s).astype(F32).astype(BF16), (chosen[0] + chosen[1]).astype(BF16), ((1,), (0,))
    )
    slots = []
    for j in range(2):
        rank = jnp.sum(earlier * chosen[j], axis=1, keepdims=True).astype(jnp.int32)
        expert = ids[:, j:j + 1]
        owner = expert // local_experts
        local = expert % local_experts
        slots.append(
            ((local // PAIR) * owners + owner) * GROUP_ROWS + (local % PAIR) * CAP + rank
        )
    return slots


def pack_dense_kernel(chunks, local_experts, residual_ref, piece_ref, gain_ref, ids_ref, *refs):
    stream_ref, out_refs = refs[0], refs[1:1 + chunks]
    parts, rows, _ = piece_ref.shape
    owners, groups, _, width = out_refs[0].shape
    normed = jnp.concatenate([piece_ref[p] for p in range(parts)], axis=1)
    stream = (residual_ref[...].astype(F32) + normed.astype(F32)).astype(BF16)
    stream_ref[...] = stream
    wide = stream.astype(F32)
    scale = lax.rsqrt(jnp.mean(wide * wide, axis=-1, keepdims=True) + EPS)
    ffn_in = (wide * scale * gain_ref[...]).astype(BF16)
    experts = owners * local_experts
    slot0, slot1 = slot_columns(ids_ref[...], experts, local_experts)
    span = owners * GROUP_ROWS
    for c in range(chunks):
        for g in range(groups):
            base = (c * groups + g) * span
            lanes = lax.broadcasted_iota(jnp.int32, (rows, span), 1) + base
            spread = jnp.where((slot0 == lanes) | (slot1 == lanes), 1.0, 0.0).astype(BF16)
            packed = contract(spread, ffn_in, ((0,), (0,))).astype(BF16)
            out_refs[c][:, g] = packed.reshape(owners, GROUP_ROWS, width)


def pack_dense(residual, pieces, gain, ids, chunks, owners, local_experts):
    tokens, width = residual.shape
    groups = local_experts // PAIR // chunks
    parcel = jax.ShapeDtypeStruct((owners, groups, GROUP_ROWS, width), BF16)
    out = pl.pallas_call(
        functools.partial(pack_dense_kernel, chunks, local_experts),
        name="pack_dense",
        out_shape=[jax.ShapeDtypeStruct((tokens, width), BF16)] + [parcel] * chunks,
        compiler_params=params(),
    )(residual, pieces, gain, ids)
    return out[0], out[1:]


def expert_dense_kernel(x_ref, gate_ref, up_ref, down_ref, out_ref, acc_ref):
    e = pl.program_id(1)
    f = pl.program_id(2)
    owners, rows, width = x_ref.shape
    x = x_ref[...].reshape(owners * rows, width)
    gate = contract(x, gate_ref[...], ((1,), (0,)))
    upward = contract(x, up_ref[...], ((1,), (0,)))
    row = lax.broadcasted_iota(jnp.int32, gate.shape, 0)
    mine = (row // CAP) % PAIR == e
    hidden = gate / (1.0 + jnp.exp(-gate)) * upward
    hidden = jnp.where(mine, hidden, 0.0).astype(BF16)
    part = contract(hidden, down_ref[...], ((1,), (0,)))
    first = (e == 0) & (f == 0)

    @pl.when(first)
    def _():
        acc_ref[...] = part

    @pl.when(jnp.logical_not(first))
    def _():
        acc_ref[...] = acc_ref[...] + part

    @pl.when((e == pl.num_programs(1) - 1) & (f == pl.num_programs(2) - 1))
    def _():
        out_ref[...] = acc_ref[...].astype(BF16).reshape(owners, rows, width)


def serve_dense(received, w_gate, w_up, w_down, chunk):
    owners, groups, rows, width = received.shape
    hidden = w_gate.shape[2]
    split = 2
    step = hidden // split
    first = chunk * groups * PAIR
    token_spec = pl.BlockSpec((owners, None, rows, width), lambda g, e, f: (0, g, 0, 0))
    in_spec = pl.BlockSpec((None, width, step), lambda g, e, f: (first + g * PAIR + e, 0, f))
    return pl.pallas_call(
        expert_dense_kernel,
        grid=(groups, PAIR, split),
        in_specs=[
            token_spec,
            in_spec,
            in_spec,
            pl.BlockSpec((None, step, width), lambda g, e, f: (first + g * PAIR + e, f, 0)),
        ],
        out_specs=token_spec,
        out_shape=jax.ShapeDtypeStruct(received.shape, BF16),
        scratch_shapes=[pltpu.VMEM((owners * rows, width), F32)],
        compiler_params=params(),
    )(received, w_gate, w_up, w_down)


def combine_dense_kernel(chunks, local_experts, stream_ref, ids_ref, gates_ref, *refs):
    back_refs, out_ref, first_ref, second_ref = refs[:chunks], refs[chunks], refs[-2], refs[-1]
    owners, groups, rows, _ = back_refs[0].shape
    span = owners * rows

    @pl.when(pl.program_id(0) == 0)
    def _():
        slot0, slot1 = slot_columns(ids_ref[...], owners * local_experts, local_experts)
        lanes = lax.broadcasted_iota(jnp.int32, first_ref.shape, 1)
        first_ref[...] = jnp.where(slot0 == lanes, 1.0, 0.0).astype(BF16)
        second_ref[...] = jnp.where(slot1 == lanes, 1.0, 0.0).astype(BF16)

    back = jnp.concatenate(
        [
            back_refs[c][:, g].reshape(span, back_refs[c].shape[3])
            for c in range(chunks)
            for g in range(groups)
        ],
        axis=0,
    )
    gates = gates_ref[...]
    total = stream_ref[...].astype(F32)
    total = total + gates[:, 0:1] * contract(first_ref[...], back, ((1,), (0,)))
    total = total + gates[:, 1:2] * contract(second_ref[...], back, ((1,), (0,)))
    out_ref[...] = total.astype(BF16)


def combine_dense(stream, ids, gates, backs, local_experts):
    tokens, width = stream.shape
    owners, groups, rows, _ = backs[0].shape
    chunks = len(backs)
    slots = owners * groups * rows * chunks
    step = min(512, width)
    back_spec = pl.BlockSpec((owners, groups, rows, step), lambda d: (0, 0, 0, d))
    return pl.pallas_call(
        functools.partial(combine_dense_kernel, chunks, local_experts),
        name="combine_dense",
        grid=(width // step,),
        in_specs=[
            pl.BlockSpec((tokens, step), lambda d: (0, d)),
            pl.BlockSpec(ids.shape, lambda d: (0, 0)),
            pl.BlockSpec(gates.shape, lambda d: (0, 0)),
        ]
        + [back_spec] * chunks,
        out_specs=pl.BlockSpec((tokens, step), lambda d: (0, d)),
        out_shape=jax.ShapeDtypeStruct((tokens, width), BF16),
        scratch_shapes=[pltpu.VMEM((tokens, slots), BF16)] * 2,
        compiler_params=params(),
    )(stream, ids, gates, *backs)


class Plan:
    def __init__(self, local_experts):
        dense = local_experts * CAP
        self.ahead = local_experts // 2
        first = self.ahead * CAP
        self.out = (first, first // 2, dense - first - first // 2)
        self.back = (first // 2, first, dense - first - first // 2)


def in_round(place, bounds, k, owner):
    low = sum(bounds[:k])
    inside = (place >= low) & (place < low + bounds[k])
    return jnp.where(inside, owner * bounds[k] + place - low, -1)


def one_hot(column, width):
    lanes = lax.broadcasted_iota(jnp.int32, (column.shape[0], width), 1)
    return jnp.where(column == lanes, 1.0, 0.0).astype(BF16)


VMEM = pl.BlockSpec(memory_space=pltpu.VMEM)
SMEM = pl.BlockSpec(memory_space=pltpu.SMEM)


def route_kernel(local_experts, plan, parts, head_ref, *refs):
    id_refs, (code_ref, meta_ref), spread_refs = refs[:parts], refs[parts:parts + 2], refs[parts + 2:]
    tokens = id_refs[0].shape[1]
    contexts = meta_ref.shape[0]
    owners = contexts * parts
    experts = owners * local_experts
    head = head_ref[0]
    t = lax.broadcasted_iota(jnp.int32, (tokens, tokens), 0)
    s = lax.broadcasted_iota(jnp.int32, (tokens, tokens), 1)
    earlier_mask = (t > s).astype(F32).astype(BF16)
    row = lax.broadcasted_iota(jnp.int32, (experts, experts), 0)
    col = lax.broadcasted_iota(jnp.int32, (experts, experts), 1)
    mates = row // local_experts == col // local_experts
    below = jnp.where(mates & (row < col), 1.0, 0.0).astype(BF16)
    ahead = jnp.where(mates & (row % local_experts < plan.ahead), 1.0, 0.0).astype(BF16)
    lanes = lax.broadcasted_iota(jnp.int32, (tokens, experts), 1)
    owner_lane = lax.broadcasted_iota(jnp.int32, (tokens, owners), 1)
    local_lane = lax.broadcasted_iota(jnp.int32, (tokens, HD), 1)
    owner_row = lax.broadcasted_iota(jnp.int32, (contexts, owners), 1)
    context_row = lax.broadcasted_iota(jnp.int32, (contexts, owners), 0)
    mine = jnp.where(owner_row == context_row * parts + head, 1.0, 0.0).astype(BF16)
    lane = lax.broadcasted_iota(jnp.int32, (owners, HD), 1)
    pair_rows = [ref[...].astype(F32) for ref in id_refs]
    id_rows = jnp.concatenate(pair_rows + [jnp.zeros((-2 * parts % 8, tokens), F32)] * (2 * parts % 8 > 0), axis=0)
    id_cols = id_rows.T
    flags = 0.0
    metas = []
    for b in range(parts):
        ids = [id_cols[:, 2 * b + j:2 * b + j + 1].astype(jnp.int32) for j in range(2)]
        chosen = [(i == lanes).astype(F32) for i in ids]
        both = (chosen[0] + chosen[1]).astype(BF16)
        counts = contract(jnp.ones((8, tokens), BF16), both, ((1,), (0,))).astype(BF16)
        position = contract(earlier_mask, both, ((1,), (0,))) + contract(counts, below, ((1,), (0,)))[0:1]
        places = [jnp.sum(position * c, axis=1, keepdims=True) for c in chosen]
        wide = jnp.concatenate(places + [jnp.zeros((tokens, HD - 2), F32)], axis=1)
        place_rows = wide.T[0:8]
        parcel_counts = 0.0
        for j in range(2):
            parcel_counts = parcel_counts + contract(
                (ids[j] // local_experts == owner_lane).astype(F32).astype(BF16),
                (ids[j] % local_experts == local_lane).astype(F32).astype(BF16),
                ((0,), (0,)),
            )
        if b == 0:
            aheads = contract(counts, ahead, ((1,), (0,)))[0:1]
            slot_lane = lax.broadcasted_iota(jnp.int32, code_ref.shape, 1)
            code = jnp.zeros(code_ref.shape, jnp.int32)
            for j in range(2):
                place = places[j].astype(jnp.int32)
                front = jnp.sum(aheads * chosen[j], axis=1, keepdims=True).astype(jnp.int32)
                back = jnp.where(
                    (ids[j] % local_experts < plan.ahead) & (place < plan.back[0]),
                    place,
                    plan.back[0] + place - jnp.minimum(front, plan.back[0]),
                )
                code = jnp.where(slot_lane == j, ids[j] // local_experts, code)
                code = jnp.where(slot_lane == 4 + j, back, code)
            code_ref[...] = code
        for k, spread_ref in enumerate(spread_refs):
            slots = spread_ref.shape[1]
            slot = lax.broadcasted_iota(jnp.int32, (slots, tokens), 0)
            hit = None
            for j in range(2):
                owner = id_rows[2 * b + j:2 * b + j + 1].astype(jnp.int32) // local_experts
                index = in_round(place_rows[j:j + 1].astype(jnp.int32), plan.out, k, owner)
                hit = (slot == index) if hit is None else hit | (slot == index)
            spread_ref[b] = jnp.where(hit, 1.0, 0.0).astype(BF16)
        total = jnp.sum(parcel_counts, axis=1, keepdims=True)
        front = jnp.sum(jnp.where(lane < plan.ahead, parcel_counts, 0.0), axis=1, keepdims=True)
        over = (total > sum(plan.out[:2])) | (
            total - jnp.minimum(front, plan.back[0]) > plan.back[1]
        )
        flags = jnp.maximum(flags, jnp.max(jnp.where(over, 1.0, 0.0), axis=0, keepdims=True))
        metas.append(contract(mine, parcel_counts.astype(BF16), ((1,), (0,))))
    meta_lane = lax.broadcasted_iota(jnp.int32, (contexts, HD), 1)
    meta_ref[...] = jnp.zeros(meta_ref.shape, F32)
    for b in range(parts):
        marked = jnp.where(meta_lane == local_experts, flags, metas[b])
        for c in range(contexts):
            meta_ref[c, b:b + 1, :] = marked[c:c + 1]


def route(head, ids, contexts, local_experts, plan):
    parts = len(ids)
    tokens = ids[0].shape[1]
    owners = contexts * parts
    return pl.pallas_call(
        functools.partial(route_kernel, local_experts, plan, parts),
        name="route",
        in_specs=[SMEM] + [VMEM] * parts,
        out_specs=[VMEM] * 5,
        out_shape=[
            jax.ShapeDtypeStruct((tokens, HD), jnp.int32),
            jax.ShapeDtypeStruct((contexts, parts + -parts % 8, HD), F32),
        ]
        + [jax.ShapeDtypeStruct((parts, owners * rows, tokens), BF16) for rows in plan.out],
        compiler_params=params(),
    )(head, *ids)


def prefix_with_counts_kernel(piece_ref, meta_ref, out_ref):
    ranks, rows, _ = piece_ref.shape
    total = jnp.zeros(piece_ref.shape[1:], F32)
    for r in range(ranks):
        out_ref[r, :rows, :] = total.astype(BF16)
        out_ref[r, rows:, :] = meta_ref[r].astype(BF16)
        if r + 1 < ranks:
            total = total + piece_ref[r].astype(F32)


def prefix_with_counts(pieces, meta):
    ranks, rows, width = pieces.shape
    return pl.pallas_call(
        prefix_with_counts_kernel,
        name="prefix_with_counts",
        in_specs=[VMEM] * 2,
        out_specs=VMEM,
        out_shape=jax.ShapeDtypeStruct((ranks, rows + meta.shape[1], width), BF16),
        compiler_params=params(),
    )(pieces, meta)


def columns_kernel(parts, head_ref, whole_ref, *out_refs):
    step = whole_ref.shape[1] // parts
    for s in range(parts):
        start = pl.multiple_of((head_ref[0] + s) % parts * step, step)
        out_refs[s][...] = whole_ref[:, pl.ds(start, step)]


def columns_by_turn(head, whole, parts):
    tokens, width = whole.shape
    return pl.pallas_call(
        functools.partial(columns_kernel, parts),
        name="columns_by_turn",
        in_specs=[SMEM, VMEM],
        out_specs=[VMEM] * parts,
        out_shape=[jax.ShapeDtypeStruct((tokens, width // parts), BF16)] * parts,
        compiler_params=params(),
    )(head, whole)


def mix_pack_kernel(
    parts, local_experts, plan, head_ref, query_ref, state_ref, tail_ref, local_ref, route_col_ref, gain_ref, *refs
):
    residual_refs, spread_refs = refs[:parts], refs[parts:parts + 3]
    refs = refs[parts + 3:]
    meta_ref, flag_ref, parcel_refs, stream_refs = refs[0], refs[1], refs[2:5], refs[5:5 + parts]
    normed_ref = refs[-1]
    head = head_ref[0]
    share, rows, _ = state_ref.shape
    contexts, tail, _ = tail_ref.shape
    rows -= tail
    query = query_ref[...]
    column = route_col_ref[...]
    wide = jnp.concatenate(
        [query * jnp.where(column == m, 2.0, 1.0).astype(BF16) for m in range(M)], axis=1
    )
    state = jnp.concatenate([state_ref[i, :rows, :] for i in range(share)], axis=0)
    mixed = contract(wide, state, ((1,), (0,))) + local_ref[...]
    scale = lax.rsqrt(jnp.mean(mixed * mixed, axis=-1, keepdims=True) + EPS)
    normed_ref[...] = (mixed * scale * gain_ref[...]).astype(BF16)

    counts = tail_ref[...].astype(F32)
    owners = contexts * parts
    lane = lax.broadcasted_iota(jnp.int32, counts.shape, 2)
    over = jnp.max(jnp.where(lane == local_experts, counts, 0.0))
    flag = (over > 0.5).astype(jnp.int32)
    flag_ref[0] = flag

    @pl.when(pl.program_id(0) == 0)
    def _():
        source = lax.broadcasted_iota(jnp.int32, (owners, contexts * tail), 0)
        given = lax.broadcasted_iota(jnp.int32, (owners, contexts * tail), 1)
        turn = (head - source % parts + parts) % parts
        order = jnp.where(given == source // parts * tail + turn, 1.0, 0.0).astype(BF16)
        flat = counts.reshape(contexts * tail, counts.shape[2]).astype(BF16)
        meta_ref[...] = contract(order, flat, ((1,), (0,))).astype(jnp.int32)

    tokens = residual_refs[0].shape[0]
    for s in range(parts):
        start = pl.multiple_of((head - s + parts) % parts * tokens, tokens)
        normed = normed_ref[pl.ds(start, tokens), :]
        stream = (residual_refs[s][...].astype(F32) + normed.astype(F32)).astype(BF16)
        stream_refs[s][...] = stream

    def fill(k):
        each = plan.out[k]
        for s in range(parts):
            packed = contract(spread_refs[k][s], stream_refs[s][...], ((1,), (0,))).astype(BF16)
            parcel_refs[k][:, s * each:(s + 1) * each, :] = packed.reshape(owners, each, HD)

    fill(0)
    fill(1)

    @pl.when(flag > 0)
    def _():
        fill(2)


def mix_and_pack(head, queries, carried, tail, local, route_col, head_gain, residuals, spreads, local_experts, plan):
    length, width = queries.shape
    heads = width // HD
    contexts, rows, _ = carried.shape
    share = contexts // heads
    parts = len(residuals)
    tokens = length // parts
    owners = contexts * parts
    wide = pl.BlockSpec((length, HD), lambda h: (0, h))
    narrow = pl.BlockSpec((tokens, HD), lambda h: (0, h))

    def whole(x):
        return pl.BlockSpec(x.shape, lambda h: (0,) * len(x.shape))

    parcels = [jax.ShapeDtypeStruct((owners, parts * r, width), BF16) for r in plan.out]
    meta = jax.ShapeDtypeStruct((owners, HD), jnp.int32)
    out = pl.pallas_call(
        functools.partial(mix_pack_kernel, parts, local_experts, plan),
        name="mix_and_pack",
        grid=(heads,),
        in_specs=[
            SMEM,
            wide,
            pl.BlockSpec((share, rows, HD), lambda h: (h, 0, 0)),
            pl.BlockSpec((contexts, tail, HD), lambda h: (0, (rows - tail) // tail, 0)),
            wide,
            pl.BlockSpec((length, 1), lambda h: (0, 0)),
            pl.BlockSpec((1, HD), lambda h: (0, h)),
        ]
        + [narrow] * parts
        + [whole(x) for x in spreads],
        out_specs=[whole(meta), SMEM]
        + [pl.BlockSpec((owners, x.shape[1], HD), lambda h: (0, 0, h)) for x in parcels]
        + [narrow] * parts,
        out_shape=[meta, jax.ShapeDtypeStruct((1,), jnp.int32)]
        + parcels
        + [jax.ShapeDtypeStruct((tokens, width), BF16)] * parts,
        scratch_shapes=[pltpu.VMEM((length, HD), BF16)],
        compiler_params=params(),
    )(head, queries, carried, carried, local, route_col, head_gain, *residuals, *spreads)
    return out[0], out[1], out[2:5], out[5:]


def gated(gates, spreads, back):
    total = 0.0
    for j, spread in enumerate(spreads):
        total = total + gates[:, j:j + 1] * contract(spread, back, ((1,), (0,)))
    return total


def choices(code, plan, k, owners):
    return [
        one_hot(in_round(code[:, 4 + j:5 + j], plan.back, k, code[:, j:j + 1]), owners * plan.back[k])
        for j in range(2)
    ]


def combine_ahead_kernel(plan, parts, head_ref, code_ref, gates_ref, back_ref, *refs):
    stream_refs, (acc_ref, pick_ref) = refs[:parts], refs[parts:]
    code = code_ref[...]
    owners, rows, width = back_ref.shape
    flat = back_ref[...].reshape(owners * rows, width)
    acc_ref[...] = gated(gates_ref[...], choices(code, plan, 0, owners), flat)
    step = width // parts
    for s in range(parts):
        start = pl.multiple_of((head_ref[0] + s) % parts * step, step)
        acc_ref[:, pl.ds(start, step)] = acc_ref[:, pl.ds(start, step)] + stream_refs[s][...].astype(F32)
    for j, spread in enumerate(choices(code, plan, 1, owners)):
        pick_ref[j] = spread


def combine_ahead(head, code, gates, back, streams, plan):
    owners, _, width = back.shape
    tokens = code.shape[0]
    return pl.pallas_call(
        functools.partial(combine_ahead_kernel, plan, len(streams)),
        name="combine_ahead",
        in_specs=[SMEM] + [VMEM] * (3 + len(streams)),
        out_specs=[VMEM] * 2,
        out_shape=[
            jax.ShapeDtypeStruct((tokens, width), F32),
            jax.ShapeDtypeStruct((2, tokens, owners * plan.back[1]), BF16),
        ],
        compiler_params=params(),
    )(head, code, gates, back, *streams)


def combine_kernel(plan, flag_ref, code_ref, gates_ref, acc_ref, pick_ref, back_ref, late_ref, out_ref):
    code = code_ref[...]
    gates = gates_ref[...]
    owners, rows, step = back_ref.shape
    flat = back_ref[...].reshape(owners * rows, step)
    total = acc_ref[...] + gated(gates, [pick_ref[0], pick_ref[1]], flat)
    out_ref[...] = total.astype(BF16)

    @pl.when(flag_ref[0] > 0)
    def _():
        late = late_ref[...].reshape(owners * plan.back[2], step)
        more = gated(gates, choices(code, plan, 2, owners), late)
        out_ref[...] = (total + more).astype(BF16)


def combine(flag, code, gates, acc, picks, back, late, plan):
    tokens, width = acc.shape
    owners = back.shape[0]
    step = min(512, width)

    def whole(x):
        return pl.BlockSpec(x.shape, lambda d: (0,) * len(x.shape))

    narrow = pl.BlockSpec((tokens, step), lambda d: (0, d))
    return pl.pallas_call(
        functools.partial(combine_kernel, plan),
        name="combine",
        grid=(width // step,),
        in_specs=[
            SMEM,
            whole(code),
            whole(gates),
            narrow,
            whole(picks),
            pl.BlockSpec((owners, plan.back[1], step), lambda d: (0, 0, d)),
            pl.BlockSpec((owners, plan.back[2], step), lambda d: (0, 0, d)),
        ],
        out_specs=narrow,
        out_shape=jax.ShapeDtypeStruct((tokens, width), BF16),
        compiler_params=params(),
    )(flag, code, gates, acc, picks, back, late)


def batch_columns(meta, expert, local_experts, plan):
    owners = meta.shape[0]
    counts = jnp.where(
        lax.broadcasted_iota(jnp.int32, meta.shape, 1) < local_experts, meta, 0
    ).astype(F32)
    lanes = counts.shape[1]
    row = lax.broadcasted_iota(jnp.int32, (lanes, lanes), 0)
    col = lax.broadcasted_iota(jnp.int32, (lanes, lanes), 1)
    below = jnp.where(row < col, 1.0, 0.0).astype(BF16)
    offsets = contract(counts.astype(BF16), below, ((1,), (0,)))
    batch = owners * CAP
    source_row = lax.broadcasted_iota(jnp.int32, (batch, owners), 0) // CAP
    source_col = lax.broadcasted_iota(jnp.int32, (batch, owners), 1)
    expand = jnp.where(source_row == source_col, 1.0, 0.0).astype(BF16)
    lane = lax.broadcasted_iota(jnp.int32, (batch, lanes), 1)

    def column(values, picked):
        wide = contract(expand, values.astype(BF16), ((1,), (0,)))
        return jnp.sum(jnp.where(picked, wide, 0.0), axis=1, keepdims=True).astype(jnp.int32)

    count = column(counts, lane == expert)
    offset = column(offsets, lane == expert)
    front = column(counts, lane < plan.ahead)
    index = lax.broadcasted_iota(jnp.int32, (batch, 1), 0)
    rank = index % CAP
    valid = rank < count
    place = offset + rank
    back = jnp.where(
        (expert < plan.ahead) & (place < plan.back[0]),
        place,
        plan.back[0] + place - jnp.minimum(front, plan.back[0]),
    )
    return index // CAP, jnp.where(valid, place, -1), jnp.where(valid, back, -1)


def expert_kernel(
    first, taken, given, has_base, local_experts, parts, plan, flag_ref, meta_ref, gain_ref, *refs
):
    x_refs, refs = refs[:len(taken)], refs[len(taken):]
    gate_ref, up_ref, down_ref = refs[:3]
    base_ref = refs[3] if has_base else None
    refs = refs[3 + has_base:]
    out_refs, (batch_ref, acc_ref, done_ref) = refs[:len(given)], refs[len(given):]
    e = pl.program_id(0)
    f = pl.program_id(1)
    last_f = pl.num_programs(1) - 1
    batch = batch_ref.shape[0]
    meta = meta_ref[...]

    @pl.when(f == 0)
    def _():
        source, place, _ = batch_columns(meta, first + e, local_experts, plan)

        context = source // parts
        block = source % parts

        def rows_of(i, k):
            owners, rows, step = x_refs[i].shape
            pieces = x_refs[i][...].reshape(owners // parts, parts, rows, step)
            found = []
            for h in range(parts):
                turn = (h - block + parts) % parts
                spread = one_hot(
                    in_round(place, plan.out, k, context * parts + turn), owners * plan.out[k]
                )
                flat = pieces[:, h].reshape(owners // parts * rows, step)
                found.append(contract(spread, flat, ((1,), (0,))))
            return jnp.concatenate(found, axis=1)

        total = 0.0
        for i, k in enumerate(taken):
            if k < 2:
                total = total + rows_of(i, k)
        acc_ref[...] = total
        for i, k in enumerate(taken):
            if k == 2:

                @pl.when(flag_ref[0] > 0)
                def _():
                    acc_ref[...] = acc_ref[...] + rows_of(i, k)

        stream = acc_ref[...]
        scale = lax.rsqrt(jnp.mean(stream * stream, axis=-1, keepdims=True) + EPS)
        batch_ref[...] = (stream * scale * gain_ref[...]).astype(BF16)

    x = batch_ref[...]
    gate = contract(x, gate_ref[...], ((1,), (0,)))
    upward = contract(x, up_ref[...], ((1,), (0,)))
    hidden = (gate / (1.0 + jnp.exp(-gate)) * upward).astype(BF16)
    part = contract(hidden, down_ref[...], ((1,), (0,)))

    @pl.when(f == 0)
    def _():
        acc_ref[...] = part

    @pl.when((f > 0) & (f < last_f))
    def _():
        acc_ref[...] = acc_ref[...] + part

    @pl.when(f == last_f)
    def _():
        done_ref[e] = (acc_ref[...] + part).astype(BF16)

    @pl.when((e == pl.num_programs(0) - 1) & (f == last_f))
    def _():
        count = done_ref.shape[0]
        columns = [batch_columns(meta, first + i, local_experts, plan) for i in range(count)]
        source = jnp.concatenate([c[0] for c in columns], axis=0)
        back = jnp.concatenate([c[2] for c in columns], axis=0)
        done = done_ref[...].reshape(count * batch, done_ref.shape[2])

        def put(i, k):
            owners, rows, width = out_refs[i].shape
            spread = one_hot(in_round(back, plan.back, k, source), owners * rows)
            rows_out = contract(spread, done, ((0,), (0,)))
            if has_base and k == 1:
                rows_out = rows_out + base_ref[...].reshape(owners * rows, width).astype(F32)
            out_refs[i][...] = rows_out.astype(BF16).reshape(owners, rows, width)

        for i, k in enumerate(given):
            if k < 2:
                put(i, k)
            else:

                @pl.when(flag_ref[0] > 0)
                def _():
                    put(i, k)


def serve_experts(flag, meta, gain, parts, received, weights, base, first, taken, given, plan):
    w_gate, w_up, w_down = weights
    local_experts, width, hidden = w_gate.shape
    owners = meta.shape[0]
    count = plan.ahead
    split = 2
    step = hidden // split

    def whole(x):
        return pl.BlockSpec(x.shape, lambda e, f: (0,) * len(x.shape))

    in_spec = pl.BlockSpec((None, width, step), lambda e, f: (first + e, 0, f))
    extra = [] if base is None else [base]
    outs = [jax.ShapeDtypeStruct((owners, plan.back[k], width), BF16) for k in given]
    batch = owners * CAP
    return pl.pallas_call(
        functools.partial(
            expert_kernel, first, taken, given, base is not None, local_experts, parts, plan
        ),
        grid=(count, split),
        in_specs=[SMEM, whole(meta), whole(gain)]
        + [whole(x) for x in received]
        + [
            in_spec,
            in_spec,
            pl.BlockSpec((None, step, width), lambda e, f: (first + e, f, 0)),
        ]
        + [whole(x) for x in extra],
        out_specs=[whole(x) for x in outs],
        out_shape=outs,
        scratch_shapes=[
            pltpu.VMEM((batch, width), BF16),
            pltpu.VMEM((batch, width), F32),
            pltpu.VMEM((count, batch, width), BF16),
        ],
        compiler_params=params(),
    )(flag, meta, gain, *received, w_gate, w_up, w_down, *extra)


def everywhere(x):
    return lax.all_to_all(x, ("ctx", "head"), split_axis=0, concat_axis=0, tiled=True)


def everywhere_if(flag, x):
    return lax.cond(flag[0] > 0, everywhere, lambda y: y, x)


def body_dense(
    queries,
    keys,
    values,
    mem_route,
    head_gain,
    residual_in,
    ffn_gain,
    expert_ids,
    expert_gates,
    w_gate,
    w_up,
    w_down,
):
    length = queries.shape[0]
    ctx_count = lax.axis_size("ctx")
    head_count = lax.axis_size("head")
    owners = ctx_count * head_count
    local_experts = w_gate.shape[0]
    pairs = local_experts // PAIR
    chunks = 2 if pairs % 2 == 0 else 1
    route_row = mem_route.reshape(1, length)
    route_col = mem_route.reshape(length, 1)

    states = block_states(keys, values, route_row)
    pieces = lax.all_to_all(states, "ctx", split_axis=0, concat_axis=0, tiled=True)
    before = exclusive_prefix(pieces.reshape(ctx_count, -1, HD))
    carried = lax.all_to_all(
        before.reshape(states.shape), "ctx", split_axis=0, concat_axis=0, tiled=True
    )
    local = local_attention(queries, keys, values, route_row, route_col)
    normed = mix_and_norm(queries, carried, local, route_col, head_gain[None], head_count)
    by_token = lax.all_to_all(normed, "head", split_axis=0, concat_axis=0, tiled=True)

    stream, parcels = pack_dense(
        residual_in, by_token, ffn_gain[None], expert_ids, chunks, owners, local_experts
    )
    backs = []
    for c in range(chunks):
        received = lax.all_to_all(
            parcels[c], ("ctx", "head"), split_axis=0, concat_axis=0, tiled=True
        )
        served = serve_dense(received, w_gate, w_up, w_down, c)
        backs.append(
            lax.all_to_all(served, ("ctx", "head"), split_axis=0, concat_axis=0, tiled=True)
        )
    return combine_dense(stream, expert_ids, expert_gates, backs, local_experts)


def body_compact(
    queries,
    keys,
    values,
    mem_route,
    head_gain,
    residual_in,
    ffn_gain,
    expert_ids,
    expert_gates,
    w_gate,
    w_up,
    w_down,
):
    length = queries.shape[0]
    contexts = lax.axis_size("ctx")
    parts = lax.axis_size("head")
    local_experts = w_gate.shape[0]
    plan = Plan(local_experts)
    route_row = mem_route.reshape(1, length)
    route_col = mem_route.reshape(length, 1)
    head = lax.axis_index("head").astype(jnp.int32)[None]

    def turned(pieces, step):
        return [pieces[0]] + [
            lax.ppermute(pieces[s], "head", [(h, (h + step * s) % parts) for h in range(parts)])
            for s in range(1, parts)
        ]

    ids = turned([expert_ids.T] * parts, 1)
    states = block_states(keys, values, route_row)
    pieces = lax.all_to_all(states, "ctx", split_axis=0, concat_axis=0, tiled=True)
    code, counts, *spreads = route(head, ids, contexts, local_experts, plan)
    before = prefix_with_counts(pieces.reshape(contexts, -1, HD), counts)
    carried = lax.all_to_all(before, "ctx", split_axis=0, concat_axis=0, tiled=True)
    cut = columns_by_turn(head, residual_in, parts)
    residuals = turned(cut, 1)
    local = local_attention(queries, keys, values, route_row, route_col)
    meta, flag, parcels, streams = mix_and_pack(
        head,
        queries,
        carried,
        counts.shape[1],
        local,
        route_col,
        head_gain[None],
        residuals,
        spreads,
        local_experts,
        plan,
    )
    weights = (w_gate, w_up, w_down)
    gain = ffn_gain[None]
    received = [everywhere(parcels[0])]
    received.append(everywhere(parcels[1]))
    streams = turned(streams, -1)
    back_0, base = serve_experts(
        flag, meta, gain, parts, received[:1], weights, None, 0, (0,), (0, 1), plan
    )
    received.append(everywhere_if(flag, parcels[2]))
    back_0 = everywhere(back_0)
    back_1, back_2 = serve_experts(
        flag, meta, gain, parts, received, weights, base, plan.ahead, (0, 1, 2), (1, 2), plan
    )
    back_2 = everywhere_if(flag, back_2)
    back_1 = everywhere(back_1)
    acc, picks = combine_ahead(head, code, expert_gates, back_0, streams, plan)
    return combine(flag, code, expert_gates, acc, picks, back_1, back_2, plan)


def body(*args):
    local_experts = args[-1].shape[0]
    compact = local_experts * CAP % (4 * GROUP_ROWS) == 0
    return body_compact(*args) if compact else body_dense(*args)


def solution(mesh):
    placed = (
        P("ctx", "head"),
        P("ctx", "head"),
        P("ctx", "head"),
        P("ctx"),
        P("head"),
        P(("ctx", "head"), None),
        P(),
        P(("ctx", "head"), None),
        P(("ctx", "head"), None),
        P(("ctx", "head"), None, None),
        P(("ctx", "head"), None, None),
        P(("ctx", "head"), None, None),
    )
    return jax.shard_map(
        body, mesh=mesh, in_specs=placed, out_specs=P(("ctx", "head"), None), check_vma=False
    )
```

```python
import functools

import jax
import jax.numpy as jnp
from jax import lax
from jax.experimental import pallas as pl
from jax.experimental.pallas import tpu as pltpu
from jax.sharding import PartitionSpec as P


HD = 128
M = 4
CAP = 4
PAIR = 2
GROUP_ROWS = PAIR * CAP
EPS = 1e-06
F32 = jnp.float32
BF16 = jnp.bfloat16


def params(mebibytes=60):
    return pltpu.CompilerParams(vmem_limit_bytes=mebibytes * 1024 * 1024)


def in_hbm(x):
    return pltpu.with_memory_space_constraint(x, pltpu.HBM)


def in_vmem(x):
    return pltpu.with_memory_space_constraint(x, pltpu.VMEM)


def contract(a, b, dims):
    return lax.dot_general(a, b, (dims, ((), ())), preferred_element_type=F32)


def state_kernel(key_ref, value_ref, route_ref, out_ref):
    keys_t = key_ref[...].T
    values = value_ref[...]
    route = route_ref[...]
    for m in range(M):
        mask = (route == m).astype(F32).astype(BF16)
        out_ref[pl.ds(m * HD, HD), :] = contract(keys_t * mask, values, ((1,), (0,))).astype(BF16)


def block_states(keys, values, route_row):
    length, width = keys.shape
    heads = width // HD
    return pl.pallas_call(
        state_kernel,
        name="block_states",
        grid=(heads,),
        in_specs=[
            pl.BlockSpec((length, HD), lambda h: (0, h)),
            pl.BlockSpec((length, HD), lambda h: (0, h)),
            pl.BlockSpec((1, length), lambda h: (0, 0)),
        ],
        out_specs=pl.BlockSpec((M * HD, HD), lambda h: (h, 0)),
        out_shape=pltpu.HBM((heads * M * HD, HD), BF16),
        compiler_params=params(16),
    )(in_hbm(keys), in_hbm(values), in_hbm(route_row))


def prefix_kernel(ranks, piece_ref, out_ref):
    total = jnp.zeros(piece_ref.shape[1:], F32)
    for r in range(ranks):
        out_ref[r] = total.astype(BF16)
        if r + 1 < ranks:
            total = total + piece_ref[r].astype(F32)


def exclusive_prefix(pieces):
    return pl.pallas_call(
        functools.partial(prefix_kernel, pieces.shape[0]),
        name="exclusive_prefix",
        out_shape=jax.ShapeDtypeStruct(pieces.shape, BF16),
        compiler_params=params(),
    )(pieces)


def local_kernel(rows, query_ref, key_ref, value_ref, route_row_ref, route_col_ref, out_ref, weight_ref):
    length = query_ref.shape[0]

    @pl.when(pl.program_id(0) == 0)
    def _():
        route_row = route_row_ref[...]
        for i in range(length // rows):
            span = (i + 1) * rows
            column = route_col_ref[pl.ds(i * rows, rows), :]
            same = jnp.where(column == route_row[:, :span], 2.0, 1.0)
            t = lax.broadcasted_iota(jnp.int32, (rows, span), 0) + i * rows
            s = lax.broadcasted_iota(jnp.int32, (rows, span), 1)
            weight_ref[pl.ds(i * rows, rows), :span] = jnp.where(t >= s, same, 0.0)

    for i in range(length // rows):
        span = (i + 1) * rows
        query = query_ref[pl.ds(i * rows, rows), :]
        scores = contract(query, key_ref[:span, :], ((1,), (1,)))
        weighted = (scores * weight_ref[pl.ds(i * rows, rows), :span]).astype(BF16)
        out_ref[pl.ds(i * rows, rows), :] = contract(weighted, value_ref[:span, :], ((1,), (0,)))


def local_attention(queries, keys, values, route_row, route_col):
    length, width = queries.shape
    heads = width // HD
    rows = min(256, length)
    wide = pl.BlockSpec((length, HD), lambda h: (0, h))
    return pl.pallas_call(
        functools.partial(local_kernel, rows),
        name="local_attention",
        grid=(heads,),
        in_specs=[
            wide,
            wide,
            wide,
            pl.BlockSpec((1, length), lambda h: (0, 0)),
            pl.BlockSpec((length, 1), lambda h: (0, 0)),
        ],
        out_specs=wide,
        out_shape=jax.ShapeDtypeStruct((length, width), F32),
        scratch_shapes=[pltpu.VMEM((length, length), F32)],
        compiler_params=params(32),
    )(in_hbm(queries), in_hbm(keys), in_hbm(values), route_row, route_col)


def mix_kernel(query_ref, state_ref, local_ref, route_col_ref, gain_ref, out_ref):
    parts, rows, _ = out_ref.shape
    query = query_ref[...]
    column = route_col_ref[...]
    wide = jnp.concatenate(
        [query * jnp.where(column == m, 2.0, 1.0).astype(BF16) for m in range(M)], axis=1
    )
    mixed = contract(wide, state_ref[...], ((1,), (0,))) + local_ref[...]
    scale = lax.rsqrt(jnp.mean(mixed * mixed, axis=-1, keepdims=True) + EPS)
    normed = (mixed * scale * gain_ref[...]).astype(BF16)
    for p in range(parts):
        out_ref[p] = normed[p * rows:(p + 1) * rows]


def mix_and_norm(queries, state, local, route_col, head_gain, parts):
    length, width = queries.shape
    heads = width // HD
    wide = pl.BlockSpec((length, HD), lambda h: (0, h))
    return pl.pallas_call(
        mix_kernel,
        name="mix_and_norm",
        grid=(heads,),
        in_specs=[
            wide,
            pl.BlockSpec((M * HD, HD), lambda h: (h, 0)),
            wide,
            pl.BlockSpec((length, 1), lambda h: (0, 0)),
            pl.BlockSpec((1, HD), lambda h: (0, h)),
        ],
        out_specs=pl.BlockSpec((parts, length // parts, HD), lambda h: (0, 0, h)),
        out_shape=jax.ShapeDtypeStruct((parts, length // parts, width), BF16),
        compiler_params=params(),
    )(queries, state, local, route_col, head_gain)


def slot_columns(ids, experts, local_experts):
    tokens = ids.shape[0]
    owners = experts // local_experts
    lanes = lax.broadcasted_iota(jnp.int32, (tokens, experts), 1)
    chosen = [(ids[:, j:j + 1] == lanes).astype(F32) for j in range(2)]
    t = lax.broadcasted_iota(jnp.int32, (tokens, tokens), 0)
    s = lax.broadcasted_iota(jnp.int32, (tokens, tokens), 1)
    earlier = contract(
        (t > s).astype(F32).astype(BF16), (chosen[0] + chosen[1]).astype(BF16), ((1,), (0,))
    )
    slots = []
    for j in range(2):
        rank = jnp.sum(earlier * chosen[j], axis=1, keepdims=True).astype(jnp.int32)
        expert = ids[:, j:j + 1]
        owner = expert // local_experts
        local = expert % local_experts
        slots.append(
            ((local // PAIR) * owners + owner) * GROUP_ROWS + (local % PAIR) * CAP + rank
        )
    return slots


def pack_dense_kernel(chunks, local_experts, residual_ref, piece_ref, gain_ref, ids_ref, *refs):
    stream_ref, out_refs = refs[0], refs[1:1 + chunks]
    parts, rows, _ = piece_ref.shape
    owners, groups, _, width = out_refs[0].shape
    normed = jnp.concatenate([piece_ref[p] for p in range(parts)], axis=1)
    stream = (residual_ref[...].astype(F32) + normed.astype(F32)).astype(BF16)
    stream_ref[...] = stream
    wide = stream.astype(F32)
    scale = lax.rsqrt(jnp.mean(wide * wide, axis=-1, keepdims=True) + EPS)
    ffn_in = (wide * scale * gain_ref[...]).astype(BF16)
    experts = owners * local_experts
    slot0, slot1 = slot_columns(ids_ref[...], experts, local_experts)
    span = owners * GROUP_ROWS
    for c in range(chunks):
        for g in range(groups):
            base = (c * groups + g) * span
            lanes = lax.broadcasted_iota(jnp.int32, (rows, span), 1) + base
            spread = jnp.where((slot0 == lanes) | (slot1 == lanes), 1.0, 0.0).astype(BF16)
            packed = contract(spread, ffn_in, ((0,), (0,))).astype(BF16)
            out_refs[c][:, g] = packed.reshape(owners, GROUP_ROWS, width)


def pack_dense(residual, pieces, gain, ids, chunks, owners, local_experts):
    tokens, width = residual.shape
    groups = local_experts // PAIR // chunks
    parcel = jax.ShapeDtypeStruct((owners, groups, GROUP_ROWS, width), BF16)
    out = pl.pallas_call(
        functools.partial(pack_dense_kernel, chunks, local_experts),
        name="pack_dense",
        out_shape=[jax.ShapeDtypeStruct((tokens, width), BF16)] + [parcel] * chunks,
        compiler_params=params(),
    )(residual, pieces, gain, ids)
    return out[0], out[1:]


def expert_dense_kernel(x_ref, gate_ref, up_ref, down_ref, out_ref, acc_ref):
    e = pl.program_id(1)
    f = pl.program_id(2)
    owners, rows, width = x_ref.shape
    x = x_ref[...].reshape(owners * rows, width)
    gate = contract(x, gate_ref[...], ((1,), (0,)))
    upward = contract(x, up_ref[...], ((1,), (0,)))
    row = lax.broadcasted_iota(jnp.int32, gate.shape, 0)
    mine = (row // CAP) % PAIR == e
    hidden = gate / (1.0 + jnp.exp(-gate)) * upward
    hidden = jnp.where(mine, hidden, 0.0).astype(BF16)
    part = contract(hidden, down_ref[...], ((1,), (0,)))
    first = (e == 0) & (f == 0)

    @pl.when(first)
    def _():
        acc_ref[...] = part

    @pl.when(jnp.logical_not(first))
    def _():
        acc_ref[...] = acc_ref[...] + part

    @pl.when((e == pl.num_programs(1) - 1) & (f == pl.num_programs(2) - 1))
    def _():
        out_ref[...] = acc_ref[...].astype(BF16).reshape(owners, rows, width)


def serve_dense(received, w_gate, w_up, w_down, chunk):
    owners, groups, rows, width = received.shape
    hidden = w_gate.shape[2]
    split = 2
    step = hidden // split
    first = chunk * groups * PAIR
    token_spec = pl.BlockSpec((owners, None, rows, width), lambda g, e, f: (0, g, 0, 0))
    in_spec = pl.BlockSpec((None, width, step), lambda g, e, f: (first + g * PAIR + e, 0, f))
    return pl.pallas_call(
        expert_dense_kernel,
        grid=(groups, PAIR, split),
        in_specs=[
            token_spec,
            in_spec,
            in_spec,
            pl.BlockSpec((None, step, width), lambda g, e, f: (first + g * PAIR + e, f, 0)),
        ],
        out_specs=token_spec,
        out_shape=jax.ShapeDtypeStruct(received.shape, BF16),
        scratch_shapes=[pltpu.VMEM((owners * rows, width), F32)],
        compiler_params=params(),
    )(received, w_gate, w_up, w_down)


def combine_dense_kernel(chunks, local_experts, stream_ref, ids_ref, gates_ref, *refs):
    back_refs, out_ref, first_ref, second_ref = refs[:chunks], refs[chunks], refs[-2], refs[-1]
    owners, groups, rows, _ = back_refs[0].shape
    span = owners * rows

    @pl.when(pl.program_id(0) == 0)
    def _():
        slot0, slot1 = slot_columns(ids_ref[...], owners * local_experts, local_experts)
        lanes = lax.broadcasted_iota(jnp.int32, first_ref.shape, 1)
        first_ref[...] = jnp.where(slot0 == lanes, 1.0, 0.0).astype(BF16)
        second_ref[...] = jnp.where(slot1 == lanes, 1.0, 0.0).astype(BF16)

    back = jnp.concatenate(
        [
            back_refs[c][:, g].reshape(span, back_refs[c].shape[3])
            for c in range(chunks)
            for g in range(groups)
        ],
        axis=0,
    )
    gates = gates_ref[...]
    total = stream_ref[...].astype(F32)
    total = total + gates[:, 0:1] * contract(first_ref[...], back, ((1,), (0,)))
    total = total + gates[:, 1:2] * contract(second_ref[...], back, ((1,), (0,)))
    out_ref[...] = total.astype(BF16)


def combine_dense(stream, ids, gates, backs, local_experts):
    tokens, width = stream.shape
    owners, groups, rows, _ = backs[0].shape
    chunks = len(backs)
    slots = owners * groups * rows * chunks
    step = min(512, width)
    back_spec = pl.BlockSpec((owners, groups, rows, step), lambda d: (0, 0, 0, d))
    return pl.pallas_call(
        functools.partial(combine_dense_kernel, chunks, local_experts),
        name="combine_dense",
        grid=(width // step,),
        in_specs=[
            pl.BlockSpec((tokens, step), lambda d: (0, d)),
            pl.BlockSpec(ids.shape, lambda d: (0, 0)),
            pl.BlockSpec(gates.shape, lambda d: (0, 0)),
        ]
        + [back_spec] * chunks,
        out_specs=pl.BlockSpec((tokens, step), lambda d: (0, d)),
        out_shape=jax.ShapeDtypeStruct((tokens, width), BF16),
        scratch_shapes=[pltpu.VMEM((tokens, slots), BF16)] * 2,
        compiler_params=params(),
    )(stream, ids, gates, *backs)


class Plan:
    def __init__(self, local_experts):
        dense = local_experts * CAP
        self.ahead = local_experts // 2
        first = self.ahead * CAP
        self.out = (first, first // 2, dense - first - first // 2)
        self.back = (first // 2, first, dense - first - first // 2)


def in_round(place, bounds, k, owner):
    low = sum(bounds[:k])
    inside = (place >= low) & (place < low + bounds[k])
    return jnp.where(inside, owner * bounds[k] + place - low, -1)


def one_hot(column, width):
    lanes = lax.broadcasted_iota(jnp.int32, (column.shape[0], width), 1)
    return jnp.where(column == lanes, 1.0, 0.0).astype(BF16)


VMEM = pl.BlockSpec(memory_space=pltpu.VMEM)
SMEM = pl.BlockSpec(memory_space=pltpu.SMEM)


def route_kernel(local_experts, plan, parts, head_ref, *refs):
    id_refs, (code_ref, meta_ref), spread_refs = refs[:parts], refs[parts:parts + 2], refs[parts + 2:]
    tokens = id_refs[0].shape[1]
    contexts = meta_ref.shape[0]
    owners = contexts * parts
    experts = owners * local_experts
    head = head_ref[0]
    t = lax.broadcasted_iota(jnp.int32, (tokens, tokens), 0)
    s = lax.broadcasted_iota(jnp.int32, (tokens, tokens), 1)
    earlier_mask = (t > s).astype(F32).astype(BF16)
    row = lax.broadcasted_iota(jnp.int32, (experts, experts), 0)
    col = lax.broadcasted_iota(jnp.int32, (experts, experts), 1)
    mates = row // local_experts == col // local_experts
    below = jnp.where(mates & (row < col), 1.0, 0.0).astype(BF16)
    ahead = jnp.where(mates & (row % local_experts < plan.ahead), 1.0, 0.0).astype(BF16)
    lanes = lax.broadcasted_iota(jnp.int32, (tokens, experts), 1)
    owner_lane = lax.broadcasted_iota(jnp.int32, (tokens, owners), 1)
    local_lane = lax.broadcasted_iota(jnp.int32, (tokens, HD), 1)
    owner_row = lax.broadcasted_iota(jnp.int32, (contexts, owners), 1)
    context_row = lax.broadcasted_iota(jnp.int32, (contexts, owners), 0)
    mine = jnp.where(owner_row == context_row * parts + head, 1.0, 0.0).astype(BF16)
    lane = lax.broadcasted_iota(jnp.int32, (owners, HD), 1)
    pair_rows = [ref[...].astype(F32) for ref in id_refs]
    id_rows = jnp.concatenate(pair_rows + [jnp.zeros((-2 * parts % 8, tokens), F32)] * (2 * parts % 8 > 0), axis=0)
    id_cols = id_rows.T
    flags = 0.0
    metas = []
    for b in range(parts):
        ids = [id_cols[:, 2 * b + j:2 * b + j + 1].astype(jnp.int32) for j in range(2)]
        chosen = [(i == lanes).astype(F32) for i in ids]
        both = (chosen[0] + chosen[1]).astype(BF16)
        counts = contract(jnp.ones((8, tokens), BF16), both, ((1,), (0,))).astype(BF16)
        position = contract(earlier_mask, both, ((1,), (0,))) + contract(counts, below, ((1,), (0,)))[0:1]
        places = [jnp.sum(position * c, axis=1, keepdims=True) for c in chosen]
        wide = jnp.concatenate(places + [jnp.zeros((tokens, HD - 2), F32)], axis=1)
        place_rows = wide.T[0:8]
        parcel_counts = 0.0
        for j in range(2):
            parcel_counts = parcel_counts + contract(
                (ids[j] // local_experts == owner_lane).astype(F32).astype(BF16),
                (ids[j] % local_experts == local_lane).astype(F32).astype(BF16),
                ((0,), (0,)),
            )
        if b == 0:
            aheads = contract(counts, ahead, ((1,), (0,)))[0:1]
            slot_lane = lax.broadcasted_iota(jnp.int32, code_ref.shape, 1)
            code = jnp.zeros(code_ref.shape, jnp.int32)
            for j in range(2):
                place = places[j].astype(jnp.int32)
                front = jnp.sum(aheads * chosen[j], axis=1, keepdims=True).astype(jnp.int32)
                back = jnp.where(
                    (ids[j] % local_experts < plan.ahead) & (place < plan.back[0]),
                    place,
                    plan.back[0] + place - jnp.minimum(front, plan.back[0]),
                )
                code = jnp.where(slot_lane == j, ids[j] // local_experts, code)
                code = jnp.where(slot_lane == 4 + j, back, code)
            code_ref[...] = code
        for k, spread_ref in enumerate(spread_refs):
            slots = spread_ref.shape[1]
            slot = lax.broadcasted_iota(jnp.int32, (slots, tokens), 0)
            hit = None
            for j in range(2):
                owner = id_rows[2 * b + j:2 * b + j + 1].astype(jnp.int32) // local_experts
                index = in_round(place_rows[j:j + 1].astype(jnp.int32), plan.out, k, owner)
                hit = (slot == index) if hit is None else hit | (slot == index)
            spread_ref[b] = jnp.where(hit, 1.0, 0.0).astype(BF16)
        total = jnp.sum(parcel_counts, axis=1, keepdims=True)
        front = jnp.sum(jnp.where(lane < plan.ahead, parcel_counts, 0.0), axis=1, keepdims=True)
        over = (total > sum(plan.out[:2])) | (
            total - jnp.minimum(front, plan.back[0]) > plan.back[1]
        )
        flags = jnp.maximum(flags, jnp.max(jnp.where(over, 1.0, 0.0), axis=0, keepdims=True))
        metas.append(contract(mine, parcel_counts.astype(BF16), ((1,), (0,))))
    meta_lane = lax.broadcasted_iota(jnp.int32, (contexts, HD), 1)
    meta_ref[...] = jnp.zeros(meta_ref.shape, F32)
    for b in range(parts):
        marked = jnp.where(meta_lane == local_experts, flags, metas[b])
        for c in range(contexts):
            meta_ref[c, b:b + 1, :] = marked[c:c + 1]


def route(head, ids, contexts, local_experts, plan):
    parts = len(ids)
    tokens = ids[0].shape[1]
    owners = contexts * parts
    return pl.pallas_call(
        functools.partial(route_kernel, local_experts, plan, parts),
        name="route",
        in_specs=[SMEM] + [VMEM] * parts,
        out_specs=[VMEM] * 5,
        out_shape=[
            pltpu.HBM((tokens, HD), jnp.int32),
            jax.ShapeDtypeStruct((contexts, parts + -parts % 8, HD), F32),
        ]
        + [pltpu.HBM((parts, owners * rows, tokens), BF16) for rows in plan.out],
        compiler_params=params(24),
    )(head, *ids)


def prefix_with_counts_kernel(piece_ref, meta_ref, out_ref):
    ranks, rows, _ = piece_ref.shape
    total = jnp.zeros(piece_ref.shape[1:], F32)
    for r in range(ranks):
        out_ref[r, :rows, :] = total.astype(BF16)
        out_ref[r, rows:, :] = meta_ref[r].astype(BF16)
        if r + 1 < ranks:
            total = total + piece_ref[r].astype(F32)


def prefix_with_counts(pieces, meta):
    ranks, rows, width = pieces.shape
    return pl.pallas_call(
        prefix_with_counts_kernel,
        name="prefix_with_counts",
        in_specs=[VMEM] * 2,
        out_specs=VMEM,
        out_shape=pltpu.HBM((ranks, rows + meta.shape[1], width), BF16),
        compiler_params=params(12),
    )(pieces, meta)


def columns_kernel(parts, head_ref, whole_ref, *out_refs):
    step = whole_ref.shape[1] // parts
    for s in range(parts):
        start = pl.multiple_of((head_ref[0] + s) % parts * step, step)
        out_refs[s][...] = whole_ref[:, pl.ds(start, step)]


def columns_by_turn(head, whole, parts):
    tokens, width = whole.shape
    return pl.pallas_call(
        functools.partial(columns_kernel, parts),
        name="columns_by_turn",
        in_specs=[SMEM, VMEM],
        out_specs=[VMEM] * parts,
        out_shape=[pltpu.HBM((tokens, width // parts), BF16)] * parts,
        compiler_params=params(12),
    )(head, whole)


def mix_pack_kernel(
    parts, local_experts, plan, head_ref, query_ref, state_ref, tail_ref, local_ref, route_col_ref, gain_ref, *refs
):
    residual_refs, spread_ref = refs[:parts], refs[parts]
    refs = refs[parts + 1:]
    meta_ref, flag_ref, parcel_ref, stream_refs = refs[0], refs[1], refs[2], refs[3:3 + parts]
    normed_ref = refs[-1]
    head = head_ref[0]
    pieces, rows, _ = state_ref.shape
    contexts, tail, _ = tail_ref.shape
    rows -= tail
    width = query_ref.shape[1]
    together = width // HD
    share = pieces // together
    column = route_col_ref[...]
    doubled = [jnp.where(column == m, 2.0, 1.0).astype(BF16) for m in range(M)]
    for g in range(together):
        span = slice(g * HD, (g + 1) * HD)
        query = query_ref[:, span]
        wide = jnp.concatenate([query * weight for weight in doubled], axis=1)
        state = jnp.concatenate([state_ref[g * share + i, :rows, :] for i in range(share)], axis=0)
        mixed = contract(wide, state, ((1,), (0,))) + local_ref[:, span]
        scale = lax.rsqrt(jnp.mean(mixed * mixed, axis=-1, keepdims=True) + EPS)
        normed_ref[:, span] = (mixed * scale * gain_ref[:, span]).astype(BF16)

    @pl.when(pl.program_id(0) == 0)
    def _():
        counts = tail_ref[...].astype(F32)
        owners = contexts * parts
        lane = lax.broadcasted_iota(jnp.int32, counts.shape, 2)
        over = jnp.max(jnp.where(lane == local_experts, counts, 0.0))
        flag_ref[0] = (over > 0.5).astype(jnp.int32)
        source = lax.broadcasted_iota(jnp.int32, (owners, contexts * tail), 0)
        given = lax.broadcasted_iota(jnp.int32, (owners, contexts * tail), 1)
        turn = (head - source % parts + parts) % parts
        order = jnp.where(given == source // parts * tail + turn, 1.0, 0.0).astype(BF16)
        flat = counts.reshape(contexts * tail, counts.shape[2]).astype(BF16)
        meta_ref[...] = contract(order, flat, ((1,), (0,))).astype(jnp.int32)

    tokens = residual_refs[0].shape[0]
    for s in range(parts):
        start = pl.multiple_of((head - s + parts) % parts * tokens, tokens)
        normed = normed_ref[pl.ds(start, tokens), :]
        stream = (residual_refs[s][...].astype(F32) + normed.astype(F32)).astype(BF16)
        stream_refs[s][...] = stream
        put_parcels(plan.out[0], s, spread_ref[s], stream, parcel_ref)


def put_parcels(each, s, spread, stream, parcel_ref):
    owners, _, width = parcel_ref.shape
    packed = contract(spread, stream, ((1,), (0,))).astype(BF16)
    parcel_ref[:, s * each:(s + 1) * each, :] = packed.reshape(owners, each, width)


def mix_and_pack(head, queries, carried, tail, local, route_col, head_gain, residuals, spread, local_experts, plan):
    length, width = queries.shape
    heads = width // HD
    together = 2 if heads % 2 == 0 else 1
    step = together * HD
    contexts, rows, _ = carried.shape
    share = contexts * together // heads
    parts = len(residuals)
    tokens = length // parts
    owners = contexts * parts
    wide = pl.BlockSpec((length, step), lambda h: (0, h))
    narrow = pl.BlockSpec((tokens, step), lambda h: (0, h))

    def whole(x):
        return pl.BlockSpec(x.shape, lambda h: (0,) * len(x.shape))

    each = parts * plan.out[0]
    meta = pltpu.HBM((owners, HD), jnp.int32)
    out = pl.pallas_call(
        functools.partial(mix_pack_kernel, parts, local_experts, plan),
        name="mix_and_pack",
        grid=(heads // together,),
        in_specs=[
            SMEM,
            wide,
            pl.BlockSpec((share, rows, HD), lambda h: (h, 0, 0)),
            pl.BlockSpec((contexts, tail, HD), lambda h: (0, (rows - tail) // tail, 0)),
            wide,
            pl.BlockSpec((length, 1), lambda h: (0, 0)),
            pl.BlockSpec((1, step), lambda h: (0, h)),
        ]
        + [narrow] * parts
        + [whole(spread)],
        out_specs=[whole(meta), SMEM, pl.BlockSpec((owners, each, step), lambda h: (0, 0, h))]
        + [narrow] * parts,
        out_shape=[
            meta,
            jax.ShapeDtypeStruct((1,), jnp.int32),
            pltpu.HBM((owners, each, width), BF16),
        ]
        + [pltpu.HBM((tokens, width), BF16)] * parts,
        scratch_shapes=[pltpu.VMEM((length, step), BF16)],
        compiler_params=params(32),
    )(
        head,
        in_hbm(queries),
        carried,
        carried,
        local,
        route_col,
        head_gain,
        *map(in_hbm, residuals),
        in_hbm(spread),
    )
    return out[0], out[1], out[2], out[3:]


def pack_kernel(each, spread_ref, *refs):
    for s, stream_ref in enumerate(refs[:-1]):
        put_parcels(each, s, spread_ref[s], stream_ref[...], refs[-1])


def pack(k, spread, streams, owners, plan):
    each = plan.out[k]
    shape = (owners, len(streams) * each, streams[0].shape[1])
    return pl.pallas_call(
        functools.partial(pack_kernel, each),
        in_specs=[VMEM] * (1 + len(streams)),
        out_specs=VMEM,
        out_shape=pltpu.HBM(shape, BF16),
        compiler_params=params(24),
    )(in_hbm(spread), *map(in_hbm, streams))


def unset_kernel(out_ref):
    pass


def unset(shape):
    return pl.pallas_call(
        unset_kernel,
        name="unset",
        out_specs=pl.BlockSpec(memory_space=pl.ANY),
        out_shape=pltpu.HBM(shape, BF16),
        compiler_params=params(4),
    )()


def gated(gates, spreads, back):
    total = 0.0
    for j, spread in enumerate(spreads):
        total = total + gates[:, j:j + 1] * contract(spread, back, ((1,), (0,)))
    return total


def choices(code, plan, k, owners):
    return [
        one_hot(in_round(code[:, 4 + j:5 + j], plan.back, k, code[:, j:j + 1]), owners * plan.back[k])
        for j in range(2)
    ]


def combine_ahead_kernel(plan, parts, head_ref, flag_ref, code_ref, gates_ref, back_ref, late_ref, *refs):
    stream_refs, (acc_ref, pick_ref) = refs[:parts], refs[parts:]
    code = code_ref[...]
    owners, rows, width = back_ref.shape
    flat = back_ref[...].reshape(owners * rows, width)
    acc_ref[...] = gated(gates_ref[...], choices(code, plan, 0, owners), flat)
    step = width // parts
    for s in range(parts):
        start = pl.multiple_of((head_ref[0] + s) % parts * step, step)
        acc_ref[:, pl.ds(start, step)] = acc_ref[:, pl.ds(start, step)] + stream_refs[s][...].astype(F32)
    for j, spread in enumerate(choices(code, plan, 1, owners)):
        pick_ref[j] = spread

    @pl.when(flag_ref[0] > 0)
    def _():
        late = late_ref[...].reshape(owners * plan.back[2], width)
        acc_ref[...] = acc_ref[...] + gated(gates_ref[...], choices(code, plan, 2, owners), late)


def combine_ahead(head, flag, code, gates, back, late, streams, plan):
    owners, _, width = back.shape
    tokens = code.shape[0]
    return pl.pallas_call(
        functools.partial(combine_ahead_kernel, plan, len(streams)),
        name="combine_ahead",
        in_specs=[SMEM] * 2 + [VMEM] * (4 + len(streams)),
        out_specs=[VMEM] * 2,
        out_shape=[
            pltpu.HBM((tokens, width), F32),
            pltpu.HBM((2, tokens, owners * plan.back[1]), BF16),
        ],
        compiler_params=params(28),
    )(head, flag, code, gates, back, late, *streams)


def combine_kernel(gates_ref, acc_ref, pick_ref, back_ref, out_ref):
    owners, rows, step = back_ref.shape
    flat = back_ref[...].reshape(owners * rows, step)
    total = acc_ref[...]
    for j in range(2):
        total = total + gates_ref[:, j:j + 1] * contract(pick_ref[j], flat, ((1,), (0,)))
    out_ref[...] = total.astype(BF16)


def combine(gates, acc, picks, back):
    tokens, width = acc.shape
    owners, rows, _ = back.shape
    step = min(512, width)

    def whole(x):
        return pl.BlockSpec(x.shape, lambda d: (0,) * len(x.shape))

    narrow = pl.BlockSpec((tokens, step), lambda d: (0, d))
    return pl.pallas_call(
        combine_kernel,
        name="combine",
        grid=(width // step,),
        in_specs=[
            whole(gates),
            narrow,
            whole(picks),
            pl.BlockSpec((owners, rows, step), lambda d: (0, 0, d)),
        ],
        out_specs=narrow,
        out_shape=jax.ShapeDtypeStruct((tokens, width), BF16),
        compiler_params=params(20),
    )(gates, in_hbm(acc), in_hbm(picks), in_vmem(back))


def batch_columns(meta, expert, local_experts, plan):
    owners = meta.shape[0]
    counts = jnp.where(
        lax.broadcasted_iota(jnp.int32, meta.shape, 1) < local_experts, meta, 0
    ).astype(F32)
    lanes = counts.shape[1]
    row = lax.broadcasted_iota(jnp.int32, (lanes, lanes), 0)
    col = lax.broadcasted_iota(jnp.int32, (lanes, lanes), 1)
    below = jnp.where(row < col, 1.0, 0.0).astype(BF16)
    offsets = contract(counts.astype(BF16), below, ((1,), (0,)))
    batch = owners * CAP
    source_row = lax.broadcasted_iota(jnp.int32, (batch, owners), 0) // CAP
    source_col = lax.broadcasted_iota(jnp.int32, (batch, owners), 1)
    expand = jnp.where(source_row == source_col, 1.0, 0.0).astype(BF16)
    lane = lax.broadcasted_iota(jnp.int32, (batch, lanes), 1)

    def column(values, picked):
        wide = contract(expand, values.astype(BF16), ((1,), (0,)))
        return jnp.sum(jnp.where(picked, wide, 0.0), axis=1, keepdims=True).astype(jnp.int32)

    count = column(counts, lane == expert)
    offset = column(offsets, lane == expert)
    front = column(counts, lane < plan.ahead)
    index = lax.broadcasted_iota(jnp.int32, (batch, 1), 0)
    rank = index % CAP
    valid = rank < count
    place = offset + rank
    back = jnp.where(
        (expert < plan.ahead) & (place < plan.back[0]),
        place,
        plan.back[0] + place - jnp.minimum(front, plan.back[0]),
    )
    return index // CAP, jnp.where(valid, place, -1), jnp.where(valid, back, -1)


def expert_kernel(
    first, taken, given, has_base, local_experts, parts, plan, flag_ref, meta_ref, gain_ref, *refs
):
    x_refs, refs = refs[:len(taken)], refs[len(taken):]
    gate_ref, up_ref, down_ref = refs[:3]
    base_ref = refs[3] if has_base else None
    refs = refs[3 + has_base:]
    out_refs, (batch_ref, acc_ref, done_ref) = refs[:len(given)], refs[len(given):]
    e = pl.program_id(0)
    f = pl.program_id(1)
    last_f = pl.num_programs(1) - 1
    batch = batch_ref.shape[0]
    meta = meta_ref[...]

    @pl.when(f == 0)
    def _():
        source, place, _ = batch_columns(meta, first + e, local_experts, plan)

        context = source // parts
        block = source % parts

        def rows_of(i, k):
            owners, rows, step = x_refs[i].shape
            pieces = x_refs[i][...].reshape(owners // parts, parts, rows, step)
            found = []
            for h in range(parts):
                turn = (h - block + parts) % parts
                spread = one_hot(
                    in_round(place, plan.out, k, context * parts + turn), owners * plan.out[k]
                )
                flat = pieces[:, h].reshape(owners // parts * rows, step)
                found.append(contract(spread, flat, ((1,), (0,))))
            return jnp.concatenate(found, axis=1)

        total = 0.0
        for i, k in enumerate(taken):
            if k < 2:
                total = total + rows_of(i, k)
        acc_ref[...] = total
        for i, k in enumerate(taken):
            if k == 2:

                @pl.when(flag_ref[0] > 0)
                def _():
                    acc_ref[...] = acc_ref[...] + rows_of(i, k)

        stream = acc_ref[...]
        scale = lax.rsqrt(jnp.mean(stream * stream, axis=-1, keepdims=True) + EPS)
        batch_ref[...] = (stream * scale * gain_ref[...]).astype(BF16)

    x = batch_ref[...]
    gate = contract(x, gate_ref[...], ((1,), (0,)))
    upward = contract(x, up_ref[...], ((1,), (0,)))
    hidden = (gate / (1.0 + jnp.exp(-gate)) * upward).astype(BF16)
    part = contract(hidden, down_ref[...], ((1,), (0,)))

    @pl.when(f == 0)
    def _():
        acc_ref[...] = part

    @pl.when((f > 0) & (f < last_f))
    def _():
        acc_ref[...] = acc_ref[...] + part

    @pl.when(f == last_f)
    def _():
        done_ref[e] = (acc_ref[...] + part).astype(BF16)

    @pl.when((e == pl.num_programs(0) - 1) & (f == last_f))
    def _():
        count = done_ref.shape[0]
        columns = [batch_columns(meta, first + i, local_experts, plan) for i in range(count)]
        source = jnp.concatenate([c[0] for c in columns], axis=0)
        back = jnp.concatenate([c[2] for c in columns], axis=0)
        done = done_ref[...].reshape(count * batch, done_ref.shape[2])

        def put(i, k):
            owners, rows, width = out_refs[i].shape
            spread = one_hot(in_round(back, plan.back, k, source), owners * rows)
            rows_out = contract(spread, done, ((0,), (0,)))
            if has_base and k == 1:
                rows_out = rows_out + base_ref[...].reshape(owners * rows, width).astype(F32)
            out_refs[i][...] = rows_out.astype(BF16).reshape(owners, rows, width)

        for i, k in enumerate(given):
            if k < 2:
                put(i, k)
            else:

                @pl.when(flag_ref[0] > 0)
                def _():
                    put(i, k)


def serve_experts(flag, meta, gain, parts, received, weights, base, first, taken, given, plan):
    w_gate, w_up, w_down = weights
    local_experts, width, hidden = w_gate.shape
    owners = meta.shape[0]
    count = plan.ahead
    split = 2
    step = hidden // split

    def whole(x):
        return pl.BlockSpec(x.shape, lambda e, f: (0,) * len(x.shape))

    in_spec = pl.BlockSpec((None, width, step), lambda e, f: (first + e, 0, f))
    extra = [] if base is None else [in_hbm(base)]
    outs = [pltpu.HBM((owners, plan.back[k], width), BF16) for k in given]
    received = [in_vmem(x) if k == 1 else in_hbm(x) for k, x in zip(taken, received)]
    batch = owners * CAP
    return pl.pallas_call(
        functools.partial(
            expert_kernel, first, taken, given, base is not None, local_experts, parts, plan
        ),
        grid=(count, split),
        in_specs=[SMEM, whole(meta), whole(gain)]
        + [whole(x) for x in received]
        + [
            in_spec,
            in_spec,
            pl.BlockSpec((None, step, width), lambda e, f: (first + e, f, 0)),
        ]
        + [whole(x) for x in extra],
        out_specs=[whole(x) for x in outs],
        out_shape=outs,
        scratch_shapes=[
            pltpu.VMEM((batch, width), BF16),
            pltpu.VMEM((batch, width), F32),
            pltpu.VMEM((count, batch, width), BF16),
        ],
        compiler_params=params(44),
    )(flag, meta, gain, *received, w_gate, w_up, w_down, *extra)


def everywhere(x):
    return lax.all_to_all(x, ("ctx", "head"), split_axis=0, concat_axis=0, tiled=True)


def everywhere_if(flag, x):
    return lax.cond(flag[0] > 0, everywhere, lambda y: unset(y.shape), x)


def body_dense(
    queries,
    keys,
    values,
    mem_route,
    head_gain,
    residual_in,
    ffn_gain,
    expert_ids,
    expert_gates,
    w_gate,
    w_up,
    w_down,
):
    length = queries.shape[0]
    ctx_count = lax.axis_size("ctx")
    head_count = lax.axis_size("head")
    owners = ctx_count * head_count
    local_experts = w_gate.shape[0]
    pairs = local_experts // PAIR
    chunks = 2 if pairs % 2 == 0 else 1
    route_row = mem_route.reshape(1, length)
    route_col = mem_route.reshape(length, 1)

    states = block_states(keys, values, route_row)
    pieces = lax.all_to_all(states, "ctx", split_axis=0, concat_axis=0, tiled=True)
    before = exclusive_prefix(pieces.reshape(ctx_count, -1, HD))
    carried = lax.all_to_all(
        before.reshape(states.shape), "ctx", split_axis=0, concat_axis=0, tiled=True
    )
    local = local_attention(queries, keys, values, route_row, route_col)
    normed = mix_and_norm(queries, carried, local, route_col, head_gain[None], head_count)
    by_token = lax.all_to_all(normed, "head", split_axis=0, concat_axis=0, tiled=True)

    stream, parcels = pack_dense(
        residual_in, by_token, ffn_gain[None], expert_ids, chunks, owners, local_experts
    )
    backs = []
    for c in range(chunks):
        received = lax.all_to_all(
            parcels[c], ("ctx", "head"), split_axis=0, concat_axis=0, tiled=True
        )
        served = serve_dense(received, w_gate, w_up, w_down, c)
        backs.append(
            lax.all_to_all(served, ("ctx", "head"), split_axis=0, concat_axis=0, tiled=True)
        )
    return combine_dense(stream, expert_ids, expert_gates, backs, local_experts)


def body_compact(
    queries,
    keys,
    values,
    mem_route,
    head_gain,
    residual_in,
    ffn_gain,
    expert_ids,
    expert_gates,
    w_gate,
    w_up,
    w_down,
):
    length = queries.shape[0]
    contexts = lax.axis_size("ctx")
    parts = lax.axis_size("head")
    local_experts = w_gate.shape[0]
    plan = Plan(local_experts)
    route_row = mem_route.reshape(1, length)
    route_col = mem_route.reshape(length, 1)
    head = lax.axis_index("head").astype(jnp.int32)[None]

    def turned(pieces, step):
        return [pieces[0]] + [
            lax.ppermute(pieces[s], "head", [(h, (h + step * s) % parts) for h in range(parts)])
            for s in range(1, parts)
        ]

    ids = turned([expert_ids.T] * parts, 1)
    states = block_states(keys, values, route_row)
    pieces = lax.all_to_all(states, "ctx", split_axis=0, concat_axis=0, tiled=True)
    code, counts, *spreads = route(head, ids, contexts, local_experts, plan)
    before = prefix_with_counts(pieces.reshape(contexts, -1, HD), counts)
    carried = lax.all_to_all(before, "ctx", split_axis=0, concat_axis=0, tiled=True)
    cut = columns_by_turn(head, residual_in, parts)
    residuals = turned(cut, 1)
    local = local_attention(queries, keys, values, route_row, route_col)
    meta, flag, parcels, own_streams = mix_and_pack(
        head,
        queries,
        carried,
        counts.shape[1],
        local,
        route_col,
        head_gain[None],
        residuals,
        spreads[0],
        local_experts,
        plan,
    )
    weights = (w_gate, w_up, w_down)
    gain = ffn_gain[None]
    received = [everywhere(parcels)]
    parcels = pack(1, spreads[1], own_streams, contexts * parts, plan)
    received.append(everywhere(parcels))
    streams = turned(own_streams, -1)
    back_0, base = serve_experts(
        flag, meta, gain, parts, received[:1], weights, None, 0, (0,), (0, 1), plan
    )
    received.append(
        lax.cond(
            flag[0] > 0,
            lambda spread, pieces: everywhere(pack(2, spread, pieces, contexts * parts, plan)),
            lambda spread, pieces: unset(
                (contexts * parts, parts * plan.out[2], pieces[0].shape[1])
            ),
            spreads[2],
            own_streams,
        )
    )
    back_0 = everywhere(back_0)
    back_1, back_2 = serve_experts(
        flag, meta, gain, parts, received, weights, base, plan.ahead, (0, 1, 2), (1, 2), plan
    )
    back_2 = everywhere_if(flag, back_2)
    back_1 = everywhere(back_1)
    acc, picks = combine_ahead(head, flag, code, expert_gates, back_0, back_2, streams, plan)
    return combine(expert_gates, acc, picks, back_1)


def body(*args):
    local_experts = args[-1].shape[0]
    compact = local_experts * CAP % (4 * GROUP_ROWS) == 0
    return body_compact(*args) if compact else body_dense(*args)


def solution(mesh):
    placed = (
        P("ctx", "head"),
        P("ctx", "head"),
        P("ctx", "head"),
        P("ctx"),
        P("head"),
        P(("ctx", "head"), None),
        P(),
        P(("ctx", "head"), None),
        P(("ctx", "head"), None),
        P(("ctx", "head"), None, None),
        P(("ctx", "head"), None, None),
        P(("ctx", "head"), None, None),
    )
    return jax.shard_map(
        body, mesh=mesh, in_specs=placed, out_specs=P(("ctx", "head"), None), check_vma=False
    )
```

```python
import functools

import jax
import jax.numpy as jnp
from jax import lax
from jax.experimental import pallas as pl
from jax.experimental.pallas import tpu as pltpu
from jax.sharding import PartitionSpec as P


HD = 128
M = 4
CAP = 4
PAIR = 2
GROUP_ROWS = PAIR * CAP
EPS = 1e-06
F32 = jnp.float32
BF16 = jnp.bfloat16


def params(mebibytes=60):
    return pltpu.CompilerParams(vmem_limit_bytes=mebibytes * 1024 * 1024)


def in_hbm(x):
    return pltpu.with_memory_space_constraint(x, pltpu.HBM)


def in_vmem(x):
    return pltpu.with_memory_space_constraint(x, pltpu.VMEM)


def contract(a, b, dims):
    return lax.dot_general(a, b, (dims, ((), ())), preferred_element_type=F32)


def state_kernel(key_ref, value_ref, route_ref, out_ref):
    keys_t = key_ref[...].T
    values = value_ref[...]
    route = route_ref[...]
    for m in range(M):
        mask = (route == m).astype(F32).astype(BF16)
        out_ref[pl.ds(m * HD, HD), :] = contract(keys_t * mask, values, ((1,), (0,))).astype(BF16)


def block_states(keys, values, route_row):
    length, width = keys.shape
    heads = width // HD
    return pl.pallas_call(
        state_kernel,
        name="block_states",
        grid=(heads,),
        in_specs=[
            pl.BlockSpec((length, HD), lambda h: (0, h)),
            pl.BlockSpec((length, HD), lambda h: (0, h)),
            pl.BlockSpec((1, length), lambda h: (0, 0)),
        ],
        out_specs=pl.BlockSpec((M * HD, HD), lambda h: (h, 0)),
        out_shape=pltpu.HBM((heads * M * HD, HD), BF16),
        compiler_params=params(16),
    )(in_hbm(keys), in_hbm(values), in_hbm(route_row))


def prefix_kernel(ranks, piece_ref, out_ref):
    total = jnp.zeros(piece_ref.shape[1:], F32)
    for r in range(ranks):
        out_ref[r] = total.astype(BF16)
        if r + 1 < ranks:
            total = total + piece_ref[r].astype(F32)


def exclusive_prefix(pieces):
    return pl.pallas_call(
        functools.partial(prefix_kernel, pieces.shape[0]),
        name="exclusive_prefix",
        out_shape=jax.ShapeDtypeStruct(pieces.shape, BF16),
        compiler_params=params(),
    )(pieces)


def local_kernel(rows, query_ref, key_ref, value_ref, route_row_ref, route_col_ref, out_ref, weight_ref):
    length = query_ref.shape[0]

    @pl.when(pl.program_id(0) == 0)
    def _():
        route_row = route_row_ref[...]
        for i in range(length // rows):
            span = (i + 1) * rows
            column = route_col_ref[pl.ds(i * rows, rows), :]
            same = jnp.where(column == route_row[:, :span], 2.0, 1.0)
            t = lax.broadcasted_iota(jnp.int32, (rows, span), 0) + i * rows
            s = lax.broadcasted_iota(jnp.int32, (rows, span), 1)
            weight_ref[pl.ds(i * rows, rows), :span] = jnp.where(t >= s, same, 0.0)

    for i in range(length // rows):
        span = (i + 1) * rows
        query = query_ref[pl.ds(i * rows, rows), :]
        scores = contract(query, key_ref[:span, :], ((1,), (1,)))
        weighted = (scores * weight_ref[pl.ds(i * rows, rows), :span]).astype(BF16)
        out_ref[pl.ds(i * rows, rows), :] = contract(weighted, value_ref[:span, :], ((1,), (0,)))


def local_attention(queries, keys, values, route_row, route_col):
    length, width = queries.shape
    heads = width // HD
    rows = min(256, length)
    wide = pl.BlockSpec((length, HD), lambda h: (0, h))
    return pl.pallas_call(
        functools.partial(local_kernel, rows),
        name="local_attention",
        grid=(heads,),
        in_specs=[
            wide,
            wide,
            wide,
            pl.BlockSpec((1, length), lambda h: (0, 0)),
            pl.BlockSpec((length, 1), lambda h: (0, 0)),
        ],
        out_specs=wide,
        out_shape=jax.ShapeDtypeStruct((length, width), F32),
        scratch_shapes=[pltpu.VMEM((length, length), F32)],
        compiler_params=params(32),
    )(in_hbm(queries), in_hbm(keys), in_hbm(values), route_row, route_col)


def mix_kernel(query_ref, state_ref, local_ref, route_col_ref, gain_ref, out_ref):
    parts, rows, _ = out_ref.shape
    query = query_ref[...]
    column = route_col_ref[...]
    wide = jnp.concatenate(
        [query * jnp.where(column == m, 2.0, 1.0).astype(BF16) for m in range(M)], axis=1
    )
    mixed = contract(wide, state_ref[...], ((1,), (0,))) + local_ref[...]
    scale = lax.rsqrt(jnp.mean(mixed * mixed, axis=-1, keepdims=True) + EPS)
    normed = (mixed * scale * gain_ref[...]).astype(BF16)
    for p in range(parts):
        out_ref[p] = normed[p * rows:(p + 1) * rows]


def mix_and_norm(queries, state, local, route_col, head_gain, parts):
    length, width = queries.shape
    heads = width // HD
    wide = pl.BlockSpec((length, HD), lambda h: (0, h))
    return pl.pallas_call(
        mix_kernel,
        name="mix_and_norm",
        grid=(heads,),
        in_specs=[
            wide,
            pl.BlockSpec((M * HD, HD), lambda h: (h, 0)),
            wide,
            pl.BlockSpec((length, 1), lambda h: (0, 0)),
            pl.BlockSpec((1, HD), lambda h: (0, h)),
        ],
        out_specs=pl.BlockSpec((parts, length // parts, HD), lambda h: (0, 0, h)),
        out_shape=jax.ShapeDtypeStruct((parts, length // parts, width), BF16),
        compiler_params=params(),
    )(queries, state, local, route_col, head_gain)


def slot_columns(ids, experts, local_experts):
    tokens = ids.shape[0]
    owners = experts // local_experts
    lanes = lax.broadcasted_iota(jnp.int32, (tokens, experts), 1)
    chosen = [(ids[:, j:j + 1] == lanes).astype(F32) for j in range(2)]
    t = lax.broadcasted_iota(jnp.int32, (tokens, tokens), 0)
    s = lax.broadcasted_iota(jnp.int32, (tokens, tokens), 1)
    earlier = contract(
        (t > s).astype(F32).astype(BF16), (chosen[0] + chosen[1]).astype(BF16), ((1,), (0,))
    )
    slots = []
    for j in range(2):
        rank = jnp.sum(earlier * chosen[j], axis=1, keepdims=True).astype(jnp.int32)
        expert = ids[:, j:j + 1]
        owner = expert // local_experts
        local = expert % local_experts
        slots.append(
            ((local // PAIR) * owners + owner) * GROUP_ROWS + (local % PAIR) * CAP + rank
        )
    return slots


def pack_dense_kernel(chunks, local_experts, residual_ref, piece_ref, gain_ref, ids_ref, *refs):
    stream_ref, out_refs = refs[0], refs[1:1 + chunks]
    parts, rows, _ = piece_ref.shape
    owners, groups, _, width = out_refs[0].shape
    normed = jnp.concatenate([piece_ref[p] for p in range(parts)], axis=1)
    stream = (residual_ref[...].astype(F32) + normed.astype(F32)).astype(BF16)
    stream_ref[...] = stream
    wide = stream.astype(F32)
    scale = lax.rsqrt(jnp.mean(wide * wide, axis=-1, keepdims=True) + EPS)
    ffn_in = (wide * scale * gain_ref[...]).astype(BF16)
    experts = owners * local_experts
    slot0, slot1 = slot_columns(ids_ref[...], experts, local_experts)
    span = owners * GROUP_ROWS
    for c in range(chunks):
        for g in range(groups):
            base = (c * groups + g) * span
            lanes = lax.broadcasted_iota(jnp.int32, (rows, span), 1) + base
            spread = jnp.where((slot0 == lanes) | (slot1 == lanes), 1.0, 0.0).astype(BF16)
            packed = contract(spread, ffn_in, ((0,), (0,))).astype(BF16)
            out_refs[c][:, g] = packed.reshape(owners, GROUP_ROWS, width)


def pack_dense(residual, pieces, gain, ids, chunks, owners, local_experts):
    tokens, width = residual.shape
    groups = local_experts // PAIR // chunks
    parcel = jax.ShapeDtypeStruct((owners, groups, GROUP_ROWS, width), BF16)
    out = pl.pallas_call(
        functools.partial(pack_dense_kernel, chunks, local_experts),
        name="pack_dense",
        out_shape=[jax.ShapeDtypeStruct((tokens, width), BF16)] + [parcel] * chunks,
        compiler_params=params(),
    )(residual, pieces, gain, ids)
    return out[0], out[1:]


def expert_dense_kernel(x_ref, gate_ref, up_ref, down_ref, out_ref, acc_ref):
    e = pl.program_id(1)
    f = pl.program_id(2)
    owners, rows, width = x_ref.shape
    x = x_ref[...].reshape(owners * rows, width)
    gate = contract(x, gate_ref[...], ((1,), (0,)))
    upward = contract(x, up_ref[...], ((1,), (0,)))
    row = lax.broadcasted_iota(jnp.int32, gate.shape, 0)
    mine = (row // CAP) % PAIR == e
    hidden = gate / (1.0 + jnp.exp(-gate)) * upward
    hidden = jnp.where(mine, hidden, 0.0).astype(BF16)
    part = contract(hidden, down_ref[...], ((1,), (0,)))
    first = (e == 0) & (f == 0)

    @pl.when(first)
    def _():
        acc_ref[...] = part

    @pl.when(jnp.logical_not(first))
    def _():
        acc_ref[...] = acc_ref[...] + part

    @pl.when((e == pl.num_programs(1) - 1) & (f == pl.num_programs(2) - 1))
    def _():
        out_ref[...] = acc_ref[...].astype(BF16).reshape(owners, rows, width)


def serve_dense(received, w_gate, w_up, w_down, chunk):
    owners, groups, rows, width = received.shape
    hidden = w_gate.shape[2]
    split = 2
    step = hidden // split
    first = chunk * groups * PAIR
    token_spec = pl.BlockSpec((owners, None, rows, width), lambda g, e, f: (0, g, 0, 0))
    in_spec = pl.BlockSpec((None, width, step), lambda g, e, f: (first + g * PAIR + e, 0, f))
    return pl.pallas_call(
        expert_dense_kernel,
        grid=(groups, PAIR, split),
        in_specs=[
            token_spec,
            in_spec,
            in_spec,
            pl.BlockSpec((None, step, width), lambda g, e, f: (first + g * PAIR + e, f, 0)),
        ],
        out_specs=token_spec,
        out_shape=jax.ShapeDtypeStruct(received.shape, BF16),
        scratch_shapes=[pltpu.VMEM((owners * rows, width), F32)],
        compiler_params=params(),
    )(received, w_gate, w_up, w_down)


def combine_dense_kernel(chunks, local_experts, stream_ref, ids_ref, gates_ref, *refs):
    back_refs, out_ref, first_ref, second_ref = refs[:chunks], refs[chunks], refs[-2], refs[-1]
    owners, groups, rows, _ = back_refs[0].shape
    span = owners * rows

    @pl.when(pl.program_id(0) == 0)
    def _():
        slot0, slot1 = slot_columns(ids_ref[...], owners * local_experts, local_experts)
        lanes = lax.broadcasted_iota(jnp.int32, first_ref.shape, 1)
        first_ref[...] = jnp.where(slot0 == lanes, 1.0, 0.0).astype(BF16)
        second_ref[...] = jnp.where(slot1 == lanes, 1.0, 0.0).astype(BF16)

    back = jnp.concatenate(
        [
            back_refs[c][:, g].reshape(span, back_refs[c].shape[3])
            for c in range(chunks)
            for g in range(groups)
        ],
        axis=0,
    )
    gates = gates_ref[...]
    total = stream_ref[...].astype(F32)
    total = total + gates[:, 0:1] * contract(first_ref[...], back, ((1,), (0,)))
    total = total + gates[:, 1:2] * contract(second_ref[...], back, ((1,), (0,)))
    out_ref[...] = total.astype(BF16)


def combine_dense(stream, ids, gates, backs, local_experts):
    tokens, width = stream.shape
    owners, groups, rows, _ = backs[0].shape
    chunks = len(backs)
    slots = owners * groups * rows * chunks
    step = min(512, width)
    back_spec = pl.BlockSpec((owners, groups, rows, step), lambda d: (0, 0, 0, d))
    return pl.pallas_call(
        functools.partial(combine_dense_kernel, chunks, local_experts),
        name="combine_dense",
        grid=(width // step,),
        in_specs=[
            pl.BlockSpec((tokens, step), lambda d: (0, d)),
            pl.BlockSpec(ids.shape, lambda d: (0, 0)),
            pl.BlockSpec(gates.shape, lambda d: (0, 0)),
        ]
        + [back_spec] * chunks,
        out_specs=pl.BlockSpec((tokens, step), lambda d: (0, d)),
        out_shape=jax.ShapeDtypeStruct((tokens, width), BF16),
        scratch_shapes=[pltpu.VMEM((tokens, slots), BF16)] * 2,
        compiler_params=params(),
    )(stream, ids, gates, *backs)


class Plan:
    def __init__(self, local_experts):
        dense = local_experts * CAP
        self.ahead = local_experts // 2
        first = self.ahead * CAP
        self.out = (first, first // 2, dense - first - first // 2)
        self.back = (first // 2, first, dense - first - first // 2)


def in_round(place, bounds, k, owner):
    low = sum(bounds[:k])
    inside = (place >= low) & (place < low + bounds[k])
    return jnp.where(inside, owner * bounds[k] + place - low, -1)


def one_hot(column, width):
    lanes = lax.broadcasted_iota(jnp.int32, (column.shape[0], width), 1)
    return jnp.where(column == lanes, 1.0, 0.0).astype(BF16)


VMEM = pl.BlockSpec(memory_space=pltpu.VMEM)
SMEM = pl.BlockSpec(memory_space=pltpu.SMEM)


def id_columns(id_refs):
    parts = len(id_refs)
    pad = -2 * parts % 8
    rows = [ref[...].astype(F32) for ref in id_refs]
    if pad:
        rows.append(jnp.zeros((pad, id_refs[0].shape[1]), F32))
    rows = jnp.concatenate(rows, axis=0)
    return rows, rows.T


def counts_kernel(local_experts, plan, parts, head_ref, *refs):
    id_refs, meta_ref = refs[:parts], refs[parts]
    tokens = id_refs[0].shape[1]
    contexts = meta_ref.shape[0]
    owners = contexts * parts
    head = head_ref[0]
    owner_lane = lax.broadcasted_iota(jnp.int32, (tokens, owners), 1)
    local_lane = lax.broadcasted_iota(jnp.int32, (tokens, HD), 1)
    owner_row = lax.broadcasted_iota(jnp.int32, (contexts, owners), 1)
    context_row = lax.broadcasted_iota(jnp.int32, (contexts, owners), 0)
    mine = jnp.where(owner_row == context_row * parts + head, 1.0, 0.0).astype(BF16)
    lane = lax.broadcasted_iota(jnp.int32, (owners, HD), 1)
    _, id_cols = id_columns(id_refs)
    flags = 0.0
    metas = []
    for b in range(parts):
        counts = 0.0
        for j in range(2):
            ids = id_cols[:, 2 * b + j:2 * b + j + 1].astype(jnp.int32)
            counts = counts + contract(
                (ids // local_experts == owner_lane).astype(F32).astype(BF16),
                (ids % local_experts == local_lane).astype(F32).astype(BF16),
                ((0,), (0,)),
            )
        total = jnp.sum(counts, axis=1, keepdims=True)
        front = jnp.sum(jnp.where(lane < plan.ahead, counts, 0.0), axis=1, keepdims=True)
        over = (total > sum(plan.out[:2])) | (
            total - jnp.minimum(front, plan.back[0]) > plan.back[1]
        )
        flags = jnp.maximum(flags, jnp.max(jnp.where(over, 1.0, 0.0), axis=0, keepdims=True))
        metas.append(contract(mine, counts.astype(BF16), ((1,), (0,))))
    meta_lane = lax.broadcasted_iota(jnp.int32, (contexts, HD), 1)
    meta_ref[...] = jnp.zeros(meta_ref.shape, F32)
    for b in range(parts):
        marked = jnp.where(meta_lane == local_experts, flags, metas[b])
        for c in range(contexts):
            meta_ref[c, b:b + 1, :] = marked[c:c + 1]


def count_choices(head, ids, contexts, local_experts, plan):
    parts = len(ids)
    return pl.pallas_call(
        functools.partial(counts_kernel, local_experts, plan, parts),
        name="count_choices",
        in_specs=[SMEM] + [VMEM] * parts,
        out_specs=VMEM,
        out_shape=jax.ShapeDtypeStruct((contexts, parts + -parts % 8, HD), F32),
        compiler_params=params(16),
    )(head, *ids)


def route_kernel(local_experts, experts, plan, parts, *refs):
    id_refs, code_ref, spread_refs = refs[:parts], refs[parts], refs[parts + 1:]
    tokens = id_refs[0].shape[1]
    t = lax.broadcasted_iota(jnp.int32, (tokens, tokens), 0)
    s = lax.broadcasted_iota(jnp.int32, (tokens, tokens), 1)
    earlier_mask = (t > s).astype(F32).astype(BF16)
    row = lax.broadcasted_iota(jnp.int32, (experts, experts), 0)
    col = lax.broadcasted_iota(jnp.int32, (experts, experts), 1)
    mates = row // local_experts == col // local_experts
    below = jnp.where(mates & (row < col), 1.0, 0.0).astype(BF16)
    ahead = jnp.where(mates & (row % local_experts < plan.ahead), 1.0, 0.0).astype(BF16)
    lanes = lax.broadcasted_iota(jnp.int32, (tokens, experts), 1)
    id_rows, id_cols = id_columns(id_refs)
    for b in range(parts):
        ids = [id_cols[:, 2 * b + j:2 * b + j + 1].astype(jnp.int32) for j in range(2)]
        chosen = [(i == lanes).astype(F32) for i in ids]
        both = (chosen[0] + chosen[1]).astype(BF16)
        counts = contract(jnp.ones((8, tokens), BF16), both, ((1,), (0,))).astype(BF16)
        position = contract(earlier_mask, both, ((1,), (0,))) + contract(counts, below, ((1,), (0,)))[0:1]
        places = [jnp.sum(position * c, axis=1, keepdims=True) for c in chosen]
        wide = jnp.concatenate(places + [jnp.zeros((tokens, HD - 2), F32)], axis=1)
        place_rows = wide.T[0:8]
        if b == 0:
            aheads = contract(counts, ahead, ((1,), (0,)))[0:1]
            slot_lane = lax.broadcasted_iota(jnp.int32, code_ref.shape, 1)
            code = jnp.zeros(code_ref.shape, jnp.int32)
            for j in range(2):
                place = places[j].astype(jnp.int32)
                front = jnp.sum(aheads * chosen[j], axis=1, keepdims=True).astype(jnp.int32)
                back = jnp.where(
                    (ids[j] % local_experts < plan.ahead) & (place < plan.back[0]),
                    place,
                    plan.back[0] + place - jnp.minimum(front, plan.back[0]),
                )
                code = jnp.where(slot_lane == j, ids[j] // local_experts, code)
                code = jnp.where(slot_lane == 4 + j, back, code)
            code_ref[...] = code
        for k, spread_ref in enumerate(spread_refs):
            slots = spread_ref.shape[1]
            slot = lax.broadcasted_iota(jnp.int32, (slots, tokens), 0)
            hit = None
            for j in range(2):
                owner = id_rows[2 * b + j:2 * b + j + 1].astype(jnp.int32) // local_experts
                index = in_round(place_rows[j:j + 1].astype(jnp.int32), plan.out, k, owner)
                hit = (slot == index) if hit is None else hit | (slot == index)
            spread_ref[b] = jnp.where(hit, 1.0, 0.0).astype(BF16)


def route(ids, contexts, local_experts, plan):
    parts = len(ids)
    tokens = ids[0].shape[1]
    owners = contexts * parts
    return pl.pallas_call(
        functools.partial(route_kernel, local_experts, owners * local_experts, plan, parts),
        name="route",
        in_specs=[VMEM] * parts,
        out_specs=[VMEM] * 4,
        out_shape=[pltpu.HBM((tokens, HD), jnp.int32)]
        + [pltpu.HBM((parts, owners * rows, tokens), BF16) for rows in plan.out],
        compiler_params=params(24),
    )(*ids)


def prefix_with_counts_kernel(piece_ref, meta_ref, out_ref):
    ranks, rows, _ = piece_ref.shape
    total = jnp.zeros(piece_ref.shape[1:], F32)
    for r in range(ranks):
        out_ref[r, :rows, :] = total.astype(BF16)
        out_ref[r, rows:, :] = meta_ref[r].astype(BF16)
        if r + 1 < ranks:
            total = total + piece_ref[r].astype(F32)


def prefix_with_counts(pieces, meta):
    ranks, rows, width = pieces.shape
    return pl.pallas_call(
        prefix_with_counts_kernel,
        name="prefix_with_counts",
        in_specs=[VMEM] * 2,
        out_specs=VMEM,
        out_shape=pltpu.HBM((ranks, rows + meta.shape[1], width), BF16),
        compiler_params=params(12),
    )(pieces, meta)


def columns_kernel(parts, head_ref, whole_ref, *out_refs):
    step = whole_ref.shape[1] // parts
    for s in range(parts):
        start = pl.multiple_of((head_ref[0] + s) % parts * step, step)
        out_refs[s][...] = whole_ref[:, pl.ds(start, step)]


def columns_by_turn(head, whole, parts):
    tokens, width = whole.shape
    return pl.pallas_call(
        functools.partial(columns_kernel, parts),
        name="columns_by_turn",
        in_specs=[SMEM, VMEM],
        out_specs=[VMEM] * parts,
        out_shape=[pltpu.HBM((tokens, width // parts), BF16)] * parts,
        compiler_params=params(12),
    )(head, whole)


def mix_pack_kernel(
    parts, local_experts, plan, head_ref, query_ref, state_ref, tail_ref, local_ref, route_col_ref, gain_ref, *refs
):
    residual_refs, spread_ref = refs[:parts], refs[parts]
    refs = refs[parts + 1:]
    meta_ref, flag_ref, parcel_ref, stream_refs = refs[0], refs[1], refs[2], refs[3:3 + parts]
    normed_ref = refs[-1]
    head = head_ref[0]
    pieces, rows, _ = state_ref.shape
    contexts, tail, _ = tail_ref.shape
    rows -= tail
    width = query_ref.shape[1]
    together = width // HD
    share = pieces // together
    column = route_col_ref[...]
    doubled = [jnp.where(column == m, 2.0, 1.0).astype(BF16) for m in range(M)]
    for g in range(together):
        span = slice(g * HD, (g + 1) * HD)
        query = query_ref[:, span]
        wide = jnp.concatenate([query * weight for weight in doubled], axis=1)
        state = jnp.concatenate([state_ref[g * share + i, :rows, :] for i in range(share)], axis=0)
        mixed = contract(wide, state, ((1,), (0,))) + local_ref[:, span]
        scale = lax.rsqrt(jnp.mean(mixed * mixed, axis=-1, keepdims=True) + EPS)
        normed_ref[:, span] = (mixed * scale * gain_ref[:, span]).astype(BF16)

    @pl.when(pl.program_id(0) == 0)
    def _():
        counts = tail_ref[...].astype(F32)
        owners = contexts * parts
        lane = lax.broadcasted_iota(jnp.int32, counts.shape, 2)
        over = jnp.max(jnp.where(lane == local_experts, counts, 0.0))
        flag_ref[0] = (over > 0.5).astype(jnp.int32)
        source = lax.broadcasted_iota(jnp.int32, (owners, contexts * tail), 0)
        given = lax.broadcasted_iota(jnp.int32, (owners, contexts * tail), 1)
        turn = (head - source % parts + parts) % parts
        order = jnp.where(given == source // parts * tail + turn, 1.0, 0.0).astype(BF16)
        flat = counts.reshape(contexts * tail, counts.shape[2]).astype(BF16)
        meta_ref[...] = contract(order, flat, ((1,), (0,))).astype(jnp.int32)

    tokens = residual_refs[0].shape[0]
    for s in range(parts):
        start = pl.multiple_of((head - s + parts) % parts * tokens, tokens)
        normed = normed_ref[pl.ds(start, tokens), :]
        stream = (residual_refs[s][...].astype(F32) + normed.astype(F32)).astype(BF16)
        stream_refs[s][...] = stream
        put_parcels(plan.out[0], s, spread_ref[s], stream, parcel_ref)


def put_parcels(each, s, spread, stream, parcel_ref):
    owners, _, width = parcel_ref.shape
    packed = contract(spread, stream, ((1,), (0,))).astype(BF16)
    parcel_ref[:, s * each:(s + 1) * each, :] = packed.reshape(owners, each, width)


def mix_and_pack(head, queries, carried, tail, local, route_col, head_gain, residuals, spread, local_experts, plan):
    length, width = queries.shape
    heads = width // HD
    together = 2 if heads % 2 == 0 else 1
    step = together * HD
    contexts, rows, _ = carried.shape
    share = contexts * together // heads
    parts = len(residuals)
    tokens = length // parts
    owners = contexts * parts
    wide = pl.BlockSpec((length, step), lambda h: (0, h))
    narrow = pl.BlockSpec((tokens, step), lambda h: (0, h))

    def whole(x):
        return pl.BlockSpec(x.shape, lambda h: (0,) * len(x.shape))

    each = parts * plan.out[0]
    meta = pltpu.HBM((owners, HD), jnp.int32)
    out = pl.pallas_call(
        functools.partial(mix_pack_kernel, parts, local_experts, plan),
        name="mix_and_pack",
        grid=(heads // together,),
        in_specs=[
            SMEM,
            wide,
            pl.BlockSpec((share, rows, HD), lambda h: (h, 0, 0)),
            pl.BlockSpec((contexts, tail, HD), lambda h: (0, (rows - tail) // tail, 0)),
            wide,
            pl.BlockSpec((length, 1), lambda h: (0, 0)),
            pl.BlockSpec((1, step), lambda h: (0, h)),
        ]
        + [narrow] * parts
        + [whole(spread)],
        out_specs=[whole(meta), SMEM, pl.BlockSpec((owners, each, step), lambda h: (0, 0, h))]
        + [narrow] * parts,
        out_shape=[
            meta,
            jax.ShapeDtypeStruct((1,), jnp.int32),
            pltpu.HBM((owners, each, width), BF16),
        ]
        + [pltpu.HBM((tokens, width), BF16)] * parts,
        scratch_shapes=[pltpu.VMEM((length, step), BF16)],
        compiler_params=params(32),
    )(
        head,
        in_hbm(queries),
        carried,
        carried,
        local,
        route_col,
        head_gain,
        *map(in_hbm, residuals),
        in_hbm(spread),
    )
    return out[0], out[1], out[2], out[3:]


def pack_kernel(each, spread_ref, *refs):
    for s, stream_ref in enumerate(refs[:-1]):
        put_parcels(each, s, spread_ref[s], stream_ref[...], refs[-1])


def pack(k, spread, streams, owners, plan):
    each = plan.out[k]
    shape = (owners, len(streams) * each, streams[0].shape[1])
    return pl.pallas_call(
        functools.partial(pack_kernel, each),
        in_specs=[VMEM] * (1 + len(streams)),
        out_specs=VMEM,
        out_shape=pltpu.HBM(shape, BF16),
        compiler_params=params(24),
    )(in_hbm(spread), *map(in_hbm, streams))


def unset_kernel(out_ref):
    pass


def unset(shape):
    return pl.pallas_call(
        unset_kernel,
        name="unset",
        out_specs=pl.BlockSpec(memory_space=pl.ANY),
        out_shape=pltpu.HBM(shape, BF16),
        compiler_params=params(4),
    )()


def gated(gates, spreads, back):
    total = 0.0
    for j, spread in enumerate(spreads):
        total = total + gates[:, j:j + 1] * contract(spread, back, ((1,), (0,)))
    return total


def choices(code, plan, k, owners):
    return [
        one_hot(in_round(code[:, 4 + j:5 + j], plan.back, k, code[:, j:j + 1]), owners * plan.back[k])
        for j in range(2)
    ]


def combine_ahead_kernel(plan, parts, head_ref, flag_ref, code_ref, gates_ref, back_ref, late_ref, *refs):
    stream_refs, (acc_ref, pick_ref) = refs[:parts], refs[parts:]
    code = code_ref[...]
    owners, rows, width = back_ref.shape
    flat = back_ref[...].reshape(owners * rows, width)
    acc_ref[...] = gated(gates_ref[...], choices(code, plan, 0, owners), flat)
    step = width // parts
    for s in range(parts):
        start = pl.multiple_of((head_ref[0] + s) % parts * step, step)
        acc_ref[:, pl.ds(start, step)] = acc_ref[:, pl.ds(start, step)] + stream_refs[s][...].astype(F32)
    for j, spread in enumerate(choices(code, plan, 1, owners)):
        pick_ref[j] = spread

    @pl.when(flag_ref[0] > 0)
    def _():
        late = late_ref[...].reshape(owners * plan.back[2], width)
        acc_ref[...] = acc_ref[...] + gated(gates_ref[...], choices(code, plan, 2, owners), late)


def combine_ahead(head, flag, code, gates, back, late, streams, plan):
    owners, _, width = back.shape
    tokens = code.shape[0]
    return pl.pallas_call(
        functools.partial(combine_ahead_kernel, plan, len(streams)),
        name="combine_ahead",
        in_specs=[SMEM] * 2 + [VMEM] * (4 + len(streams)),
        out_specs=[VMEM] * 2,
        out_shape=[
            pltpu.HBM((tokens, width), F32),
            pltpu.HBM((2, tokens, owners * plan.back[1]), BF16),
        ],
        compiler_params=params(28),
    )(head, flag, code, gates, back, late, *streams)


def combine_kernel(gates_ref, acc_ref, pick_ref, back_ref, out_ref):
    owners, rows, _ = back_ref.shape
    step = out_ref.shape[1]
    start = pl.multiple_of(pl.program_id(0) * step, step)
    flat = back_ref[:, :, pl.ds(start, step)].reshape(owners * rows, step)
    total = acc_ref[...]
    for j in range(2):
        total = total + gates_ref[:, j:j + 1] * contract(pick_ref[j], flat, ((1,), (0,)))
    out_ref[...] = total.astype(BF16)


def combine(gates, acc, picks, back):
    tokens, width = acc.shape
    step = min(512, width)

    def whole(x):
        return pl.BlockSpec(x.shape, lambda d: (0,) * len(x.shape))

    narrow = pl.BlockSpec((tokens, step), lambda d: (0, d))
    return pl.pallas_call(
        combine_kernel,
        name="combine",
        grid=(width // step,),
        in_specs=[
            whole(gates),
            narrow,
            whole(picks),
            VMEM,
        ],
        out_specs=narrow,
        out_shape=jax.ShapeDtypeStruct((tokens, width), BF16),
        compiler_params=params(20),
    )(gates, in_hbm(acc), in_hbm(picks), in_vmem(back))


def batch_columns(meta, expert, local_experts, plan):
    owners = meta.shape[0]
    counts = jnp.where(
        lax.broadcasted_iota(jnp.int32, meta.shape, 1) < local_experts, meta, 0
    ).astype(F32)
    lanes = counts.shape[1]
    row = lax.broadcasted_iota(jnp.int32, (lanes, lanes), 0)
    col = lax.broadcasted_iota(jnp.int32, (lanes, lanes), 1)
    below = jnp.where(row < col, 1.0, 0.0).astype(BF16)
    offsets = contract(counts.astype(BF16), below, ((1,), (0,)))
    batch = owners * CAP
    source_row = lax.broadcasted_iota(jnp.int32, (batch, owners), 0) // CAP
    source_col = lax.broadcasted_iota(jnp.int32, (batch, owners), 1)
    expand = jnp.where(source_row == source_col, 1.0, 0.0).astype(BF16)
    lane = lax.broadcasted_iota(jnp.int32, (batch, lanes), 1)

    def column(values, picked):
        wide = contract(expand, values.astype(BF16), ((1,), (0,)))
        return jnp.sum(jnp.where(picked, wide, 0.0), axis=1, keepdims=True).astype(jnp.int32)

    count = column(counts, lane == expert)
    offset = column(offsets, lane == expert)
    front = column(counts, lane < plan.ahead)
    index = lax.broadcasted_iota(jnp.int32, (batch, 1), 0)
    rank = index % CAP
    valid = rank < count
    place = offset + rank
    back = jnp.where(
        (expert < plan.ahead) & (place < plan.back[0]),
        place,
        plan.back[0] + place - jnp.minimum(front, plan.back[0]),
    )
    return index // CAP, jnp.where(valid, place, -1), jnp.where(valid, back, -1)


def expert_kernel(
    first, taken, given, has_base, local_experts, parts, plan, flag_ref, meta_ref, gain_ref, *refs
):
    x_refs, refs = refs[:len(taken)], refs[len(taken):]
    gate_ref, up_ref, down_ref = refs[:3]
    base_ref = refs[3] if has_base else None
    refs = refs[3 + has_base:]
    out_refs, (batch_ref, acc_ref, done_ref) = refs[:len(given)], refs[len(given):]
    e = pl.program_id(0)
    f = pl.program_id(1)
    last_f = pl.num_programs(1) - 1
    batch = batch_ref.shape[0]
    meta = meta_ref[...]

    @pl.when(f == 0)
    def _():
        source, place, _ = batch_columns(meta, first + e, local_experts, plan)

        context = source // parts
        block = source % parts

        def rows_of(i, k):
            owners, rows, step = x_refs[i].shape
            pieces = x_refs[i][...].reshape(owners // parts, parts, rows, step)
            found = []
            for h in range(parts):
                turn = (h - block + parts) % parts
                spread = one_hot(
                    in_round(place, plan.out, k, context * parts + turn), owners * plan.out[k]
                )
                flat = pieces[:, h].reshape(owners // parts * rows, step)
                found.append(contract(spread, flat, ((1,), (0,))))
            return jnp.concatenate(found, axis=1)

        total = 0.0
        for i, k in enumerate(taken):
            if k < 2:
                total = total + rows_of(i, k)
        acc_ref[...] = total
        for i, k in enumerate(taken):
            if k == 2:

                @pl.when(flag_ref[0] > 0)
                def _():
                    acc_ref[...] = acc_ref[...] + rows_of(i, k)

        stream = acc_ref[...]
        scale = lax.rsqrt(jnp.mean(stream * stream, axis=-1, keepdims=True) + EPS)
        batch_ref[...] = (stream * scale * gain_ref[...]).astype(BF16)

    x = batch_ref[...]
    gate = contract(x, gate_ref[...], ((1,), (0,)))
    upward = contract(x, up_ref[...], ((1,), (0,)))
    hidden = (gate / (1.0 + jnp.exp(-gate)) * upward).astype(BF16)
    part = contract(hidden, down_ref[...], ((1,), (0,)))

    @pl.when(f == 0)
    def _():
        acc_ref[...] = part

    @pl.when((f > 0) & (f < last_f))
    def _():
        acc_ref[...] = acc_ref[...] + part

    @pl.when(f == last_f)
    def _():
        done_ref[e] = (acc_ref[...] + part).astype(BF16)

    @pl.when((e == pl.num_programs(0) - 1) & (f == last_f))
    def _():
        count = done_ref.shape[0]
        columns = [batch_columns(meta, first + i, local_experts, plan) for i in range(count)]
        source = jnp.concatenate([c[0] for c in columns], axis=0)
        back = jnp.concatenate([c[2] for c in columns], axis=0)
        done = done_ref[...].reshape(count * batch, done_ref.shape[2])

        def put(i, k):
            owners, rows, width = out_refs[i].shape
            spread = one_hot(in_round(back, plan.back, k, source), owners * rows)
            rows_out = contract(spread, done, ((0,), (0,)))
            if has_base and k == 1:
                rows_out = rows_out + base_ref[...].reshape(owners * rows, width).astype(F32)
            out_refs[i][...] = rows_out.astype(BF16).reshape(owners, rows, width)

        for i, k in enumerate(given):
            if k < 2:
                put(i, k)
            else:

                @pl.when(flag_ref[0] > 0)
                def _():
                    put(i, k)


def serve_experts(flag, meta, gain, parts, received, weights, base, first, taken, given, plan):
    w_gate, w_up, w_down = weights
    local_experts, width, hidden = w_gate.shape
    owners = meta.shape[0]
    count = plan.ahead
    split = 2
    step = hidden // split

    def whole(x):
        return pl.BlockSpec(x.shape, lambda e, f: (0,) * len(x.shape))

    in_spec = pl.BlockSpec((None, width, step), lambda e, f: (first + e, 0, f))
    extra = [] if base is None else [in_hbm(base)]
    outs = [pltpu.HBM((owners, plan.back[k], width), BF16) for k in given]
    received = [in_vmem(x) if k == 1 else in_hbm(x) for k, x in zip(taken, received)]
    batch = owners * CAP
    return pl.pallas_call(
        functools.partial(
            expert_kernel, first, taken, given, base is not None, local_experts, parts, plan
        ),
        grid=(count, split),
        in_specs=[SMEM, whole(meta), whole(gain)]
        + [whole(x) for x in received]
        + [
            in_spec,
            in_spec,
            pl.BlockSpec((None, step, width), lambda e, f: (first + e, f, 0)),
        ]
        + [whole(x) for x in extra],
        out_specs=[whole(x) for x in outs],
        out_shape=outs,
        scratch_shapes=[
            pltpu.VMEM((batch, width), BF16),
            pltpu.VMEM((batch, width), F32),
            pltpu.VMEM((count, batch, width), BF16),
        ],
        compiler_params=params(44),
    )(flag, meta, gain, *received, w_gate, w_up, w_down, *extra)


def everywhere(x):
    return lax.all_to_all(x, ("ctx", "head"), split_axis=0, concat_axis=0, tiled=True)


def everywhere_if(flag, x):
    return lax.cond(flag[0] > 0, everywhere, lambda y: unset(y.shape), x)


def body_dense(
    queries,
    keys,
    values,
    mem_route,
    head_gain,
    residual_in,
    ffn_gain,
    expert_ids,
    expert_gates,
    w_gate,
    w_up,
    w_down,
):
    length = queries.shape[0]
    ctx_count = lax.axis_size("ctx")
    head_count = lax.axis_size("head")
    owners = ctx_count * head_count
    local_experts = w_gate.shape[0]
    pairs = local_experts // PAIR
    chunks = 2 if pairs % 2 == 0 else 1
    route_row = mem_route.reshape(1, length)
    route_col = mem_route.reshape(length, 1)

    states = block_states(keys, values, route_row)
    pieces = lax.all_to_all(states, "ctx", split_axis=0, concat_axis=0, tiled=True)
    before = exclusive_prefix(pieces.reshape(ctx_count, -1, HD))
    carried = lax.all_to_all(
        before.reshape(states.shape), "ctx", split_axis=0, concat_axis=0, tiled=True
    )
    local = local_attention(queries, keys, values, route_row, route_col)
    normed = mix_and_norm(queries, carried, local, route_col, head_gain[None], head_count)
    by_token = lax.all_to_all(normed, "head", split_axis=0, concat_axis=0, tiled=True)

    stream, parcels = pack_dense(
        residual_in, by_token, ffn_gain[None], expert_ids, chunks, owners, local_experts
    )
    backs = []
    for c in range(chunks):
        received = lax.all_to_all(
            parcels[c], ("ctx", "head"), split_axis=0, concat_axis=0, tiled=True
        )
        served = serve_dense(received, w_gate, w_up, w_down, c)
        backs.append(
            lax.all_to_all(served, ("ctx", "head"), split_axis=0, concat_axis=0, tiled=True)
        )
    return combine_dense(stream, expert_ids, expert_gates, backs, local_experts)


def body_compact(
    queries,
    keys,
    values,
    mem_route,
    head_gain,
    residual_in,
    ffn_gain,
    expert_ids,
    expert_gates,
    w_gate,
    w_up,
    w_down,
):
    length = queries.shape[0]
    contexts = lax.axis_size("ctx")
    parts = lax.axis_size("head")
    local_experts = w_gate.shape[0]
    plan = Plan(local_experts)
    route_row = mem_route.reshape(1, length)
    route_col = mem_route.reshape(length, 1)
    head = lax.axis_index("head").astype(jnp.int32)[None]

    def turned(pieces, step):
        return [pieces[0]] + [
            lax.ppermute(pieces[s], "head", [(h, (h + step * s) % parts) for h in range(parts)])
            for s in range(1, parts)
        ]

    ids = turned([expert_ids.T] * parts, 1)
    states = block_states(keys, values, route_row)
    pieces = lax.all_to_all(states, "ctx", split_axis=0, concat_axis=0, tiled=True)
    counts = count_choices(head, ids, contexts, local_experts, plan)
    before = prefix_with_counts(pieces.reshape(contexts, -1, HD), counts)
    carried = lax.all_to_all(before, "ctx", split_axis=0, concat_axis=0, tiled=True)
    cut = columns_by_turn(head, residual_in, parts)
    residuals = turned(cut, 1)
    code, *spreads = route(ids, contexts, local_experts, plan)
    local = local_attention(queries, keys, values, route_row, route_col)
    meta, flag, parcels, own_streams = mix_and_pack(
        head,
        queries,
        carried,
        counts.shape[1],
        local,
        route_col,
        head_gain[None],
        residuals,
        spreads[0],
        local_experts,
        plan,
    )
    weights = (w_gate, w_up, w_down)
    gain = ffn_gain[None]
    received = [everywhere(parcels)]
    parcels = pack(1, spreads[1], own_streams, contexts * parts, plan)
    received.append(everywhere(parcels))
    streams = turned(own_streams, -1)
    back_0, base = serve_experts(
        flag, meta, gain, parts, received[:1], weights, None, 0, (0,), (0, 1), plan
    )
    received.append(
        lax.cond(
            flag[0] > 0,
            lambda spread, pieces: everywhere(pack(2, spread, pieces, contexts * parts, plan)),
            lambda spread, pieces: unset(
                (contexts * parts, parts * plan.out[2], pieces[0].shape[1])
            ),
            spreads[2],
            own_streams,
        )
    )
    back_0 = everywhere(back_0)
    back_1, back_2 = serve_experts(
        flag, meta, gain, parts, received, weights, base, plan.ahead, (0, 1, 2), (1, 2), plan
    )
    back_2 = everywhere_if(flag, back_2)
    back_1 = everywhere(back_1)
    acc, picks = combine_ahead(head, flag, code, expert_gates, back_0, back_2, streams, plan)
    return combine(expert_gates, acc, picks, back_1)


def body(*args):
    local_experts = args[-1].shape[0]
    compact = local_experts * CAP % (4 * GROUP_ROWS) == 0
    return body_compact(*args) if compact else body_dense(*args)


def solution(mesh):
    placed = (
        P("ctx", "head"),
        P("ctx", "head"),
        P("ctx", "head"),
        P("ctx"),
        P("head"),
        P(("ctx", "head"), None),
        P(),
        P(("ctx", "head"), None),
        P(("ctx", "head"), None),
        P(("ctx", "head"), None, None),
        P(("ctx", "head"), None, None),
        P(("ctx", "head"), None, None),
    )
    return jax.shard_map(
        body, mesh=mesh, in_specs=placed, out_specs=P(("ctx", "head"), None), check_vma=False
    )
```

```python
import functools

import jax
import jax.numpy as jnp
from jax import lax
from jax.experimental import pallas as pl
from jax.experimental.pallas import tpu as pltpu
from jax.sharding import PartitionSpec as P


HD = 128
M = 4
CAP = 4
PAIR = 2
GROUP_ROWS = PAIR * CAP
EPS = 1e-06
F32 = jnp.float32
BF16 = jnp.bfloat16


def params(mebibytes=60):
    return pltpu.CompilerParams(vmem_limit_bytes=mebibytes * 1024 * 1024)


def in_hbm(x):
    return pltpu.with_memory_space_constraint(x, pltpu.HBM)


def in_vmem(x):
    return pltpu.with_memory_space_constraint(x, pltpu.VMEM)


def contract(a, b, dims):
    return lax.dot_general(a, b, (dims, ((), ())), preferred_element_type=F32)


def state_kernel(key_ref, value_ref, route_ref, out_ref):
    route = route_ref[...]
    masks = [(route == m).astype(F32).astype(BF16) for m in range(M)]
    for h in range(key_ref.shape[1] // HD):
        keys_t = key_ref[:, h * HD:(h + 1) * HD].T
        values = value_ref[:, h * HD:(h + 1) * HD]
        for m in range(M):
            found = contract(keys_t * masks[m], values, ((1,), (0,)))
            out_ref[pl.ds((h * M + m) * HD, HD), :] = found.astype(BF16)


def block_states(keys, values, route_row):
    length, width = keys.shape
    heads = width // HD
    together = 2 if heads % 2 == 0 else 1
    return pl.pallas_call(
        state_kernel,
        name="block_states",
        grid=(heads // together,),
        in_specs=[
            pl.BlockSpec((length, together * HD), lambda h: (0, h)),
            pl.BlockSpec((length, together * HD), lambda h: (0, h)),
            pl.BlockSpec((1, length), lambda h: (0, 0)),
        ],
        out_specs=pl.BlockSpec((together * M * HD, HD), lambda h: (h, 0)),
        out_shape=pltpu.HBM((heads * M * HD, HD), BF16),
        compiler_params=params(16),
    )(in_hbm(keys), in_hbm(values), in_hbm(route_row))


def prefix_kernel(ranks, piece_ref, out_ref):
    total = jnp.zeros(piece_ref.shape[1:], F32)
    for r in range(ranks):
        out_ref[r] = total.astype(BF16)
        if r + 1 < ranks:
            total = total + piece_ref[r].astype(F32)


def exclusive_prefix(pieces):
    return pl.pallas_call(
        functools.partial(prefix_kernel, pieces.shape[0]),
        name="exclusive_prefix",
        out_shape=jax.ShapeDtypeStruct(pieces.shape, BF16),
        compiler_params=params(),
    )(pieces)


def local_kernel(rows, query_ref, key_ref, value_ref, route_row_ref, route_col_ref, out_ref, weight_ref):
    length = query_ref.shape[0]

    @pl.when(pl.program_id(0) == 0)
    def _():
        route_row = route_row_ref[...]
        for i in range(length // rows):
            span = (i + 1) * rows
            column = route_col_ref[pl.ds(i * rows, rows), :]
            same = jnp.where(column == route_row[:, :span], 2.0, 1.0)
            t = lax.broadcasted_iota(jnp.int32, (rows, span), 0) + i * rows
            s = lax.broadcasted_iota(jnp.int32, (rows, span), 1)
            weight_ref[pl.ds(i * rows, rows), :span] = jnp.where(t >= s, same, 0.0)

    for i in range(length // rows):
        span = (i + 1) * rows
        query = query_ref[pl.ds(i * rows, rows), :]
        scores = contract(query, key_ref[:span, :], ((1,), (1,)))
        weighted = (scores * weight_ref[pl.ds(i * rows, rows), :span]).astype(BF16)
        out_ref[pl.ds(i * rows, rows), :] = contract(weighted, value_ref[:span, :], ((1,), (0,)))


def local_attention(queries, keys, values, route_row, route_col):
    length, width = queries.shape
    heads = width // HD
    rows = min(256, length)
    wide = pl.BlockSpec((length, HD), lambda h: (0, h))
    return pl.pallas_call(
        functools.partial(local_kernel, rows),
        name="local_attention",
        grid=(heads,),
        in_specs=[
            wide,
            wide,
            wide,
            pl.BlockSpec((1, length), lambda h: (0, 0)),
            pl.BlockSpec((length, 1), lambda h: (0, 0)),
        ],
        out_specs=wide,
        out_shape=jax.ShapeDtypeStruct((length, width), F32),
        scratch_shapes=[pltpu.VMEM((length, length), F32)],
        compiler_params=params(32),
    )(in_hbm(queries), in_hbm(keys), in_hbm(values), route_row, route_col)


def mix_kernel(query_ref, state_ref, local_ref, route_col_ref, gain_ref, out_ref):
    parts, rows, _ = out_ref.shape
    query = query_ref[...]
    column = route_col_ref[...]
    wide = jnp.concatenate(
        [query * jnp.where(column == m, 2.0, 1.0).astype(BF16) for m in range(M)], axis=1
    )
    mixed = contract(wide, state_ref[...], ((1,), (0,))) + local_ref[...]
    scale = lax.rsqrt(jnp.mean(mixed * mixed, axis=-1, keepdims=True) + EPS)
    normed = (mixed * scale * gain_ref[...]).astype(BF16)
    for p in range(parts):
        out_ref[p] = normed[p * rows:(p + 1) * rows]


def mix_and_norm(queries, state, local, route_col, head_gain, parts):
    length, width = queries.shape
    heads = width // HD
    wide = pl.BlockSpec((length, HD), lambda h: (0, h))
    return pl.pallas_call(
        mix_kernel,
        name="mix_and_norm",
        grid=(heads,),
        in_specs=[
            wide,
            pl.BlockSpec((M * HD, HD), lambda h: (h, 0)),
            wide,
            pl.BlockSpec((length, 1), lambda h: (0, 0)),
            pl.BlockSpec((1, HD), lambda h: (0, h)),
        ],
        out_specs=pl.BlockSpec((parts, length // parts, HD), lambda h: (0, 0, h)),
        out_shape=jax.ShapeDtypeStruct((parts, length // parts, width), BF16),
        compiler_params=params(),
    )(queries, state, local, route_col, head_gain)


def slot_columns(ids, experts, local_experts):
    tokens = ids.shape[0]
    owners = experts // local_experts
    lanes = lax.broadcasted_iota(jnp.int32, (tokens, experts), 1)
    chosen = [(ids[:, j:j + 1] == lanes).astype(F32) for j in range(2)]
    t = lax.broadcasted_iota(jnp.int32, (tokens, tokens), 0)
    s = lax.broadcasted_iota(jnp.int32, (tokens, tokens), 1)
    earlier = contract(
        (t > s).astype(F32).astype(BF16), (chosen[0] + chosen[1]).astype(BF16), ((1,), (0,))
    )
    slots = []
    for j in range(2):
        rank = jnp.sum(earlier * chosen[j], axis=1, keepdims=True).astype(jnp.int32)
        expert = ids[:, j:j + 1]
        owner = expert // local_experts
        local = expert % local_experts
        slots.append(
            ((local // PAIR) * owners + owner) * GROUP_ROWS + (local % PAIR) * CAP + rank
        )
    return slots


def pack_dense_kernel(chunks, local_experts, residual_ref, piece_ref, gain_ref, ids_ref, *refs):
    stream_ref, out_refs = refs[0], refs[1:1 + chunks]
    parts, rows, _ = piece_ref.shape
    owners, groups, _, width = out_refs[0].shape
    normed = jnp.concatenate([piece_ref[p] for p in range(parts)], axis=1)
    stream = (residual_ref[...].astype(F32) + normed.astype(F32)).astype(BF16)
    stream_ref[...] = stream
    wide = stream.astype(F32)
    scale = lax.rsqrt(jnp.mean(wide * wide, axis=-1, keepdims=True) + EPS)
    ffn_in = (wide * scale * gain_ref[...]).astype(BF16)
    experts = owners * local_experts
    slot0, slot1 = slot_columns(ids_ref[...], experts, local_experts)
    span = owners * GROUP_ROWS
    for c in range(chunks):
        for g in range(groups):
            base = (c * groups + g) * span
            lanes = lax.broadcasted_iota(jnp.int32, (rows, span), 1) + base
            spread = jnp.where((slot0 == lanes) | (slot1 == lanes), 1.0, 0.0).astype(BF16)
            packed = contract(spread, ffn_in, ((0,), (0,))).astype(BF16)
            out_refs[c][:, g] = packed.reshape(owners, GROUP_ROWS, width)


def pack_dense(residual, pieces, gain, ids, chunks, owners, local_experts):
    tokens, width = residual.shape
    groups = local_experts // PAIR // chunks
    parcel = jax.ShapeDtypeStruct((owners, groups, GROUP_ROWS, width), BF16)
    out = pl.pallas_call(
        functools.partial(pack_dense_kernel, chunks, local_experts),
        name="pack_dense",
        out_shape=[jax.ShapeDtypeStruct((tokens, width), BF16)] + [parcel] * chunks,
        compiler_params=params(),
    )(residual, pieces, gain, ids)
    return out[0], out[1:]


def expert_dense_kernel(x_ref, gate_ref, up_ref, down_ref, out_ref, acc_ref):
    e = pl.program_id(1)
    f = pl.program_id(2)
    owners, rows, width = x_ref.shape
    x = x_ref[...].reshape(owners * rows, width)
    gate = contract(x, gate_ref[...], ((1,), (0,)))
    upward = contract(x, up_ref[...], ((1,), (0,)))
    row = lax.broadcasted_iota(jnp.int32, gate.shape, 0)
    mine = (row // CAP) % PAIR == e
    hidden = gate / (1.0 + jnp.exp(-gate)) * upward
    hidden = jnp.where(mine, hidden, 0.0).astype(BF16)
    part = contract(hidden, down_ref[...], ((1,), (0,)))
    first = (e == 0) & (f == 0)

    @pl.when(first)
    def _():
        acc_ref[...] = part

    @pl.when(jnp.logical_not(first))
    def _():
        acc_ref[...] = acc_ref[...] + part

    @pl.when((e == pl.num_programs(1) - 1) & (f == pl.num_programs(2) - 1))
    def _():
        out_ref[...] = acc_ref[...].astype(BF16).reshape(owners, rows, width)


def serve_dense(received, w_gate, w_up, w_down, chunk):
    owners, groups, rows, width = received.shape
    hidden = w_gate.shape[2]
    split = 2
    step = hidden // split
    first = chunk * groups * PAIR
    token_spec = pl.BlockSpec((owners, None, rows, width), lambda g, e, f: (0, g, 0, 0))
    in_spec = pl.BlockSpec((None, width, step), lambda g, e, f: (first + g * PAIR + e, 0, f))
    return pl.pallas_call(
        expert_dense_kernel,
        grid=(groups, PAIR, split),
        in_specs=[
            token_spec,
            in_spec,
            in_spec,
            pl.BlockSpec((None, step, width), lambda g, e, f: (first + g * PAIR + e, f, 0)),
        ],
        out_specs=token_spec,
        out_shape=jax.ShapeDtypeStruct(received.shape, BF16),
        scratch_shapes=[pltpu.VMEM((owners * rows, width), F32)],
        compiler_params=params(),
    )(received, w_gate, w_up, w_down)


def combine_dense_kernel(chunks, local_experts, stream_ref, ids_ref, gates_ref, *refs):
    back_refs, out_ref, first_ref, second_ref = refs[:chunks], refs[chunks], refs[-2], refs[-1]
    owners, groups, rows, _ = back_refs[0].shape
    span = owners * rows

    @pl.when(pl.program_id(0) == 0)
    def _():
        slot0, slot1 = slot_columns(ids_ref[...], owners * local_experts, local_experts)
        lanes = lax.broadcasted_iota(jnp.int32, first_ref.shape, 1)
        first_ref[...] = jnp.where(slot0 == lanes, 1.0, 0.0).astype(BF16)
        second_ref[...] = jnp.where(slot1 == lanes, 1.0, 0.0).astype(BF16)

    back = jnp.concatenate(
        [
            back_refs[c][:, g].reshape(span, back_refs[c].shape[3])
            for c in range(chunks)
            for g in range(groups)
        ],
        axis=0,
    )
    gates = gates_ref[...]
    total = stream_ref[...].astype(F32)
    total = total + gates[:, 0:1] * contract(first_ref[...], back, ((1,), (0,)))
    total = total + gates[:, 1:2] * contract(second_ref[...], back, ((1,), (0,)))
    out_ref[...] = total.astype(BF16)


def combine_dense(stream, ids, gates, backs, local_experts):
    tokens, width = stream.shape
    owners, groups, rows, _ = backs[0].shape
    chunks = len(backs)
    slots = owners * groups * rows * chunks
    step = min(512, width)
    back_spec = pl.BlockSpec((owners, groups, rows, step), lambda d: (0, 0, 0, d))
    return pl.pallas_call(
        functools.partial(combine_dense_kernel, chunks, local_experts),
        name="combine_dense",
        grid=(width // step,),
        in_specs=[
            pl.BlockSpec((tokens, step), lambda d: (0, d)),
            pl.BlockSpec(ids.shape, lambda d: (0, 0)),
            pl.BlockSpec(gates.shape, lambda d: (0, 0)),
        ]
        + [back_spec] * chunks,
        out_specs=pl.BlockSpec((tokens, step), lambda d: (0, d)),
        out_shape=jax.ShapeDtypeStruct((tokens, width), BF16),
        scratch_shapes=[pltpu.VMEM((tokens, slots), BF16)] * 2,
        compiler_params=params(),
    )(stream, ids, gates, *backs)


class Plan:
    def __init__(self, local_experts):
        dense = local_experts * CAP
        self.ahead = local_experts // 2
        first = self.ahead * CAP
        self.out = (first, first // 2, dense - first - first // 2)
        self.back = (first // 2, first, dense - first - first // 2)


def in_round(place, bounds, k, owner):
    low = sum(bounds[:k])
    inside = (place >= low) & (place < low + bounds[k])
    return jnp.where(inside, owner * bounds[k] + place - low, -1)


def one_hot(column, width):
    lanes = lax.broadcasted_iota(jnp.int32, (column.shape[0], width), 1)
    return jnp.where(column == lanes, 1.0, 0.0).astype(BF16)


VMEM = pl.BlockSpec(memory_space=pltpu.VMEM)
SMEM = pl.BlockSpec(memory_space=pltpu.SMEM)


def id_columns(id_refs):
    parts = len(id_refs)
    pad = -2 * parts % 8
    rows = [ref[...].astype(F32) for ref in id_refs]
    if pad:
        rows.append(jnp.zeros((pad, id_refs[0].shape[1]), F32))
    rows = jnp.concatenate(rows, axis=0)
    return rows, rows.T


def counts_kernel(local_experts, plan, parts, head_ref, *refs):
    id_refs, meta_ref = refs[:parts], refs[parts]
    tokens = id_refs[0].shape[1]
    contexts = meta_ref.shape[0]
    owners = contexts * parts
    head = head_ref[0]
    owner_lane = lax.broadcasted_iota(jnp.int32, (tokens, owners), 1)
    local_lane = lax.broadcasted_iota(jnp.int32, (tokens, HD), 1)
    owner_row = lax.broadcasted_iota(jnp.int32, (contexts, owners), 1)
    context_row = lax.broadcasted_iota(jnp.int32, (contexts, owners), 0)
    mine = jnp.where(owner_row == context_row * parts + head, 1.0, 0.0).astype(BF16)
    lane = lax.broadcasted_iota(jnp.int32, (owners, HD), 1)
    _, id_cols = id_columns(id_refs)
    flags = 0.0
    metas = []
    for b in range(parts):
        counts = 0.0
        for j in range(2):
            ids = id_cols[:, 2 * b + j:2 * b + j + 1].astype(jnp.int32)
            counts = counts + contract(
                (ids // local_experts == owner_lane).astype(F32).astype(BF16),
                (ids % local_experts == local_lane).astype(F32).astype(BF16),
                ((0,), (0,)),
            )
        total = jnp.sum(counts, axis=1, keepdims=True)
        front = jnp.sum(jnp.where(lane < plan.ahead, counts, 0.0), axis=1, keepdims=True)
        over = (total > sum(plan.out[:2])) | (
            total - jnp.minimum(front, plan.back[0]) > plan.back[1]
        )
        flags = jnp.maximum(flags, jnp.max(jnp.where(over, 1.0, 0.0), axis=0, keepdims=True))
        metas.append(contract(mine, counts.astype(BF16), ((1,), (0,))))
    meta_lane = lax.broadcasted_iota(jnp.int32, (contexts, HD), 1)
    meta_ref[...] = jnp.zeros(meta_ref.shape, F32)
    for b in range(parts):
        marked = jnp.where(meta_lane == local_experts, flags, metas[b])
        for c in range(contexts):
            meta_ref[c, b:b + 1, :] = marked[c:c + 1]


def count_choices(head, ids, contexts, local_experts, plan):
    parts = len(ids)
    return pl.pallas_call(
        functools.partial(counts_kernel, local_experts, plan, parts),
        name="count_choices",
        in_specs=[SMEM] + [VMEM] * parts,
        out_specs=VMEM,
        out_shape=jax.ShapeDtypeStruct((contexts, parts + -parts % 8, HD), F32),
        compiler_params=params(16),
    )(head, *ids)


def route_kernel(local_experts, experts, plan, parts, *refs):
    id_refs, code_ref, spread_refs = refs[:parts], refs[parts], refs[parts + 1:]
    tokens = id_refs[0].shape[1]
    t = lax.broadcasted_iota(jnp.int32, (tokens, tokens), 0)
    s = lax.broadcasted_iota(jnp.int32, (tokens, tokens), 1)
    earlier_mask = (t > s).astype(F32).astype(BF16)
    row = lax.broadcasted_iota(jnp.int32, (experts, experts), 0)
    col = lax.broadcasted_iota(jnp.int32, (experts, experts), 1)
    mates = row // local_experts == col // local_experts
    below = jnp.where(mates & (row < col), 1.0, 0.0).astype(BF16)
    ahead = jnp.where(mates & (row % local_experts < plan.ahead), 1.0, 0.0).astype(BF16)
    lanes = lax.broadcasted_iota(jnp.int32, (tokens, experts), 1)
    id_rows, id_cols = id_columns(id_refs)
    for b in range(parts):
        ids = [id_cols[:, 2 * b + j:2 * b + j + 1].astype(jnp.int32) for j in range(2)]
        chosen = [(i == lanes).astype(F32) for i in ids]
        both = (chosen[0] + chosen[1]).astype(BF16)
        counts = contract(jnp.ones((8, tokens), BF16), both, ((1,), (0,))).astype(BF16)
        position = contract(earlier_mask, both, ((1,), (0,))) + contract(counts, below, ((1,), (0,)))[0:1]
        places = [jnp.sum(position * c, axis=1, keepdims=True) for c in chosen]
        wide = jnp.concatenate(places + [jnp.zeros((tokens, HD - 2), F32)], axis=1)
        place_rows = wide.T[0:8]
        if b == 0:
            aheads = contract(counts, ahead, ((1,), (0,)))[0:1]
            slot_lane = lax.broadcasted_iota(jnp.int32, code_ref.shape, 1)
            code = jnp.zeros(code_ref.shape, jnp.int32)
            for j in range(2):
                place = places[j].astype(jnp.int32)
                front = jnp.sum(aheads * chosen[j], axis=1, keepdims=True).astype(jnp.int32)
                back = jnp.where(
                    (ids[j] % local_experts < plan.ahead) & (place < plan.back[0]),
                    place,
                    plan.back[0] + place - jnp.minimum(front, plan.back[0]),
                )
                code = jnp.where(slot_lane == j, ids[j] // local_experts, code)
                code = jnp.where(slot_lane == 4 + j, back, code)
            code_ref[...] = code
        for k, spread_ref in enumerate(spread_refs):
            slots = spread_ref.shape[1]
            slot = lax.broadcasted_iota(jnp.int32, (slots, tokens), 0)
            hit = None
            for j in range(2):
                owner = id_rows[2 * b + j:2 * b + j + 1].astype(jnp.int32) // local_experts
                index = in_round(place_rows[j:j + 1].astype(jnp.int32), plan.out, k, owner)
                hit = (slot == index) if hit is None else hit | (slot == index)
            spread_ref[b] = jnp.where(hit, 1.0, 0.0).astype(BF16)


def route(ids, contexts, local_experts, plan):
    parts = len(ids)
    tokens = ids[0].shape[1]
    owners = contexts * parts
    return pl.pallas_call(
        functools.partial(route_kernel, local_experts, owners * local_experts, plan, parts),
        name="route",
        in_specs=[VMEM] * parts,
        out_specs=[VMEM] * 4,
        out_shape=[pltpu.HBM((tokens, HD), jnp.int32)]
        + [pltpu.HBM((parts, owners * rows, tokens), BF16) for rows in plan.out],
        compiler_params=params(24),
    )(*ids)


def prefix_with_counts_kernel(piece_ref, meta_ref, out_ref):
    ranks, rows, _ = piece_ref.shape
    total = jnp.zeros(piece_ref.shape[1:], F32)
    for r in range(ranks):
        out_ref[r, :rows, :] = total.astype(BF16)
        out_ref[r, rows:, :] = meta_ref[r].astype(BF16)
        if r + 1 < ranks:
            total = total + piece_ref[r].astype(F32)


def prefix_with_counts(pieces, meta):
    ranks, rows, width = pieces.shape
    return pl.pallas_call(
        prefix_with_counts_kernel,
        name="prefix_with_counts",
        in_specs=[VMEM] * 2,
        out_specs=VMEM,
        out_shape=pltpu.HBM((ranks, rows + meta.shape[1], width), BF16),
        compiler_params=params(12),
    )(pieces, meta)


def columns_kernel(parts, head_ref, whole_ref, *out_refs):
    step = whole_ref.shape[1] // parts
    for s in range(parts):
        start = pl.multiple_of((head_ref[0] + s) % parts * step, step)
        out_refs[s][...] = whole_ref[:, pl.ds(start, step)]


def columns_by_turn(head, whole, parts):
    tokens, width = whole.shape
    return pl.pallas_call(
        functools.partial(columns_kernel, parts),
        name="columns_by_turn",
        in_specs=[SMEM, VMEM],
        out_specs=[VMEM] * parts,
        out_shape=[pltpu.HBM((tokens, width // parts), BF16)] * parts,
        compiler_params=params(12),
    )(head, whole)


def mix_pack_kernel(
    parts, local_experts, plan, head_ref, query_ref, state_ref, tail_ref, local_ref, route_col_ref, gain_ref, *refs
):
    residual_refs, spread_ref = refs[:parts], refs[parts]
    refs = refs[parts + 1:]
    meta_ref, flag_ref, parcel_ref, stream_refs = refs[0], refs[1], refs[2], refs[3:3 + parts]
    normed_ref = refs[-1]
    head = head_ref[0]
    pieces, rows, _ = state_ref.shape
    contexts, tail, _ = tail_ref.shape
    rows -= tail
    width = query_ref.shape[1]
    together = width // HD
    share = pieces // together
    column = route_col_ref[...]
    doubled = [jnp.where(column == m, 2.0, 1.0).astype(BF16) for m in range(M)]
    for g in range(together):
        span = slice(g * HD, (g + 1) * HD)
        query = query_ref[:, span]
        wide = jnp.concatenate([query * weight for weight in doubled], axis=1)
        state = jnp.concatenate([state_ref[g * share + i, :rows, :] for i in range(share)], axis=0)
        mixed = contract(wide, state, ((1,), (0,))) + local_ref[:, span]
        scale = lax.rsqrt(jnp.mean(mixed * mixed, axis=-1, keepdims=True) + EPS)
        normed_ref[:, span] = (mixed * scale * gain_ref[:, span]).astype(BF16)

    @pl.when(pl.program_id(0) == 0)
    def _():
        counts = tail_ref[...].astype(F32)
        owners = contexts * parts
        lane = lax.broadcasted_iota(jnp.int32, counts.shape, 2)
        over = jnp.max(jnp.where(lane == local_experts, counts, 0.0))
        flag_ref[0] = (over > 0.5).astype(jnp.int32)
        source = lax.broadcasted_iota(jnp.int32, (owners, contexts * tail), 0)
        given = lax.broadcasted_iota(jnp.int32, (owners, contexts * tail), 1)
        turn = (head - source % parts + parts) % parts
        order = jnp.where(given == source // parts * tail + turn, 1.0, 0.0).astype(BF16)
        flat = counts.reshape(contexts * tail, counts.shape[2]).astype(BF16)
        meta_ref[...] = contract(order, flat, ((1,), (0,))).astype(jnp.int32)

    tokens = residual_refs[0].shape[0]
    for s in range(parts):
        start = pl.multiple_of((head - s + parts) % parts * tokens, tokens)
        normed = normed_ref[pl.ds(start, tokens), :]
        stream = (residual_refs[s][...].astype(F32) + normed.astype(F32)).astype(BF16)
        stream_refs[s][...] = stream
        put_parcels(plan.out[0], s, spread_ref[s], stream, parcel_ref)


def put_parcels(each, s, spread, stream, parcel_ref):
    owners, _, width = parcel_ref.shape
    packed = contract(spread, stream, ((1,), (0,))).astype(BF16)
    parcel_ref[:, s * each:(s + 1) * each, :] = packed.reshape(owners, each, width)


def mix_and_pack(head, queries, carried, tail, local, route_col, head_gain, residuals, spread, local_experts, plan):
    length, width = queries.shape
    heads = width // HD
    together = 2 if heads % 2 == 0 else 1
    step = together * HD
    contexts, rows, _ = carried.shape
    share = contexts * together // heads
    parts = len(residuals)
    tokens = length // parts
    owners = contexts * parts
    wide = pl.BlockSpec((length, step), lambda h: (0, h))
    narrow = pl.BlockSpec((tokens, step), lambda h: (0, h))

    def whole(x):
        return pl.BlockSpec(x.shape, lambda h: (0,) * len(x.shape))

    each = parts * plan.out[0]
    meta = pltpu.HBM((owners, HD), jnp.int32)
    out = pl.pallas_call(
        functools.partial(mix_pack_kernel, parts, local_experts, plan),
        name="mix_and_pack",
        grid=(heads // together,),
        in_specs=[
            SMEM,
            wide,
            pl.BlockSpec((share, rows, HD), lambda h: (h, 0, 0)),
            pl.BlockSpec((contexts, tail, HD), lambda h: (0, (rows - tail) // tail, 0)),
            wide,
            pl.BlockSpec((length, 1), lambda h: (0, 0)),
            pl.BlockSpec((1, step), lambda h: (0, h)),
        ]
        + [narrow] * parts
        + [whole(spread)],
        out_specs=[whole(meta), SMEM, pl.BlockSpec((owners, each, step), lambda h: (0, 0, h))]
        + [narrow] * parts,
        out_shape=[
            meta,
            jax.ShapeDtypeStruct((1,), jnp.int32),
            pltpu.HBM((owners, each, width), BF16),
        ]
        + [pltpu.HBM((tokens, width), BF16)] * parts,
        scratch_shapes=[pltpu.VMEM((length, step), BF16)],
        compiler_params=params(32),
    )(
        head,
        in_hbm(queries),
        carried,
        carried,
        local,
        route_col,
        head_gain,
        *map(in_hbm, residuals),
        in_hbm(spread),
    )
    return out[0], out[1], out[2], out[3:]


def pack_kernel(each, spread_ref, *refs):
    for s, stream_ref in enumerate(refs[:-1]):
        put_parcels(each, s, spread_ref[s], stream_ref[...], refs[-1])


def pack(k, spread, streams, owners, plan):
    each = plan.out[k]
    shape = (owners, len(streams) * each, streams[0].shape[1])
    return pl.pallas_call(
        functools.partial(pack_kernel, each),
        in_specs=[VMEM] * (1 + len(streams)),
        out_specs=VMEM,
        out_shape=pltpu.HBM(shape, BF16),
        compiler_params=params(24),
    )(in_hbm(spread), *map(in_hbm, streams))


def unset_kernel(out_ref):
    pass


def unset(shape):
    return pl.pallas_call(
        unset_kernel,
        name="unset",
        out_specs=pl.BlockSpec(memory_space=pl.ANY),
        out_shape=pltpu.HBM(shape, BF16),
        compiler_params=params(4),
    )()


def gated(gates, spreads, back):
    total = 0.0
    for j, spread in enumerate(spreads):
        total = total + gates[:, j:j + 1] * contract(spread, back, ((1,), (0,)))
    return total


def choices(code, plan, k, owners):
    return [
        one_hot(in_round(code[:, 4 + j:5 + j], plan.back, k, code[:, j:j + 1]), owners * plan.back[k])
        for j in range(2)
    ]


def combine_ahead_kernel(plan, parts, head_ref, flag_ref, code_ref, gates_ref, back_ref, late_ref, *refs):
    stream_refs, (acc_ref, pick_ref) = refs[:parts], refs[parts:]
    code = code_ref[...]
    owners, rows, width = back_ref.shape
    flat = back_ref[...].reshape(owners * rows, width)
    acc_ref[...] = gated(gates_ref[...], choices(code, plan, 0, owners), flat)
    step = width // parts
    for s in range(parts):
        start = pl.multiple_of((head_ref[0] + s) % parts * step, step)
        acc_ref[:, pl.ds(start, step)] = acc_ref[:, pl.ds(start, step)] + stream_refs[s][...].astype(F32)
    for j, spread in enumerate(choices(code, plan, 1, owners)):
        pick_ref[j] = spread

    @pl.when(flag_ref[0] > 0)
    def _():
        late = late_ref[...].reshape(owners * plan.back[2], width)
        acc_ref[...] = acc_ref[...] + gated(gates_ref[...], choices(code, plan, 2, owners), late)


def combine_ahead(head, flag, code, gates, back, late, streams, plan):
    owners, _, width = back.shape
    tokens = code.shape[0]
    return pl.pallas_call(
        functools.partial(combine_ahead_kernel, plan, len(streams)),
        name="combine_ahead",
        in_specs=[SMEM] * 2 + [VMEM] * (4 + len(streams)),
        out_specs=[VMEM] * 2,
        out_shape=[
            pltpu.HBM((tokens, width), F32),
            pltpu.HBM((2, tokens, owners * plan.back[1]), BF16),
        ],
        compiler_params=params(28),
    )(head, flag, code, gates, back, late, *streams)


def combine_kernel(gates_ref, acc_ref, pick_ref, back_ref, out_ref):
    owners, rows, _ = back_ref.shape
    step = out_ref.shape[1]
    start = pl.multiple_of(pl.program_id(0) * step, step)
    flat = back_ref[:, :, pl.ds(start, step)].reshape(owners * rows, step)
    total = acc_ref[...]
    for j in range(2):
        total = total + gates_ref[:, j:j + 1] * contract(pick_ref[j], flat, ((1,), (0,)))
    out_ref[...] = total.astype(BF16)


def combine(gates, acc, picks, back):
    tokens, width = acc.shape
    step = min(1024, width)

    def whole(x):
        return pl.BlockSpec(x.shape, lambda d: (0,) * len(x.shape))

    narrow = pl.BlockSpec((tokens, step), lambda d: (0, d))
    return pl.pallas_call(
        combine_kernel,
        name="combine",
        grid=(width // step,),
        in_specs=[
            whole(gates),
            narrow,
            whole(picks),
            VMEM,
        ],
        out_specs=narrow,
        out_shape=jax.ShapeDtypeStruct((tokens, width), BF16),
        compiler_params=params(20),
    )(gates, in_hbm(acc), in_hbm(picks), in_vmem(back))


def batch_columns(meta, expert, local_experts, plan):
    owners = meta.shape[0]
    counts = jnp.where(
        lax.broadcasted_iota(jnp.int32, meta.shape, 1) < local_experts, meta, 0
    ).astype(F32)
    lanes = counts.shape[1]
    row = lax.broadcasted_iota(jnp.int32, (lanes, lanes), 0)
    col = lax.broadcasted_iota(jnp.int32, (lanes, lanes), 1)
    below = jnp.where(row < col, 1.0, 0.0).astype(BF16)
    offsets = contract(counts.astype(BF16), below, ((1,), (0,)))
    batch = owners * CAP
    source_row = lax.broadcasted_iota(jnp.int32, (batch, owners), 0) // CAP
    source_col = lax.broadcasted_iota(jnp.int32, (batch, owners), 1)
    expand = jnp.where(source_row == source_col, 1.0, 0.0).astype(BF16)
    lane = lax.broadcasted_iota(jnp.int32, (batch, lanes), 1)

    def column(values, picked):
        wide = contract(expand, values.astype(BF16), ((1,), (0,)))
        return jnp.sum(jnp.where(picked, wide, 0.0), axis=1, keepdims=True).astype(jnp.int32)

    count = column(counts, lane == expert)
    offset = column(offsets, lane == expert)
    front = column(counts, lane < plan.ahead)
    index = lax.broadcasted_iota(jnp.int32, (batch, 1), 0)
    rank = index % CAP
    valid = rank < count
    place = offset + rank
    back = jnp.where(
        (expert < plan.ahead) & (place < plan.back[0]),
        place,
        plan.back[0] + place - jnp.minimum(front, plan.back[0]),
    )
    return index // CAP, jnp.where(valid, place, -1), jnp.where(valid, back, -1)


def expert_kernel(
    first, taken, given, has_base, local_experts, parts, plan, flag_ref, meta_ref, gain_ref, *refs
):
    x_refs, refs = refs[:len(taken)], refs[len(taken):]
    gate_ref, up_ref, down_ref = refs[:3]
    base_ref = refs[3] if has_base else None
    refs = refs[3 + has_base:]
    out_refs, (batch_ref, acc_ref, done_ref) = refs[:len(given)], refs[len(given):]
    e = pl.program_id(0)
    f = pl.program_id(1)
    last_f = pl.num_programs(1) - 1
    batch = batch_ref.shape[0]
    meta = meta_ref[...]

    @pl.when(f == 0)
    def _():
        source, place, _ = batch_columns(meta, first + e, local_experts, plan)

        context = source // parts
        block = source % parts

        def rows_of(i, k):
            owners, rows, step = x_refs[i].shape
            pieces = x_refs[i][...].reshape(owners // parts, parts, rows, step)
            found = []
            for h in range(parts):
                turn = (h - block + parts) % parts
                spread = one_hot(
                    in_round(place, plan.out, k, context * parts + turn), owners * plan.out[k]
                )
                flat = pieces[:, h].reshape(owners // parts * rows, step)
                found.append(contract(spread, flat, ((1,), (0,))))
            return jnp.concatenate(found, axis=1)

        total = 0.0
        for i, k in enumerate(taken):
            if k < 2:
                total = total + rows_of(i, k)
        acc_ref[...] = total
        for i, k in enumerate(taken):
            if k == 2:

                @pl.when(flag_ref[0] > 0)
                def _():
                    acc_ref[...] = acc_ref[...] + rows_of(i, k)

        stream = acc_ref[...]
        scale = lax.rsqrt(jnp.mean(stream * stream, axis=-1, keepdims=True) + EPS)
        batch_ref[...] = (stream * scale * gain_ref[...]).astype(BF16)

    x = batch_ref[...]
    gate = contract(x, gate_ref[...], ((1,), (0,)))
    upward = contract(x, up_ref[...], ((1,), (0,)))
    hidden = (gate / (1.0 + jnp.exp(-gate)) * upward).astype(BF16)
    part = contract(hidden, down_ref[...], ((1,), (0,)))

    @pl.when(f == 0)
    def _():
        acc_ref[...] = part

    @pl.when((f > 0) & (f < last_f))
    def _():
        acc_ref[...] = acc_ref[...] + part

    @pl.when(f == last_f)
    def _():
        done_ref[e] = (acc_ref[...] + part).astype(BF16)

    @pl.when((e == pl.num_programs(0) - 1) & (f == last_f))
    def _():
        count = done_ref.shape[0]
        columns = [batch_columns(meta, first + i, local_experts, plan) for i in range(count)]
        source = jnp.concatenate([c[0] for c in columns], axis=0)
        back = jnp.concatenate([c[2] for c in columns], axis=0)
        done = done_ref[...].reshape(count * batch, done_ref.shape[2])

        def put(i, k):
            owners, rows, width = out_refs[i].shape
            spread = one_hot(in_round(back, plan.back, k, source), owners * rows)
            rows_out = contract(spread, done, ((0,), (0,)))
            if has_base and k == 1:
                rows_out = rows_out + base_ref[...].reshape(owners * rows, width).astype(F32)
            out_refs[i][...] = rows_out.astype(BF16).reshape(owners, rows, width)

        for i, k in enumerate(given):
            if k < 2:
                put(i, k)
            else:

                @pl.when(flag_ref[0] > 0)
                def _():
                    put(i, k)


def serve_experts(flag, meta, gain, parts, received, weights, base, first, taken, given, plan):
    w_gate, w_up, w_down = weights
    local_experts, width, hidden = w_gate.shape
    owners = meta.shape[0]
    count = plan.ahead
    split = 2
    step = hidden // split

    def whole(x):
        return pl.BlockSpec(x.shape, lambda e, f: (0,) * len(x.shape))

    in_spec = pl.BlockSpec((None, width, step), lambda e, f: (first + e, 0, f))
    extra = [] if base is None else [in_hbm(base)]
    outs = [pltpu.HBM((owners, plan.back[k], width), BF16) for k in given]
    received = [in_vmem(x) if k == 1 else in_hbm(x) for k, x in zip(taken, received)]
    batch = owners * CAP
    return pl.pallas_call(
        functools.partial(
            expert_kernel, first, taken, given, base is not None, local_experts, parts, plan
        ),
        grid=(count, split),
        in_specs=[SMEM, whole(meta), whole(gain)]
        + [whole(x) for x in received]
        + [
            in_spec,
            in_spec,
            pl.BlockSpec((None, step, width), lambda e, f: (first + e, f, 0)),
        ]
        + [whole(x) for x in extra],
        out_specs=[whole(x) for x in outs],
        out_shape=outs,
        scratch_shapes=[
            pltpu.VMEM((batch, width), BF16),
            pltpu.VMEM((batch, width), F32),
            pltpu.VMEM((count, batch, width), BF16),
        ],
        compiler_params=params(44),
    )(flag, meta, gain, *received, w_gate, w_up, w_down, *extra)


def everywhere(x):
    return lax.all_to_all(x, ("ctx", "head"), split_axis=0, concat_axis=0, tiled=True)


def everywhere_if(flag, x):
    return lax.cond(flag[0] > 0, everywhere, lambda y: unset(y.shape), x)


def body_dense(
    queries,
    keys,
    values,
    mem_route,
    head_gain,
    residual_in,
    ffn_gain,
    expert_ids,
    expert_gates,
    w_gate,
    w_up,
    w_down,
):
    length = queries.shape[0]
    ctx_count = lax.axis_size("ctx")
    head_count = lax.axis_size("head")
    owners = ctx_count * head_count
    local_experts = w_gate.shape[0]
    pairs = local_experts // PAIR
    chunks = 2 if pairs % 2 == 0 else 1
    route_row = mem_route.reshape(1, length)
    route_col = mem_route.reshape(length, 1)

    states = block_states(keys, values, route_row)
    pieces = lax.all_to_all(states, "ctx", split_axis=0, concat_axis=0, tiled=True)
    before = exclusive_prefix(pieces.reshape(ctx_count, -1, HD))
    carried = lax.all_to_all(
        before.reshape(states.shape), "ctx", split_axis=0, concat_axis=0, tiled=True
    )
    local = local_attention(queries, keys, values, route_row, route_col)
    normed = mix_and_norm(queries, carried, local, route_col, head_gain[None], head_count)
    by_token = lax.all_to_all(normed, "head", split_axis=0, concat_axis=0, tiled=True)

    stream, parcels = pack_dense(
        residual_in, by_token, ffn_gain[None], expert_ids, chunks, owners, local_experts
    )
    backs = []
    for c in range(chunks):
        received = lax.all_to_all(
            parcels[c], ("ctx", "head"), split_axis=0, concat_axis=0, tiled=True
        )
        served = serve_dense(received, w_gate, w_up, w_down, c)
        backs.append(
            lax.all_to_all(served, ("ctx", "head"), split_axis=0, concat_axis=0, tiled=True)
        )
    return combine_dense(stream, expert_ids, expert_gates, backs, local_experts)


def body_compact(
    queries,
    keys,
    values,
    mem_route,
    head_gain,
    residual_in,
    ffn_gain,
    expert_ids,
    expert_gates,
    w_gate,
    w_up,
    w_down,
):
    length = queries.shape[0]
    contexts = lax.axis_size("ctx")
    parts = lax.axis_size("head")
    local_experts = w_gate.shape[0]
    plan = Plan(local_experts)
    route_row = mem_route.reshape(1, length)
    route_col = mem_route.reshape(length, 1)
    head = lax.axis_index("head").astype(jnp.int32)[None]

    def turned(pieces, step):
        return [pieces[0]] + [
            lax.ppermute(pieces[s], "head", [(h, (h + step * s) % parts) for h in range(parts)])
            for s in range(1, parts)
        ]

    ids = turned([expert_ids.T] * parts, 1)
    states = block_states(keys, values, route_row)
    pieces = lax.all_to_all(states, "ctx", split_axis=0, concat_axis=0, tiled=True)
    counts = count_choices(head, ids, contexts, local_experts, plan)
    before = prefix_with_counts(pieces.reshape(contexts, -1, HD), counts)
    carried = lax.all_to_all(before, "ctx", split_axis=0, concat_axis=0, tiled=True)
    cut = columns_by_turn(head, residual_in, parts)
    residuals = turned(cut, 1)
    code, *spreads = route(ids, contexts, local_experts, plan)
    local = local_attention(queries, keys, values, route_row, route_col)
    meta, flag, parcels, own_streams = mix_and_pack(
        head,
        queries,
        carried,
        counts.shape[1],
        local,
        route_col,
        head_gain[None],
        residuals,
        spreads[0],
        local_experts,
        plan,
    )
    weights = (w_gate, w_up, w_down)
    gain = ffn_gain[None]
    received = [everywhere(parcels)]
    parcels = pack(1, spreads[1], own_streams, contexts * parts, plan)
    received.append(everywhere(parcels))
    streams = turned(own_streams, -1)
    back_0, base = serve_experts(
        flag, meta, gain, parts, received[:1], weights, None, 0, (0,), (0, 1), plan
    )
    received.append(
        lax.cond(
            flag[0] > 0,
            lambda spread, pieces: everywhere(pack(2, spread, pieces, contexts * parts, plan)),
            lambda spread, pieces: unset(
                (contexts * parts, parts * plan.out[2], pieces[0].shape[1])
            ),
            spreads[2],
            own_streams,
        )
    )
    back_0 = everywhere(back_0)
    back_1, back_2 = serve_experts(
        flag, meta, gain, parts, received, weights, base, plan.ahead, (0, 1, 2), (1, 2), plan
    )
    back_2 = everywhere_if(flag, back_2)
    back_1 = everywhere(back_1)
    acc, picks = combine_ahead(head, flag, code, expert_gates, back_0, back_2, streams, plan)
    return combine(expert_gates, acc, picks, back_1)


def body(*args):
    local_experts = args[-1].shape[0]
    compact = local_experts * CAP % (4 * GROUP_ROWS) == 0
    return body_compact(*args) if compact else body_dense(*args)


def solution(mesh):
    placed = (
        P("ctx", "head"),
        P("ctx", "head"),
        P("ctx", "head"),
        P("ctx"),
        P("head"),
        P(("ctx", "head"), None),
        P(),
        P(("ctx", "head"), None),
        P(("ctx", "head"), None),
        P(("ctx", "head"), None, None),
        P(("ctx", "head"), None, None),
        P(("ctx", "head"), None, None),
    )
    return jax.shard_map(
        body, mesh=mesh, in_specs=placed, out_specs=P(("ctx", "head"), None), check_vma=False
    )
```

```python
import functools

import jax
import jax.numpy as jnp
from jax import lax
from jax.experimental import pallas as pl
from jax.experimental.pallas import tpu as pltpu
from jax.sharding import PartitionSpec as P


HD = 128
M = 4
CAP = 4
PAIR = 2
GROUP_ROWS = PAIR * CAP
EPS = 1e-06
F32 = jnp.float32
BF16 = jnp.bfloat16


def params(mebibytes=60):
    return pltpu.CompilerParams(vmem_limit_bytes=mebibytes * 1024 * 1024)


def in_hbm(x):
    return pltpu.with_memory_space_constraint(x, pltpu.HBM)


def in_vmem(x):
    return pltpu.with_memory_space_constraint(x, pltpu.VMEM)


def contract(a, b, dims):
    return lax.dot_general(a, b, (dims, ((), ())), preferred_element_type=F32)


def state_kernel(key_ref, value_ref, route_ref, out_ref):
    route = route_ref[...]
    masks = [(route == m).astype(F32).astype(BF16) for m in range(M)]
    for h in range(key_ref.shape[1] // HD):
        keys_t = key_ref[:, h * HD:(h + 1) * HD].T
        values = value_ref[:, h * HD:(h + 1) * HD]
        for m in range(M):
            found = contract(keys_t * masks[m], values, ((1,), (0,)))
            out_ref[pl.ds((h * M + m) * HD, HD), :] = found.astype(BF16)


def block_states(keys, values, route_row):
    length, width = keys.shape
    heads = width // HD
    together = 2 if heads % 2 == 0 else 1
    return pl.pallas_call(
        state_kernel,
        name="block_states",
        grid=(heads // together,),
        in_specs=[
            pl.BlockSpec((length, together * HD), lambda h: (0, h)),
            pl.BlockSpec((length, together * HD), lambda h: (0, h)),
            pl.BlockSpec((1, length), lambda h: (0, 0)),
        ],
        out_specs=pl.BlockSpec((together * M * HD, HD), lambda h: (h, 0)),
        out_shape=pltpu.HBM((heads * M * HD, HD), BF16),
        compiler_params=params(16),
    )(in_hbm(keys), in_hbm(values), in_hbm(route_row))


def prefix_kernel(ranks, piece_ref, out_ref):
    total = jnp.zeros(piece_ref.shape[1:], F32)
    for r in range(ranks):
        out_ref[r] = total.astype(BF16)
        if r + 1 < ranks:
            total = total + piece_ref[r].astype(F32)


def exclusive_prefix(pieces):
    return pl.pallas_call(
        functools.partial(prefix_kernel, pieces.shape[0]),
        name="exclusive_prefix",
        out_shape=jax.ShapeDtypeStruct(pieces.shape, BF16),
        compiler_params=params(),
    )(pieces)


def local_kernel(rows, query_ref, key_ref, value_ref, route_row_ref, route_col_ref, out_ref, weight_ref):
    length = query_ref.shape[0]

    @pl.when(pl.program_id(0) == 0)
    def _():
        route_row = route_row_ref[...]
        for i in range(length // rows):
            span = (i + 1) * rows
            column = route_col_ref[pl.ds(i * rows, rows), :]
            same = jnp.where(column == route_row[:, :span], 2.0, 1.0)
            t = lax.broadcasted_iota(jnp.int32, (rows, span), 0) + i * rows
            s = lax.broadcasted_iota(jnp.int32, (rows, span), 1)
            weight_ref[pl.ds(i * rows, rows), :span] = jnp.where(t >= s, same, 0.0)

    for i in range(length // rows):
        span = (i + 1) * rows
        query = query_ref[pl.ds(i * rows, rows), :]
        scores = contract(query, key_ref[:span, :], ((1,), (1,)))
        weighted = (scores * weight_ref[pl.ds(i * rows, rows), :span]).astype(BF16)
        out_ref[pl.ds(i * rows, rows), :] = contract(weighted, value_ref[:span, :], ((1,), (0,)))


def local_attention(queries, keys, values, route_row, route_col):
    length, width = queries.shape
    heads = width // HD
    rows = min(256, length)
    wide = pl.BlockSpec((length, HD), lambda h: (0, h))
    return pl.pallas_call(
        functools.partial(local_kernel, rows),
        name="local_attention",
        grid=(heads,),
        in_specs=[
            wide,
            wide,
            wide,
            pl.BlockSpec((1, length), lambda h: (0, 0)),
            pl.BlockSpec((length, 1), lambda h: (0, 0)),
        ],
        out_specs=wide,
        out_shape=jax.ShapeDtypeStruct((length, width), F32),
        scratch_shapes=[pltpu.VMEM((length, length), F32)],
        compiler_params=params(32),
    )(in_hbm(queries), in_hbm(keys), in_hbm(values), route_row, route_col)


def mix_kernel(query_ref, state_ref, local_ref, route_col_ref, gain_ref, out_ref):
    parts, rows, _ = out_ref.shape
    query = query_ref[...]
    column = route_col_ref[...]
    wide = jnp.concatenate(
        [query * jnp.where(column == m, 2.0, 1.0).astype(BF16) for m in range(M)], axis=1
    )
    mixed = contract(wide, state_ref[...], ((1,), (0,))) + local_ref[...]
    scale = lax.rsqrt(jnp.mean(mixed * mixed, axis=-1, keepdims=True) + EPS)
    normed = (mixed * scale * gain_ref[...]).astype(BF16)
    for p in range(parts):
        out_ref[p] = normed[p * rows:(p + 1) * rows]


def mix_and_norm(queries, state, local, route_col, head_gain, parts):
    length, width = queries.shape
    heads = width // HD
    wide = pl.BlockSpec((length, HD), lambda h: (0, h))
    return pl.pallas_call(
        mix_kernel,
        name="mix_and_norm",
        grid=(heads,),
        in_specs=[
            wide,
            pl.BlockSpec((M * HD, HD), lambda h: (h, 0)),
            wide,
            pl.BlockSpec((length, 1), lambda h: (0, 0)),
            pl.BlockSpec((1, HD), lambda h: (0, h)),
        ],
        out_specs=pl.BlockSpec((parts, length // parts, HD), lambda h: (0, 0, h)),
        out_shape=jax.ShapeDtypeStruct((parts, length // parts, width), BF16),
        compiler_params=params(),
    )(queries, state, local, route_col, head_gain)


def slot_columns(ids, experts, local_experts):
    tokens = ids.shape[0]
    owners = experts // local_experts
    lanes = lax.broadcasted_iota(jnp.int32, (tokens, experts), 1)
    chosen = [(ids[:, j:j + 1] == lanes).astype(F32) for j in range(2)]
    t = lax.broadcasted_iota(jnp.int32, (tokens, tokens), 0)
    s = lax.broadcasted_iota(jnp.int32, (tokens, tokens), 1)
    earlier = contract(
        (t > s).astype(F32).astype(BF16), (chosen[0] + chosen[1]).astype(BF16), ((1,), (0,))
    )
    slots = []
    for j in range(2):
        rank = jnp.sum(earlier * chosen[j], axis=1, keepdims=True).astype(jnp.int32)
        expert = ids[:, j:j + 1]
        owner = expert // local_experts
        local = expert % local_experts
        slots.append(
            ((local // PAIR) * owners + owner) * GROUP_ROWS + (local % PAIR) * CAP + rank
        )
    return slots


def pack_dense_kernel(chunks, local_experts, residual_ref, piece_ref, gain_ref, ids_ref, *refs):
    stream_ref, out_refs = refs[0], refs[1:1 + chunks]
    parts, rows, _ = piece_ref.shape
    owners, groups, _, width = out_refs[0].shape
    normed = jnp.concatenate([piece_ref[p] for p in range(parts)], axis=1)
    stream = (residual_ref[...].astype(F32) + normed.astype(F32)).astype(BF16)
    stream_ref[...] = stream
    wide = stream.astype(F32)
    scale = lax.rsqrt(jnp.mean(wide * wide, axis=-1, keepdims=True) + EPS)
    ffn_in = (wide * scale * gain_ref[...]).astype(BF16)
    experts = owners * local_experts
    slot0, slot1 = slot_columns(ids_ref[...], experts, local_experts)
    span = owners * GROUP_ROWS
    for c in range(chunks):
        for g in range(groups):
            base = (c * groups + g) * span
            lanes = lax.broadcasted_iota(jnp.int32, (rows, span), 1) + base
            spread = jnp.where((slot0 == lanes) | (slot1 == lanes), 1.0, 0.0).astype(BF16)
            packed = contract(spread, ffn_in, ((0,), (0,))).astype(BF16)
            out_refs[c][:, g] = packed.reshape(owners, GROUP_ROWS, width)


def pack_dense(residual, pieces, gain, ids, chunks, owners, local_experts):
    tokens, width = residual.shape
    groups = local_experts // PAIR // chunks
    parcel = jax.ShapeDtypeStruct((owners, groups, GROUP_ROWS, width), BF16)
    out = pl.pallas_call(
        functools.partial(pack_dense_kernel, chunks, local_experts),
        name="pack_dense",
        out_shape=[jax.ShapeDtypeStruct((tokens, width), BF16)] + [parcel] * chunks,
        compiler_params=params(),
    )(residual, pieces, gain, ids)
    return out[0], out[1:]


def expert_dense_kernel(x_ref, gate_ref, up_ref, down_ref, out_ref, acc_ref):
    e = pl.program_id(1)
    f = pl.program_id(2)
    owners, rows, width = x_ref.shape
    x = x_ref[...].reshape(owners * rows, width)
    gate = contract(x, gate_ref[...], ((1,), (0,)))
    upward = contract(x, up_ref[...], ((1,), (0,)))
    row = lax.broadcasted_iota(jnp.int32, gate.shape, 0)
    mine = (row // CAP) % PAIR == e
    hidden = gate / (1.0 + jnp.exp(-gate)) * upward
    hidden = jnp.where(mine, hidden, 0.0).astype(BF16)
    part = contract(hidden, down_ref[...], ((1,), (0,)))
    first = (e == 0) & (f == 0)

    @pl.when(first)
    def _():
        acc_ref[...] = part

    @pl.when(jnp.logical_not(first))
    def _():
        acc_ref[...] = acc_ref[...] + part

    @pl.when((e == pl.num_programs(1) - 1) & (f == pl.num_programs(2) - 1))
    def _():
        out_ref[...] = acc_ref[...].astype(BF16).reshape(owners, rows, width)


def serve_dense(received, w_gate, w_up, w_down, chunk):
    owners, groups, rows, width = received.shape
    hidden = w_gate.shape[2]
    split = 2
    step = hidden // split
    first = chunk * groups * PAIR
    token_spec = pl.BlockSpec((owners, None, rows, width), lambda g, e, f: (0, g, 0, 0))
    in_spec = pl.BlockSpec((None, width, step), lambda g, e, f: (first + g * PAIR + e, 0, f))
    return pl.pallas_call(
        expert_dense_kernel,
        grid=(groups, PAIR, split),
        in_specs=[
            token_spec,
            in_spec,
            in_spec,
            pl.BlockSpec((None, step, width), lambda g, e, f: (first + g * PAIR + e, f, 0)),
        ],
        out_specs=token_spec,
        out_shape=jax.ShapeDtypeStruct(received.shape, BF16),
        scratch_shapes=[pltpu.VMEM((owners * rows, width), F32)],
        compiler_params=params(),
    )(received, w_gate, w_up, w_down)


def combine_dense_kernel(chunks, local_experts, stream_ref, ids_ref, gates_ref, *refs):
    back_refs, out_ref, first_ref, second_ref = refs[:chunks], refs[chunks], refs[-2], refs[-1]
    owners, groups, rows, _ = back_refs[0].shape
    span = owners * rows

    @pl.when(pl.program_id(0) == 0)
    def _():
        slot0, slot1 = slot_columns(ids_ref[...], owners * local_experts, local_experts)
        lanes = lax.broadcasted_iota(jnp.int32, first_ref.shape, 1)
        first_ref[...] = jnp.where(slot0 == lanes, 1.0, 0.0).astype(BF16)
        second_ref[...] = jnp.where(slot1 == lanes, 1.0, 0.0).astype(BF16)

    back = jnp.concatenate(
        [
            back_refs[c][:, g].reshape(span, back_refs[c].shape[3])
            for c in range(chunks)
            for g in range(groups)
        ],
        axis=0,
    )
    gates = gates_ref[...]
    total = stream_ref[...].astype(F32)
    total = total + gates[:, 0:1] * contract(first_ref[...], back, ((1,), (0,)))
    total = total + gates[:, 1:2] * contract(second_ref[...], back, ((1,), (0,)))
    out_ref[...] = total.astype(BF16)


def combine_dense(stream, ids, gates, backs, local_experts):
    tokens, width = stream.shape
    owners, groups, rows, _ = backs[0].shape
    chunks = len(backs)
    slots = owners * groups * rows * chunks
    step = min(512, width)
    back_spec = pl.BlockSpec((owners, groups, rows, step), lambda d: (0, 0, 0, d))
    return pl.pallas_call(
        functools.partial(combine_dense_kernel, chunks, local_experts),
        name="combine_dense",
        grid=(width // step,),
        in_specs=[
            pl.BlockSpec((tokens, step), lambda d: (0, d)),
            pl.BlockSpec(ids.shape, lambda d: (0, 0)),
            pl.BlockSpec(gates.shape, lambda d: (0, 0)),
        ]
        + [back_spec] * chunks,
        out_specs=pl.BlockSpec((tokens, step), lambda d: (0, d)),
        out_shape=jax.ShapeDtypeStruct((tokens, width), BF16),
        scratch_shapes=[pltpu.VMEM((tokens, slots), BF16)] * 2,
        compiler_params=params(),
    )(stream, ids, gates, *backs)


class Plan:
    def __init__(self, local_experts):
        dense = local_experts * CAP
        self.ahead = local_experts // 2
        first = self.ahead * CAP
        self.out = (first, first // 2, dense - first - first // 2)
        self.back = (first // 2, first, dense - first - first // 2)


def in_round(place, bounds, k, owner):
    low = sum(bounds[:k])
    inside = (place >= low) & (place < low + bounds[k])
    return jnp.where(inside, owner * bounds[k] + place - low, -1)


def one_hot(column, width):
    lanes = lax.broadcasted_iota(jnp.int32, (column.shape[0], width), 1)
    return jnp.where(column == lanes, 1.0, 0.0).astype(BF16)


VMEM = pl.BlockSpec(memory_space=pltpu.VMEM)
SMEM = pl.BlockSpec(memory_space=pltpu.SMEM)


def id_columns(id_refs):
    parts = len(id_refs)
    pad = -2 * parts % 8
    rows = [ref[...].astype(F32) for ref in id_refs]
    if pad:
        rows.append(jnp.zeros((pad, id_refs[0].shape[1]), F32))
    rows = jnp.concatenate(rows, axis=0)
    return rows, rows.T


def counts_kernel(local_experts, plan, parts, head_ref, *refs):
    id_refs, meta_ref = refs[:parts], refs[parts]
    tokens = id_refs[0].shape[1]
    contexts = meta_ref.shape[0]
    owners = contexts * parts
    head = head_ref[0]
    owner_lane = lax.broadcasted_iota(jnp.int32, (tokens, owners), 1)
    local_lane = lax.broadcasted_iota(jnp.int32, (tokens, HD), 1)
    owner_row = lax.broadcasted_iota(jnp.int32, (contexts, owners), 1)
    context_row = lax.broadcasted_iota(jnp.int32, (contexts, owners), 0)
    mine = jnp.where(owner_row == context_row * parts + head, 1.0, 0.0).astype(BF16)
    lane = lax.broadcasted_iota(jnp.int32, (owners, HD), 1)
    _, id_cols = id_columns(id_refs)
    flags = 0.0
    metas = []
    for b in range(parts):
        counts = 0.0
        for j in range(2):
            ids = id_cols[:, 2 * b + j:2 * b + j + 1].astype(jnp.int32)
            counts = counts + contract(
                (ids // local_experts == owner_lane).astype(F32).astype(BF16),
                (ids % local_experts == local_lane).astype(F32).astype(BF16),
                ((0,), (0,)),
            )
        total = jnp.sum(counts, axis=1, keepdims=True)
        front = jnp.sum(jnp.where(lane < plan.ahead, counts, 0.0), axis=1, keepdims=True)
        over = (total > sum(plan.out[:2])) | (
            total - jnp.minimum(front, plan.back[0]) > plan.back[1]
        )
        flags = jnp.maximum(flags, jnp.max(jnp.where(over, 1.0, 0.0), axis=0, keepdims=True))
        metas.append(contract(mine, counts.astype(BF16), ((1,), (0,))))
    meta_lane = lax.broadcasted_iota(jnp.int32, (contexts, HD), 1)
    meta_ref[...] = jnp.zeros(meta_ref.shape, F32)
    for b in range(parts):
        marked = jnp.where(meta_lane == local_experts, flags, metas[b])
        for c in range(contexts):
            meta_ref[c, b:b + 1, :] = marked[c:c + 1]


def count_choices(head, ids, contexts, local_experts, plan):
    parts = len(ids)
    return pl.pallas_call(
        functools.partial(counts_kernel, local_experts, plan, parts),
        name="count_choices",
        in_specs=[SMEM] + [VMEM] * parts,
        out_specs=VMEM,
        out_shape=jax.ShapeDtypeStruct((contexts, parts + -parts % 8, HD), F32),
        compiler_params=params(16),
    )(head, *ids)


def route_kernel(local_experts, experts, plan, parts, *refs):
    id_refs, code_ref, spread_refs = refs[:parts], refs[parts], refs[parts + 1:]
    tokens = id_refs[0].shape[1]
    t = lax.broadcasted_iota(jnp.int32, (tokens, tokens), 0)
    s = lax.broadcasted_iota(jnp.int32, (tokens, tokens), 1)
    earlier_mask = (t > s).astype(F32).astype(BF16)
    row = lax.broadcasted_iota(jnp.int32, (experts, experts), 0)
    col = lax.broadcasted_iota(jnp.int32, (experts, experts), 1)
    mates = row // local_experts == col // local_experts
    below = jnp.where(mates & (row < col), 1.0, 0.0).astype(BF16)
    ahead = jnp.where(mates & (row % local_experts < plan.ahead), 1.0, 0.0).astype(BF16)
    lanes = lax.broadcasted_iota(jnp.int32, (tokens, experts), 1)
    id_rows, id_cols = id_columns(id_refs)
    for b in range(parts):
        ids = [id_cols[:, 2 * b + j:2 * b + j + 1].astype(jnp.int32) for j in range(2)]
        chosen = [(i == lanes).astype(F32) for i in ids]
        both = (chosen[0] + chosen[1]).astype(BF16)
        counts = contract(jnp.ones((8, tokens), BF16), both, ((1,), (0,))).astype(BF16)
        position = contract(earlier_mask, both, ((1,), (0,))) + contract(counts, below, ((1,), (0,)))[0:1]
        places = [jnp.sum(position * c, axis=1, keepdims=True) for c in chosen]
        wide = jnp.concatenate(places + [jnp.zeros((tokens, HD - 2), F32)], axis=1)
        place_rows = wide.T[0:8]
        if b == 0:
            aheads = contract(counts, ahead, ((1,), (0,)))[0:1]
            slot_lane = lax.broadcasted_iota(jnp.int32, code_ref.shape, 1)
            code = jnp.zeros(code_ref.shape, jnp.int32)
            for j in range(2):
                place = places[j].astype(jnp.int32)
                front = jnp.sum(aheads * chosen[j], axis=1, keepdims=True).astype(jnp.int32)
                back = jnp.where(
                    (ids[j] % local_experts < plan.ahead) & (place < plan.back[0]),
                    place,
                    plan.back[0] + place - jnp.minimum(front, plan.back[0]),
                )
                code = jnp.where(slot_lane == j, ids[j] // local_experts, code)
                code = jnp.where(slot_lane == 4 + j, back, code)
            code_ref[...] = code
        for k, spread_ref in enumerate(spread_refs):
            slots = spread_ref.shape[1]
            slot = lax.broadcasted_iota(jnp.int32, (slots, tokens), 0)
            hit = None
            for j in range(2):
                owner = id_rows[2 * b + j:2 * b + j + 1].astype(jnp.int32) // local_experts
                index = in_round(place_rows[j:j + 1].astype(jnp.int32), plan.out, k, owner)
                hit = (slot == index) if hit is None else hit | (slot == index)
            spread_ref[b] = jnp.where(hit, 1.0, 0.0).astype(BF16)


def route(ids, contexts, local_experts, plan):
    parts = len(ids)
    tokens = ids[0].shape[1]
    owners = contexts * parts
    return pl.pallas_call(
        functools.partial(route_kernel, local_experts, owners * local_experts, plan, parts),
        name="route",
        in_specs=[VMEM] * parts,
        out_specs=[VMEM] * 4,
        out_shape=[pltpu.HBM((tokens, HD), jnp.int32)]
        + [pltpu.HBM((parts, owners * rows, tokens), BF16) for rows in plan.out],
        compiler_params=params(24),
    )(*ids)


def prefix_with_counts_kernel(piece_ref, meta_ref, out_ref):
    ranks, rows, _ = piece_ref.shape
    total = jnp.zeros(piece_ref.shape[1:], F32)
    for r in range(ranks):
        out_ref[r, :rows, :] = total.astype(BF16)
        out_ref[r, rows:, :] = meta_ref[r].astype(BF16)
        if r + 1 < ranks:
            total = total + piece_ref[r].astype(F32)


def prefix_with_counts(pieces, meta):
    ranks, rows, width = pieces.shape
    return pl.pallas_call(
        prefix_with_counts_kernel,
        name="prefix_with_counts",
        in_specs=[VMEM] * 2,
        out_specs=VMEM,
        out_shape=pltpu.HBM((ranks, rows + meta.shape[1], width), BF16),
        compiler_params=params(12),
    )(pieces, meta)


def columns_kernel(parts, head_ref, whole_ref, *out_refs):
    step = whole_ref.shape[1] // parts
    for s in range(parts):
        start = pl.multiple_of((head_ref[0] + s) % parts * step, step)
        out_refs[s][...] = whole_ref[:, pl.ds(start, step)]


def columns_by_turn(head, whole, parts):
    tokens, width = whole.shape
    return pl.pallas_call(
        functools.partial(columns_kernel, parts),
        name="columns_by_turn",
        in_specs=[SMEM, VMEM],
        out_specs=[VMEM] * parts,
        out_shape=[pltpu.HBM((tokens, width // parts), BF16)] * parts,
        compiler_params=params(12),
    )(head, whole)


def mix_pack_kernel(
    parts, local_experts, plan, head_ref, query_ref, state_ref, tail_ref, local_ref, route_col_ref, gain_ref, *refs
):
    residual_refs, spread_ref = refs[:parts], refs[parts]
    refs = refs[parts + 1:]
    meta_ref, flag_ref, parcel_ref, stream_refs = refs[0], refs[1], refs[2], refs[3:3 + parts]
    normed_ref = refs[-1]
    head = head_ref[0]
    pieces, rows, _ = state_ref.shape
    contexts, tail, _ = tail_ref.shape
    rows -= tail
    width = query_ref.shape[1]
    together = width // HD
    share = pieces // together
    column = route_col_ref[...]
    doubled = [jnp.where(column == m, 2.0, 1.0).astype(BF16) for m in range(M)]
    for g in range(together):
        span = slice(g * HD, (g + 1) * HD)
        query = query_ref[:, span]
        wide = jnp.concatenate([query * weight for weight in doubled], axis=1)
        state = jnp.concatenate([state_ref[g * share + i, :rows, :] for i in range(share)], axis=0)
        mixed = contract(wide, state, ((1,), (0,))) + local_ref[:, span]
        scale = lax.rsqrt(jnp.mean(mixed * mixed, axis=-1, keepdims=True) + EPS)
        normed_ref[:, span] = (mixed * scale * gain_ref[:, span]).astype(BF16)

    @pl.when(pl.program_id(0) == 0)
    def _():
        counts = tail_ref[...].astype(F32)
        owners = contexts * parts
        lane = lax.broadcasted_iota(jnp.int32, counts.shape, 2)
        over = jnp.max(jnp.where(lane == local_experts, counts, 0.0))
        flag_ref[0] = (over > 0.5).astype(jnp.int32)
        source = lax.broadcasted_iota(jnp.int32, (owners, contexts * tail), 0)
        given = lax.broadcasted_iota(jnp.int32, (owners, contexts * tail), 1)
        turn = (head - source % parts + parts) % parts
        order = jnp.where(given == source // parts * tail + turn, 1.0, 0.0).astype(BF16)
        flat = counts.reshape(contexts * tail, counts.shape[2]).astype(BF16)
        meta_ref[...] = contract(order, flat, ((1,), (0,))).astype(jnp.int32)

    tokens = residual_refs[0].shape[0]
    for s in range(parts):
        start = pl.multiple_of((head - s + parts) % parts * tokens, tokens)
        normed = normed_ref[pl.ds(start, tokens), :]
        stream = (residual_refs[s][...].astype(F32) + normed.astype(F32)).astype(BF16)
        stream_refs[s][...] = stream
        put_parcels(plan.out[0], s, spread_ref[s], stream, parcel_ref)


def put_parcels(each, s, spread, stream, parcel_ref):
    owners, _, width = parcel_ref.shape
    packed = contract(spread, stream, ((1,), (0,))).astype(BF16)
    parcel_ref[:, s * each:(s + 1) * each, :] = packed.reshape(owners, each, width)


def mix_and_pack(head, queries, carried, tail, local, route_col, head_gain, residuals, spread, local_experts, plan):
    length, width = queries.shape
    heads = width // HD
    together = 2 if heads % 2 == 0 else 1
    step = together * HD
    contexts, rows, _ = carried.shape
    share = contexts * together // heads
    parts = len(residuals)
    tokens = length // parts
    owners = contexts * parts
    wide = pl.BlockSpec((length, step), lambda h: (0, h))
    narrow = pl.BlockSpec((tokens, step), lambda h: (0, h))

    def whole(x):
        return pl.BlockSpec(x.shape, lambda h: (0,) * len(x.shape))

    each = parts * plan.out[0]
    meta = pltpu.HBM((owners, HD), jnp.int32)
    out = pl.pallas_call(
        functools.partial(mix_pack_kernel, parts, local_experts, plan),
        name="mix_and_pack",
        grid=(heads // together,),
        in_specs=[
            SMEM,
            wide,
            pl.BlockSpec((share, rows, HD), lambda h: (h, 0, 0)),
            pl.BlockSpec((contexts, tail, HD), lambda h: (0, (rows - tail) // tail, 0)),
            wide,
            pl.BlockSpec((length, 1), lambda h: (0, 0)),
            pl.BlockSpec((1, step), lambda h: (0, h)),
        ]
        + [narrow] * parts
        + [whole(spread)],
        out_specs=[whole(meta), SMEM, pl.BlockSpec((owners, each, step), lambda h: (0, 0, h))]
        + [narrow] * parts,
        out_shape=[
            meta,
            jax.ShapeDtypeStruct((1,), jnp.int32),
            pltpu.HBM((owners, each, width), BF16),
        ]
        + [pltpu.HBM((tokens, width), BF16)] * parts,
        scratch_shapes=[pltpu.VMEM((length, step), BF16)],
        compiler_params=params(32),
    )(
        head,
        in_hbm(queries),
        carried,
        carried,
        local,
        route_col,
        head_gain,
        *map(in_hbm, residuals),
        in_hbm(spread),
    )
    return out[0], out[1], out[2], out[3:]


def pack_kernel(each, spread_ref, *refs):
    for s, stream_ref in enumerate(refs[:-1]):
        put_parcels(each, s, spread_ref[s], stream_ref[...], refs[-1])


def pack(k, spread, streams, owners, plan):
    each = plan.out[k]
    shape = (owners, len(streams) * each, streams[0].shape[1])
    return pl.pallas_call(
        functools.partial(pack_kernel, each),
        in_specs=[VMEM] * (1 + len(streams)),
        out_specs=VMEM,
        out_shape=pltpu.HBM(shape, BF16),
        compiler_params=params(24),
    )(in_hbm(spread), *map(in_hbm, streams))


def unset_kernel(out_ref):
    pass


def unset(shape):
    return pl.pallas_call(
        unset_kernel,
        name="unset",
        out_specs=pl.BlockSpec(memory_space=pl.ANY),
        out_shape=pltpu.HBM(shape, BF16),
        compiler_params=params(4),
    )()


def gated(gates, spreads, back):
    total = 0.0
    for j, spread in enumerate(spreads):
        total = total + gates[:, j:j + 1] * contract(spread, back, ((1,), (0,)))
    return total


def choices(code, plan, k, owners):
    return [
        one_hot(in_round(code[:, 4 + j:5 + j], plan.back, k, code[:, j:j + 1]), owners * plan.back[k])
        for j in range(2)
    ]


def combine_ahead_kernel(plan, parts, head_ref, flag_ref, code_ref, gates_ref, back_ref, late_ref, *refs):
    stream_refs, (acc_ref, pick_ref) = refs[:parts], refs[parts:]
    code = code_ref[...]
    owners, rows, width = back_ref.shape
    flat = back_ref[...].reshape(owners * rows, width)
    acc_ref[...] = gated(gates_ref[...], choices(code, plan, 0, owners), flat)
    step = width // parts
    for s in range(parts):
        start = pl.multiple_of((head_ref[0] + s) % parts * step, step)
        acc_ref[:, pl.ds(start, step)] = acc_ref[:, pl.ds(start, step)] + stream_refs[s][...].astype(F32)
    for j, spread in enumerate(choices(code, plan, 1, owners)):
        pick_ref[j * code.shape[0]:(j + 1) * code.shape[0], :] = spread

    @pl.when(flag_ref[0] > 0)
    def _():
        late = late_ref[...].reshape(owners * plan.back[2], width)
        acc_ref[...] = acc_ref[...] + gated(gates_ref[...], choices(code, plan, 2, owners), late)


def combine_ahead(head, flag, code, gates, back, late, streams, plan):
    owners, _, width = back.shape
    tokens = code.shape[0]
    return pl.pallas_call(
        functools.partial(combine_ahead_kernel, plan, len(streams)),
        name="combine_ahead",
        in_specs=[SMEM] * 2 + [VMEM] * (4 + len(streams)),
        out_specs=[VMEM] * 2,
        out_shape=[
            pltpu.HBM((tokens, width), F32),
            pltpu.HBM((2 * tokens, owners * plan.back[1]), BF16),
        ],
        compiler_params=params(28),
    )(head, flag, code, gates, back, late, *streams)


def combine_kernel(gates_ref, acc_ref, pick_ref, back_ref, out_ref):
    owners, rows, _ = back_ref.shape
    step = out_ref.shape[1]
    start = pl.multiple_of(pl.program_id(0) * step, step)
    flat = back_ref[:, :, pl.ds(start, step)].reshape(owners * rows, step)
    tokens = acc_ref.shape[0]
    found = contract(pick_ref[...], flat, ((1,), (0,)))
    total = acc_ref[...]
    for j in range(2):
        total = total + gates_ref[:, j:j + 1] * found[j * tokens:(j + 1) * tokens]
    out_ref[...] = total.astype(BF16)


def combine(gates, acc, picks, back):
    tokens, width = acc.shape
    step = min(1024, width)

    def whole(x):
        return pl.BlockSpec(x.shape, lambda d: (0,) * len(x.shape))

    narrow = pl.BlockSpec((tokens, step), lambda d: (0, d))
    return pl.pallas_call(
        combine_kernel,
        name="combine",
        grid=(width // step,),
        in_specs=[
            whole(gates),
            narrow,
            whole(picks),
            VMEM,
        ],
        out_specs=narrow,
        out_shape=jax.ShapeDtypeStruct((tokens, width), BF16),
        compiler_params=params(20),
    )(gates, in_hbm(acc), in_hbm(picks), in_vmem(back))


def batch_columns(meta, expert, local_experts, plan):
    owners = meta.shape[0]
    counts = jnp.where(
        lax.broadcasted_iota(jnp.int32, meta.shape, 1) < local_experts, meta, 0
    ).astype(F32)
    lanes = counts.shape[1]
    row = lax.broadcasted_iota(jnp.int32, (lanes, lanes), 0)
    col = lax.broadcasted_iota(jnp.int32, (lanes, lanes), 1)
    below = jnp.where(row < col, 1.0, 0.0).astype(BF16)
    offsets = contract(counts.astype(BF16), below, ((1,), (0,)))
    batch = owners * CAP
    source_row = lax.broadcasted_iota(jnp.int32, (batch, owners), 0) // CAP
    source_col = lax.broadcasted_iota(jnp.int32, (batch, owners), 1)
    expand = jnp.where(source_row == source_col, 1.0, 0.0).astype(BF16)
    lane = lax.broadcasted_iota(jnp.int32, (batch, lanes), 1)

    def column(values, picked):
        wide = contract(expand, values.astype(BF16), ((1,), (0,)))
        return jnp.sum(jnp.where(picked, wide, 0.0), axis=1, keepdims=True).astype(jnp.int32)

    count = column(counts, lane == expert)
    offset = column(offsets, lane == expert)
    front = column(counts, lane < plan.ahead)
    index = lax.broadcasted_iota(jnp.int32, (batch, 1), 0)
    rank = index % CAP
    valid = rank < count
    place = offset + rank
    back = jnp.where(
        (expert < plan.ahead) & (place < plan.back[0]),
        place,
        plan.back[0] + place - jnp.minimum(front, plan.back[0]),
    )
    return index // CAP, jnp.where(valid, place, -1), jnp.where(valid, back, -1)


def expert_kernel(
    first, taken, given, has_base, local_experts, parts, plan, flag_ref, meta_ref, gain_ref, *refs
):
    x_refs, refs = refs[:len(taken)], refs[len(taken):]
    gate_ref, up_ref, down_ref = refs[:3]
    base_ref = refs[3] if has_base else None
    refs = refs[3 + has_base:]
    out_refs, (batch_ref, acc_ref, done_ref) = refs[:len(given)], refs[len(given):]
    e = pl.program_id(0)
    f = pl.program_id(1)
    last_f = pl.num_programs(1) - 1
    batch = batch_ref.shape[0]
    meta = meta_ref[...]

    @pl.when(f == 0)
    def _():
        source, place, _ = batch_columns(meta, first + e, local_experts, plan)

        context = source // parts
        block = source % parts

        def rows_of(i, k):
            owners, rows, step = x_refs[i].shape
            pieces = x_refs[i][...].reshape(owners // parts, parts, rows, step)
            found = []
            for h in range(parts):
                turn = (h - block + parts) % parts
                spread = one_hot(
                    in_round(place, plan.out, k, context * parts + turn), owners * plan.out[k]
                )
                flat = pieces[:, h].reshape(owners // parts * rows, step)
                found.append(contract(spread, flat, ((1,), (0,))))
            return jnp.concatenate(found, axis=1)

        total = 0.0
        for i, k in enumerate(taken):
            if k < 2:
                total = total + rows_of(i, k)
        acc_ref[...] = total
        for i, k in enumerate(taken):
            if k == 2:

                @pl.when(flag_ref[0] > 0)
                def _():
                    acc_ref[...] = acc_ref[...] + rows_of(i, k)

        stream = acc_ref[...]
        scale = lax.rsqrt(jnp.mean(stream * stream, axis=-1, keepdims=True) + EPS)
        batch_ref[...] = (stream * scale * gain_ref[...]).astype(BF16)

    x = batch_ref[...]
    gate = contract(x, gate_ref[...], ((1,), (0,)))
    upward = contract(x, up_ref[...], ((1,), (0,)))
    hidden = (gate / (1.0 + jnp.exp(-gate)) * upward).astype(BF16)
    part = contract(hidden, down_ref[...], ((1,), (0,)))

    @pl.when(f == 0)
    def _():
        acc_ref[...] = part

    @pl.when((f > 0) & (f < last_f))
    def _():
        acc_ref[...] = acc_ref[...] + part

    @pl.when(f == last_f)
    def _():
        done_ref[e] = (acc_ref[...] + part).astype(BF16)

    @pl.when((e == pl.num_programs(0) - 1) & (f == last_f))
    def _():
        count = done_ref.shape[0]
        columns = [batch_columns(meta, first + i, local_experts, plan) for i in range(count)]
        source = jnp.concatenate([c[0] for c in columns], axis=0)
        back = jnp.concatenate([c[2] for c in columns], axis=0)
        done = done_ref[...].reshape(count * batch, done_ref.shape[2])

        def put(i, k):
            owners, rows, width = out_refs[i].shape
            spread = one_hot(in_round(back, plan.back, k, source), owners * rows)
            rows_out = contract(spread, done, ((0,), (0,)))
            if has_base and k == 1:
                rows_out = rows_out + base_ref[...].reshape(owners * rows, width).astype(F32)
            out_refs[i][...] = rows_out.astype(BF16).reshape(owners, rows, width)

        for i, k in enumerate(given):
            if k < 2:
                put(i, k)
            else:

                @pl.when(flag_ref[0] > 0)
                def _():
                    put(i, k)


def serve_experts(flag, meta, gain, parts, received, weights, base, first, taken, given, plan):
    w_gate, w_up, w_down = weights
    local_experts, width, hidden = w_gate.shape
    owners = meta.shape[0]
    count = plan.ahead
    split = 2
    step = hidden // split

    def whole(x):
        return pl.BlockSpec(x.shape, lambda e, f: (0,) * len(x.shape))

    in_spec = pl.BlockSpec((None, width, step), lambda e, f: (first + e, 0, f))
    extra = [] if base is None else [in_hbm(base)]
    outs = [pltpu.HBM((owners, plan.back[k], width), BF16) for k in given]
    received = [in_vmem(x) if k == 1 else in_hbm(x) for k, x in zip(taken, received)]
    batch = owners * CAP
    return pl.pallas_call(
        functools.partial(
            expert_kernel, first, taken, given, base is not None, local_experts, parts, plan
        ),
        grid=(count, split),
        in_specs=[SMEM, whole(meta), whole(gain)]
        + [whole(x) for x in received]
        + [
            in_spec,
            in_spec,
            pl.BlockSpec((None, step, width), lambda e, f: (first + e, f, 0)),
        ]
        + [whole(x) for x in extra],
        out_specs=[whole(x) for x in outs],
        out_shape=outs,
        scratch_shapes=[
            pltpu.VMEM((batch, width), BF16),
            pltpu.VMEM((batch, width), F32),
            pltpu.VMEM((count, batch, width), BF16),
        ],
        compiler_params=params(44),
    )(flag, meta, gain, *received, w_gate, w_up, w_down, *extra)


def everywhere(x):
    return lax.all_to_all(x, ("ctx", "head"), split_axis=0, concat_axis=0, tiled=True)


def everywhere_if(flag, x):
    return lax.cond(flag[0] > 0, everywhere, lambda y: unset(y.shape), x)


def body_dense(
    queries,
    keys,
    values,
    mem_route,
    head_gain,
    residual_in,
    ffn_gain,
    expert_ids,
    expert_gates,
    w_gate,
    w_up,
    w_down,
):
    length = queries.shape[0]
    ctx_count = lax.axis_size("ctx")
    head_count = lax.axis_size("head")
    owners = ctx_count * head_count
    local_experts = w_gate.shape[0]
    pairs = local_experts // PAIR
    chunks = 2 if pairs % 2 == 0 else 1
    route_row = mem_route.reshape(1, length)
    route_col = mem_route.reshape(length, 1)

    states = block_states(keys, values, route_row)
    pieces = lax.all_to_all(states, "ctx", split_axis=0, concat_axis=0, tiled=True)
    before = exclusive_prefix(pieces.reshape(ctx_count, -1, HD))
    carried = lax.all_to_all(
        before.reshape(states.shape), "ctx", split_axis=0, concat_axis=0, tiled=True
    )
    local = local_attention(queries, keys, values, route_row, route_col)
    normed = mix_and_norm(queries, carried, local, route_col, head_gain[None], head_count)
    by_token = lax.all_to_all(normed, "head", split_axis=0, concat_axis=0, tiled=True)

    stream, parcels = pack_dense(
        residual_in, by_token, ffn_gain[None], expert_ids, chunks, owners, local_experts
    )
    backs = []
    for c in range(chunks):
        received = lax.all_to_all(
            parcels[c], ("ctx", "head"), split_axis=0, concat_axis=0, tiled=True
        )
        served = serve_dense(received, w_gate, w_up, w_down, c)
        backs.append(
            lax.all_to_all(served, ("ctx", "head"), split_axis=0, concat_axis=0, tiled=True)
        )
    return combine_dense(stream, expert_ids, expert_gates, backs, local_experts)


def body_compact(
    queries,
    keys,
    values,
    mem_route,
    head_gain,
    residual_in,
    ffn_gain,
    expert_ids,
    expert_gates,
    w_gate,
    w_up,
    w_down,
):
    length = queries.shape[0]
    contexts = lax.axis_size("ctx")
    parts = lax.axis_size("head")
    local_experts = w_gate.shape[0]
    plan = Plan(local_experts)
    route_row = mem_route.reshape(1, length)
    route_col = mem_route.reshape(length, 1)
    head = lax.axis_index("head").astype(jnp.int32)[None]

    def turned(pieces, step):
        return [pieces[0]] + [
            lax.ppermute(pieces[s], "head", [(h, (h + step * s) % parts) for h in range(parts)])
            for s in range(1, parts)
        ]

    ids = turned([expert_ids.T] * parts, 1)
    states = block_states(keys, values, route_row)
    pieces = lax.all_to_all(states, "ctx", split_axis=0, concat_axis=0, tiled=True)
    counts = count_choices(head, ids, contexts, local_experts, plan)
    before = prefix_with_counts(pieces.reshape(contexts, -1, HD), counts)
    carried = lax.all_to_all(before, "ctx", split_axis=0, concat_axis=0, tiled=True)
    cut = columns_by_turn(head, residual_in, parts)
    residuals = turned(cut, 1)
    code, *spreads = route(ids, contexts, local_experts, plan)
    local = local_attention(queries, keys, values, route_row, route_col)
    meta, flag, parcels, own_streams = mix_and_pack(
        head,
        queries,
        carried,
        counts.shape[1],
        local,
        route_col,
        head_gain[None],
        residuals,
        spreads[0],
        local_experts,
        plan,
    )
    weights = (w_gate, w_up, w_down)
    gain = ffn_gain[None]
    received = [everywhere(parcels)]
    parcels = pack(1, spreads[1], own_streams, contexts * parts, plan)
    received.append(everywhere(parcels))
    streams = turned(own_streams, -1)
    back_0, base = serve_experts(
        flag, meta, gain, parts, received[:1], weights, None, 0, (0,), (0, 1), plan
    )
    received.append(
        lax.cond(
            flag[0] > 0,
            lambda spread, pieces: everywhere(pack(2, spread, pieces, contexts * parts, plan)),
            lambda spread, pieces: unset(
                (contexts * parts, parts * plan.out[2], pieces[0].shape[1])
            ),
            spreads[2],
            own_streams,
        )
    )
    back_0 = everywhere(back_0)
    back_1, back_2 = serve_experts(
        flag, meta, gain, parts, received, weights, base, plan.ahead, (0, 1, 2), (1, 2), plan
    )
    back_2 = everywhere_if(flag, back_2)
    back_1 = everywhere(back_1)
    acc, picks = combine_ahead(head, flag, code, expert_gates, back_0, back_2, streams, plan)
    return combine(expert_gates, acc, picks, back_1)


def body(*args):
    local_experts = args[-1].shape[0]
    compact = local_experts * CAP % (4 * GROUP_ROWS) == 0
    return body_compact(*args) if compact else body_dense(*args)


def solution(mesh):
    placed = (
        P("ctx", "head"),
        P("ctx", "head"),
        P("ctx", "head"),
        P("ctx"),
        P("head"),
        P(("ctx", "head"), None),
        P(),
        P(("ctx", "head"), None),
        P(("ctx", "head"), None),
        P(("ctx", "head"), None, None),
        P(("ctx", "head"), None, None),
        P(("ctx", "head"), None, None),
    )
    return jax.shard_map(
        body, mesh=mesh, in_specs=placed, out_specs=P(("ctx", "head"), None), check_vma=False
    )
```
